32 devices in a mesh: dp: 16 (over z, x, core), mp: 2 (over y).
Axes of the slice: x: 2, y: 2, z: 4, core: 2. Of those that a mesh axis runs over, the one named last changes fastest.
Arguments:
- tokens: bfloat16 [64, 512, 768], P('dp', 'mp'), may hold values from -6 to 6
- lengths: int32 [64], P('dp'), may hold values from 128 to 512, as said below
- out_grad: bfloat16 [64, 512, 768], P('dp', 'mp'), may hold values from -6 to 6
- ln1_gain: float32 [768], replicated, may hold values from 0.25 to 1.75
- ln1_shift: float32 [768], replicated, may hold values from -1.75 to 1.75
- w_query: bfloat16 [768, 768], P(None, 'mp'), may hold values from -0.21875 to 0.21875
- b_query: float32 [768], P('mp'), may hold values from -3 to 3
- w_key: bfloat16 [768, 768], P(None, 'mp'), may hold values from -0.21875 to 0.21875
- w_value: bfloat16 [768, 768], P(None, 'mp'), may hold values from -0.21875 to 0.21875
- b_value: float32 [768], P('mp'), may hold values from -3 to 3
- w_out: bfloat16 [768, 768], P('mp'), may hold values from -1.75 to 1.75
- b_out: float32 [768], replicated, may hold values from -1.75 to 1.75
- ln2_gain: float32 [768], replicated, may hold values from 0.25 to 1.75
- ln2_shift: float32 [768], replicated, may hold values from -1.75 to 1.75
- w_up: bfloat16 [768, 3072], P(None, 'mp'), may hold values from -0.21875 to 0.21875
- b_up: float32 [3072], P('mp'), may hold values from -3 to 3
- w_down: bfloat16 [3072, 768], P('mp'), may hold values from -0.109375 to 0.109375
- b_down: float32 [768], replicated, may hold values from -1.75 to 1.75
Outputs:
- block_out: bfloat16 [64, 512, 768], P('dp', 'mp')
- input_grad: float32 [64, 512, 768], P('dp', 'mp')
- grad_ln1_gain: float32 [768], replicated
- grad_ln1_shift: float32 [768], replicated
- grad_w_query: float32 [768, 768], P(None, 'mp')
- grad_b_query: float32 [768], P('mp')
- grad_w_key: float32 [768, 768], P(None, 'mp')
- grad_w_value: float32 [768, 768], P(None, 'mp')
- grad_b_value: float32 [768], P('mp')
- grad_w_out: float32 [768, 768], P('mp')
- grad_b_out: float32 [768], replicated
- grad_ln2_gain: float32 [768], replicated
- grad_ln2_shift: float32 [768], replicated
- grad_w_up: float32 [768, 3072], P(None, 'mp')
- grad_b_up: float32 [3072], P('mp')
- grad_w_down: float32 [3072, 768], P('mp')
- grad_b_down: float32 [768], replicated
The draws below stay inside these ranges and needn't reach their ends.
Inputs may be any that keep to these rules, and one draw needn't show every extreme that they name: lengths of the rows; some row has 512 and some row a quarter of 512.
All inputs are finite; a program needn't handle non-finite values.
Results may differ from the reference program's by a relative error of at most 0.013.
The reference program's roundings to bfloat16 on the way count: a program that leaves them out, or rounds other values in their place, can miss the bound.
Values may be sent and summed in bfloat16 or wider, within the bound.
No kernel may reach another device: no remote copies, remote signals or barrier semaphores. Data moves between devices by JAX's collectives and lax.ppermute only.
A program may use at most 192 MiB of HBM per device.

```python
import math
import jax
import jax.numpy as jnp
from jax import lax

D = 768
HEADS = 12
HEAD_DIM = 64
FF = 3072
SEQ = 512
ROWS_DEV = 4
ROWS = 64


def draw_lengths(key, part):
    key_len, key_spot = jax.random.split(key)
    lengths_drawn = jax.random.randint(key_len, (ROWS,), SEQ - SEQ // 10, SEQ + 1)
    chosen = jax.random.randint(key_spot, (), 0, ROWS)
    lengths_drawn = lengths_drawn.at[chosen].set(SEQ)
    lengths_drawn = lengths_drawn.at[(chosen + ROWS // 2 + 1) % ROWS].set(SEQ // 4)
    return lengths_drawn.astype(jnp.int32)


def steps_of(rng, extent, pieces, low, top_value):
    def one(axis_at, shards_of):
        draws = jax.random.uniform(jax.random.fold_in(jax.random.fold_in(rng, 6), axis_at), (shards_of,), jnp.float32, low / len(pieces), top_value / len(pieces))
        return jnp.repeat(jnp.exp(draws), extent[axis_at] // shards_of).reshape((-1,) + (1,) * (len(extent) - axis_at - 1))

    level = one(*pieces[0])
    for cut in pieces[1:]:
        level = level * one(*cut)
    return level


def gaussian(stream_key, shape, width, most, cuts=(), kind=jnp.bfloat16):
    values = jax.random.normal(stream_key, shape, jnp.float32) * width
    if len(cuts) > 0:
        values = steps_of(stream_key, shape, cuts, -0.22, 0.18) * values
    return jnp.clip(values, min=-most, max=most).astype(kind)


def setup_inputs(seed: int = 0) -> dict:
    seeds = jax.random.split(jax.random.key(seed), 19)
    return {
        "tokens": gaussian(seeds[0], (ROWS, SEQ, D), 1.0, 6.0, ((0, 16), (1, 2))),
        "lengths": draw_lengths(jax.random.fold_in(seeds[18], 71), 0),
        "out_grad": gaussian(seeds[2], (ROWS, SEQ, D), 1.0, 6.0, ((0, 16), (1, 2))),
        "ln1_gain": jnp.clip(1.0 + 0.15 * jax.random.normal(seeds[3], (D,), jnp.float32), 0.25, 1.75),
        "ln1_shift": gaussian(seeds[4], (D,), 0.3, 1.75, (), jnp.float32),
        "w_query": gaussian(seeds[5], (D, D), D ** -0.5, 0.21875, ((1, 2),)),
        "b_query": gaussian(seeds[6], (D,), 0.5, 3.0, ((0, 2),), jnp.float32),
        "w_key": gaussian(seeds[7], (D, D), D ** -0.5, 0.21875, ((1, 2),)),
        "w_value": gaussian(seeds[8], (D, D), D ** -0.5, 0.21875, ((1, 2),)),
        "b_value": gaussian(seeds[9], (D,), 0.5, 3.0, ((0, 2),), jnp.float32),
        "w_out": gaussian(seeds[10], (D, D), (max(D * 8 // SEQ, 1)) ** -0.5, 1.75, ((0, 2),)),
        "b_out": gaussian(seeds[11], (D,), 0.3, 1.75, (), jnp.float32),
        "ln2_gain": jnp.clip(1.0 + 0.15 * jax.random.normal(seeds[12], (D,), jnp.float32), 0.25, 1.75),
        "ln2_shift": gaussian(seeds[13], (D,), 0.3, 1.75, (), jnp.float32),
        "w_up": gaussian(seeds[14], (D, FF), D ** -0.5, 0.21875, ((1, 2),)),
        "b_up": gaussian(seeds[15], (FF,), 0.5, 3.0, ((0, 2),), jnp.float32),
        "w_down": gaussian(seeds[16], (FF, D), FF ** -0.5, 0.109375, ((0, 2),)),
        "b_down": gaussian(seeds[17], (D,), 0.3, 1.75, (), jnp.float32),
    }


precise = lax.Precision.HIGHEST
epsilon = 1e-12
masked_fill = -1000000000.0

@jax.custom_vjp
def low(v):
    return lax.optimization_barrier(v.astype(jnp.bfloat16)).astype(jnp.float32)

@jax.custom_vjp
def low_back(v):
    return v

def low_keep(v):
    return (low(v), None)

def low_pass(kept, grad):
    return (grad,)

def back_keep(v):
    return (v, None)

def back_low(kept, grad):
    return (low(grad),)
low.defvjp(low_keep, low_pass)
low_back.defvjp(back_keep, back_low)

def norm_rows(values, gain_vec, offset):
    average = lax.optimization_barrier(jnp.mean(values, axis=-1, keepdims=True))
    centred = values - average
    inv_std = lax.rsqrt(lax.optimization_barrier(jnp.mean(centred * centred, axis=-1, keepdims=True)) + epsilon)
    return centred * inv_std * gain_vec + offset

def project(left_side, matrix):
    return jnp.einsum('gsd,de->gse', left_side, matrix, precision=precise)

def forward(inputs, group_len, params):
    ln1_gain, ln1_shift, w_query, b_query, w_key, w_value, b_value, w_out, b_out, ln2_gain, ln2_shift, w_up, b_up, w_down, b_down = params
    groups = inputs.shape[0]
    score_scale = 1.0 / math.sqrt(HEAD_DIM)
    normed = low(norm_rows(inputs, ln1_gain, ln1_shift))
    query_low = low_back(low(project(normed, w_query) + b_query)).reshape(groups, SEQ, HEADS, HEAD_DIM)
    keys_low = low_back(low(project(normed, w_key))).reshape(groups, SEQ, HEADS, HEAD_DIM)
    values_low = low_back(low(project(normed, w_value) + b_value)).reshape(groups, SEQ, HEADS, HEAD_DIM)
    scores = low_back(jnp.einsum('gqhd,gkhd->ghqk', query_low, keys_low, precision=precise) * score_scale)
    key_valid = (jnp.arange(SEQ, dtype=jnp.int32)[None, :] < group_len[:, None])[:, None, None, :]
    masked_all = jnp.where(key_valid, scores, masked_fill)
    log_total = jax.nn.logsumexp(masked_all, axis=-1, keepdims=True)
    weights = low(jnp.exp(masked_all - log_total))
    mixed_low = jnp.einsum('ghqk,gkhd->gqhd', weights, values_low, precision=precise).reshape(groups, SEQ, HEADS * HEAD_DIM)
    mixed_low = low_back(low(mixed_low))
    residual = inputs + low_back(project(mixed_low, w_out)) + b_out
    normed_mid = low(norm_rows(residual, ln2_gain, ln2_shift))
    hidden = low_back(project(normed_mid, w_up) + b_up)
    active = low(jax.nn.gelu(hidden, approximate=False))
    return residual + low_back(project(active, w_down)) + b_down

def reference(tokens, lengths, out_grad, ln1_gain, ln1_shift, w_query, b_query, w_key, w_value, b_value, w_out, b_out, ln2_gain, ln2_shift, w_up, b_up, w_down, b_down):
    params = tuple((member.astype(jnp.float32) for member in (ln1_gain, ln1_shift, w_query, b_query, w_key, w_value, b_value, w_out, b_out, ln2_gain, ln2_shift, w_up, b_up, w_down, b_down)))
    groups = ROWS // ROWS_DEV
    group_tokens = tokens.astype(jnp.float32).reshape(groups, ROWS_DEV, SEQ, D)
    group_lengths = lengths.astype(jnp.int32).reshape(groups, ROWS_DEV)
    group_grads = out_grad.astype(jnp.float32).reshape(groups, ROWS_DEV, SEQ, D)

    def scan_step(running, batch_item):
        group_in, group_len, group_grad = batch_item

        def apply_layer(inputs, weights_all):
            return forward(inputs, group_len, weights_all)
        result, pullback = jax.vjp(apply_layer, group_in, params)
        grad_in, grad_params = pullback(group_grad)
        running = tuple((left_side + right_side for left_side, right_side in zip(running, grad_params)))
        return (running, (result.astype(jnp.bfloat16), grad_in))
    zero_grads = tuple((jnp.zeros_like(member) for member in params))
    summed, (block_out, input_grad) = lax.scan(scan_step, zero_grads, (group_tokens, group_lengths, group_grads))
    block_out = block_out.reshape(ROWS, SEQ, D)
    input_grad = input_grad.reshape(ROWS, SEQ, D)
    return (block_out, input_grad, summed[0], summed[1], summed[2], summed[3], summed[4], summed[5], summed[6], summed[7], summed[8], summed[9], summed[10], summed[11], summed[12], summed[13], summed[14])
```

```python
import functools
import math

import jax
import jax.numpy as jnp
from jax import lax
from jax.experimental import pallas as pl
from jax.experimental.pallas import tpu as pltpu
from jax.sharding import Mesh
from jax.sharding import PartitionSpec as P

HEAD_DIM = 64
PAIR = 2 * HEAD_DIM
EPS = 1e-12
FILL = -1000000000.0
SCALE = 1.0 / math.sqrt(HEAD_DIM)
LOG2E = math.log2(math.e)
F32 = jnp.float32
BF16 = jnp.bfloat16
NT = (((1,), (1,)), ((), ()))
NN = (((1,), (0,)), ((), ()))
TN = (((0,), (0,)), ((), ()))


def mm(a, b, dims=NN):
    return lax.dot_general(a, b, dims, preferred_element_type=F32)


def key_mask(info, row, shape):
    seq = shape[0]
    slot = lax.broadcasted_iota(jnp.int32, shape, 0) + info[0]
    position = jnp.where(slot >= seq, slot - seq, slot)
    return position < info[1 + row]


def head_lanes(value, head):
    lane = lax.broadcasted_iota(jnp.int32, value.shape, 1)
    keep = lane < HEAD_DIM if head == 0 else lane >= HEAD_DIM
    return jnp.where(keep, value, jnp.zeros_like(value))


def attend_kernel(info, q_ref, k_ref, v_ref, o_ref, lse_ref):
    row = pl.program_id(0)
    q, k, v = q_ref[0], k_ref[0], v_ref[0]
    valid = key_mask(info, row, (k.shape[0], q.shape[0]))
    v_t = v.T
    parts = []
    for head in range(2):
        scores = mm(head_lanes(k, head), q, NT) * (SCALE * LOG2E)
        scores = jnp.where(valid, scores, FILL * LOG2E)
        top = jnp.max(scores, axis=0, keepdims=True)
        weight = jnp.exp2(scores - top)
        total = jnp.sum(weight, axis=0, keepdims=True)
        lse_ref[0, 0, head : head + 1, :] = top + jnp.log2(total)
        probs = (weight * (1.0 / total)).astype(BF16)
        parts.append(mm(v_t[head * HEAD_DIM : (head + 1) * HEAD_DIM], probs))
    o_ref[0] = jnp.concatenate(parts, axis=0).T.astype(BF16)


def attend_back_kernel(info, q_ref, k_ref, v_ref, do_ref, lse_ref, d_ref):
    row = pl.program_id(0)
    pair = pl.program_id(1)
    n_pairs = pl.num_programs(1)
    q, k, v, do = q_ref[0], k_ref[0], v_ref[0], do_ref[0]
    valid = key_mask(info, row, (k.shape[0], q.shape[0]))
    k_t = k.T
    dq_t, dk, dv = [], [], []
    for head in range(2):
        scores = mm(head_lanes(k, head), q, NT) * (SCALE * LOG2E)
        scores = jnp.where(valid, scores, FILL * LOG2E)
        probs = jnp.exp2(scores - lse_ref[0, 0, head : head + 1, :])
        dv.append(mm(probs.astype(BF16), do))
        dprobs = mm(head_lanes(v, head), do, NT)
        delta = jnp.sum(probs * dprobs, axis=0, keepdims=True)
        dscores = (probs * (dprobs - delta)).astype(BF16)
        dk.append(mm(dscores, q))
        dq_t.append(mm(k_t[head * HEAD_DIM : (head + 1) * HEAD_DIM], dscores))
    first = lax.broadcasted_iota(jnp.int32, dv[0].shape, 1) < HEAD_DIM
    dq = jnp.concatenate(dq_t, axis=0).T * SCALE

    def put(slot, value):
        start = pl.multiple_of((slot * n_pairs + pair) * PAIR, PAIR)
        d_ref[0, :, pl.ds(start, PAIR)] = value.astype(BF16)

    put(0, dq)
    put(1, jnp.where(first, dk[0], dk[1]) * SCALE)
    put(2, jnp.where(first, dv[0], dv[1]))


def attend_specs(seq, n_pairs):
    return [
        pl.BlockSpec((1, seq, PAIR), lambda r, p, info: (r, 0, p)),
        pl.BlockSpec((1, seq, PAIR), lambda r, p, info: (r, 0, n_pairs + p)),
        pl.BlockSpec((1, seq, PAIR), lambda r, p, info: (r, 0, 2 * n_pairs + p)),
    ]


VMEM_LIMIT = 50 * 1024 * 1024


def attend(info, qkv):
    rows, seq, width = qkv.shape
    n_pairs = width // (3 * PAIR)
    flops = rows * n_pairs * 2 * 4 * seq * seq * HEAD_DIM
    return pl.pallas_call(
        attend_kernel,
        out_shape=(
            jax.ShapeDtypeStruct((rows, seq, n_pairs * PAIR), BF16),
            jax.ShapeDtypeStruct((rows, n_pairs, 2, seq), F32),
        ),
        grid_spec=pltpu.PrefetchScalarGridSpec(
            num_scalar_prefetch=1,
            grid=(rows, n_pairs),
            in_specs=attend_specs(seq, n_pairs),
            out_specs=(
                pl.BlockSpec((1, seq, PAIR), lambda r, p, info: (r, 0, p)),
                pl.BlockSpec((1, 1, 2, seq), lambda r, p, info: (r, p, 0, 0)),
            ),
        ),
        compiler_params=pltpu.CompilerParams(vmem_limit_bytes=VMEM_LIMIT),
        cost_estimate=pl.CostEstimate(
            flops=4 * flops,
            bytes_accessed=rows * seq * width * 4,
            transcendentals=rows * n_pairs * 2 * seq * seq,
        ),
        name="attend",
    )(info, qkv, qkv, qkv)


def attend_back(info, qkv, grad_mixed, lse):
    rows, seq, width = qkv.shape
    n_pairs = width // (3 * PAIR)
    flops = rows * n_pairs * 2 * 10 * seq * seq * HEAD_DIM
    return pl.pallas_call(
        attend_back_kernel,
        out_shape=jax.ShapeDtypeStruct((rows, seq, width), BF16),
        grid_spec=pltpu.PrefetchScalarGridSpec(
            num_scalar_prefetch=1,
            grid=(rows, n_pairs),
            in_specs=attend_specs(seq, n_pairs)
            + [
                pl.BlockSpec((1, seq, PAIR), lambda r, p, info: (r, 0, p)),
                pl.BlockSpec((1, 1, 2, seq), lambda r, p, info: (r, p, 0, 0)),
            ],
            out_specs=pl.BlockSpec((1, seq, width), lambda r, p, info: (r, 0, 0)),
        ),
        compiler_params=pltpu.CompilerParams(vmem_limit_bytes=VMEM_LIMIT),
        cost_estimate=pl.CostEstimate(
            flops=4 * flops,
            bytes_accessed=rows * seq * width * 6,
            transcendentals=rows * n_pairs * 2 * seq * seq,
        ),
        name="attend_back",
    )(info, qkv, qkv, qkv, grad_mixed, lse)


def ffn_kernel(first, *refs):
    if first:
        nm, nm_t, up, wu, wd, bu, y, gnm, gwu, gwd, gbu = refs
    else:
        nm, nm_t, up, wu, wd, bu, y_in, gnm_in, y, gnm, gwu, gwd, gbu = refs
    step = pl.program_id(0)

    @pl.when(step == 0)
    def _():
        if first:
            y[...] = jnp.zeros_like(y)
            gnm[...] = jnp.zeros_like(gnm)
        else:
            y[...] = y_in[...]
            gnm[...] = gnm_in[...]

    x, g = nm[...], up[...]
    w_up, w_down = wu[...], wd[...]
    hidden = mm(x, w_up) + bu[...]
    cdf = 0.5 * (1.0 + lax.erf(hidden * (1.0 / math.sqrt(2.0))))
    active = (hidden * cdf).astype(BF16)
    slope = cdf + hidden * jnp.exp(-0.5 * hidden * hidden) * (1.0 / math.sqrt(2.0 * math.pi))
    grad_hidden = (mm(g, w_down, NT) * slope).astype(BF16)
    gbu[...] = jnp.sum(grad_hidden.astype(F32), axis=0, keepdims=True)
    y[...] += mm(active, w_down)
    gwd[...] = mm(active, g, TN).astype(BF16)
    gnm[...] += mm(grad_hidden, w_up, NT)
    gwu[...] = mm(nm_t[...], grad_hidden).astype(BF16)


def ffn(nm, nm_t, up, wu, wd, bu, sums=None, block=256):
    tokens, width = nm.shape
    units = wu.shape[1]
    first = sums is None
    whole = lambda shape: pl.BlockSpec(shape, lambda f: (0, 0))
    once = lambda shape: pl.BlockSpec(shape, lambda f: (0, 0), pipeline_mode=pl.Buffered(1))
    in_specs = [
        once((tokens, width)),
        once((width, tokens)),
        once((tokens, width)),
        pl.BlockSpec((width, block), lambda f: (0, f)),
        pl.BlockSpec((block, width), lambda f: (f, 0)),
        pl.BlockSpec((1, block), lambda f: (0, f)),
    ]
    args = [nm, nm_t, up, wu, wd, bu]
    aliases = {}
    if not first:
        in_specs += [once((tokens, width))] * 2
        args += list(sums)
        aliases = {6: 0, 7: 1}
    return pl.pallas_call(
        functools.partial(ffn_kernel, first),
        out_shape=(
            jax.ShapeDtypeStruct((tokens, width), F32),
            jax.ShapeDtypeStruct((tokens, width), F32),
            jax.ShapeDtypeStruct((width, units), BF16),
            jax.ShapeDtypeStruct((units, width), BF16),
            jax.ShapeDtypeStruct((1, units), F32),
        ),
        grid=(units // block,),
        in_specs=in_specs,
        out_specs=(
            whole((tokens, width)),
            whole((tokens, width)),
            pl.BlockSpec((width, block), lambda f: (0, f)),
            pl.BlockSpec((block, width), lambda f: (f, 0)),
            pl.BlockSpec((1, block), lambda f: (0, f)),
        ),
        input_output_aliases=aliases,
        compiler_params=pltpu.CompilerParams(vmem_limit_bytes=VMEM_LIMIT),
        cost_estimate=pl.CostEstimate(
            flops=12 * tokens * width * units,
            bytes_accessed=tokens * width * 30 + 8 * width * units,
            transcendentals=2 * tokens * units,
        ),
        name="ffn_first" if first else "ffn_second",
    )(*args)


def norm(values):
    average = jnp.mean(values, axis=-1, keepdims=True)
    centred = values - average
    inv = lax.rsqrt(jnp.mean(centred * centred, axis=-1, keepdims=True) + EPS)
    return centred * inv, inv


def norm_back(grad, unit, inv, gain):
    scaled = grad * gain
    return inv * (
        scaled
        - jnp.mean(scaled, axis=-1, keepdims=True)
        - unit * jnp.mean(scaled * unit, axis=-1, keepdims=True)
    )


def swap(value, axis):
    return lax.ppermute(value, axis, [(0, 1), (1, 0)])


def part(value, index, count):
    size = value.shape[0] // count
    return lax.dynamic_slice_in_dim(value, index * size, size, 0)


def join(index, mine, other):
    return jnp.where(index == 0, jnp.concatenate([mine, other]), jnp.concatenate([other, mine]))


def fetch_half(weight):
    core = lax.axis_index("core")
    mine = swap(part(weight, core, 2), "mp")
    return join(core, mine, swap(mine, "core"))


def reduce_pieces(own, other):
    core = lax.axis_index("core")
    got_other = swap(part(other, 1 - core, 2), "core")
    mid_other = (part(other, core, 2).astype(F32) + got_other.astype(F32)).astype(BF16)
    got = swap(mid_other, "mp")
    got_own = swap(part(own, 1 - core, 2), "core")
    mid_own = part(own, core, 2).astype(F32) + got_own.astype(F32)
    return (mid_own + got.astype(F32)).astype(BF16)


def spread_pieces(piece):
    core = lax.axis_index("core")
    return join(core, piece, swap(piece, "core")).astype(F32)


def on_device(
    sizes,
    tokens,
    lengths,
    out_grad,
    ln1_gain,
    ln1_shift,
    w_query,
    b_query,
    w_key,
    w_value,
    b_value,
    w_out,
    b_out,
    ln2_gain,
    ln2_shift,
    w_up,
    b_up,
    w_down,
    b_down,
):
    side = lax.axis_index("mp")
    rows_dev, half, width = tokens.shape
    rows = rows_dev // 2
    seq = 2 * half
    total = rows * seq
    heads_width = w_query.shape[1]

    def take_rows(value):
        return jnp.concatenate([part(value, side, 2), swap(part(value, 1 - side, 2), "mp")], axis=1)

    x = take_rows(tokens).astype(F32).reshape(total, width)
    bias_own = jnp.concatenate([b_query, b_value, b_up])
    bias_oth = swap(bias_own, "mp")
    wqkv_own = jnp.concatenate([w_query, w_key, w_value], axis=1)
    wqkv_oth = fetch_half(wqkv_own)
    wout_oth = fetch_half(w_out)
    up = take_rows(out_grad).reshape(total, width)
    wup_oth = fetch_half(w_up)
    wdown_oth = fetch_half(w_down)
    info = jnp.concatenate([(side * half)[None].astype(jnp.int32), part(lengths, side, 2)])

    unit_in, inv_in = norm(x)
    normed_in = (unit_in * ln1_gain + ln1_shift).astype(BF16)

    def project(weight, bias):
        no_key = jnp.zeros((heads_width,), F32)
        full = jnp.concatenate([bias[:heads_width], no_key, bias[heads_width : 2 * heads_width]])
        return (mm(normed_in, weight) + full).astype(BF16).reshape(rows, seq, 3 * heads_width)

    qkv_own = project(wqkv_own, bias_own)
    mixed_own, lse_own = attend(info, qkv_own)
    qkv_oth = project(wqkv_oth, bias_oth)
    mixed_oth, lse_oth = attend(info, qkv_oth)
    mixed_own = mixed_own.reshape(total, heads_width)
    mixed_oth = mixed_oth.reshape(total, heads_width)
    residual = x + mm(mixed_own, w_out) + mm(mixed_oth, wout_oth) + b_out
    unit_mid, inv_mid = norm(residual)
    normed_mid = (unit_mid * ln2_gain + ln2_shift).astype(BF16)
    normed_mid_t = normed_mid.T
    bup_own = bias_own[2 * heads_width :][None]
    bup_oth = bias_oth[2 * heads_width :][None]
    y, gnm, gup_own, gdown_own, gbup_own = ffn(normed_mid, normed_mid_t, up, w_up, w_down, bup_own)
    y, gnm, gup_oth, gdown_oth, gbup_oth = ffn(
        normed_mid, normed_mid_t, up, wup_oth, wdown_oth, bup_oth, (y, gnm)
    )
    up_piece = reduce_pieces(gup_own, gup_oth)
    down_piece = reduce_pieces(gdown_own, gdown_oth)
    up_sum, down_sum = lax.psum((up_piece, down_piece), ("rest", "nbr"))

    out = (residual + y + b_down).astype(BF16).reshape(rows, seq, width)
    up32 = up.astype(F32)
    gl2_gain = jnp.sum(gnm * unit_mid, axis=0)
    gl2_shift = jnp.sum(gnm, axis=0)
    grad_res = up32 + norm_back(gnm, unit_mid, inv_mid, ln2_gain)
    grad_res_low = grad_res.astype(BF16)
    gm_own = mm(grad_res_low, w_out, NT).astype(BF16).reshape(rows, seq, heads_width)
    gm_oth = mm(grad_res_low, wout_oth, NT).astype(BF16).reshape(rows, seq, heads_width)
    d_oth = attend_back(info, qkv_oth, gm_oth, lse_oth).reshape(total, 3 * heads_width)
    d_own = attend_back(info, qkv_own, gm_own, lse_own).reshape(total, 3 * heads_width)
    gwout_own = mm(mixed_own, grad_res_low, TN).astype(BF16)
    gwout_oth = mm(mixed_oth, grad_res_low, TN).astype(BF16)
    gqkv_oth = mm(normed_in, d_oth, TN).astype(BF16)
    gqkv_own = mm(normed_in, d_own, TN).astype(BF16)
    qkv_piece = reduce_pieces(gqkv_own, gqkv_oth)
    wout_piece = reduce_pieces(gwout_own, gwout_oth)
    gate = lax.optimization_barrier((qkv_piece, wout_piece, up_sum, down_sum))
    qkv_piece, wout_piece, up_sum, down_sum = gate
    qkv_sum, wout_sum = lax.psum((qkv_piece, wout_piece), ("rest", "nbr"))
    grad_in = mm(d_own, wqkv_own, NT) + mm(d_oth, wqkv_oth, NT)
    gl1_gain = jnp.sum(grad_in * unit_in, axis=0)
    gl1_shift = jnp.sum(grad_in, axis=0)
    dx = (grad_res + norm_back(grad_in, unit_in, inv_in, ln1_gain)).reshape(rows, seq, width)

    def give_rows(value, sent):
        mine, got = value[:, :half], swap(sent[:, half:], "mp").astype(value.dtype)
        return join(side, mine, got)

    block_out = give_rows(out, out)
    input_grad = give_rows(dx, dx.astype(BF16))

    def bias_sums(d, gbup):
        sums = jnp.sum(d.astype(F32), axis=0)
        return [sums[:heads_width], sums[2 * heads_width :], gbup[0]]

    shared = [gl1_gain, gl1_shift, gl2_gain, gl2_shift, jnp.sum(grad_res, axis=0), jnp.sum(up32, axis=0)]
    mine = jnp.concatenate(shared + bias_sums(d_own, gbup_own))
    sent = jnp.concatenate(shared + bias_sums(d_oth, gbup_oth))
    vec = mine + swap(sent, "mp")
    vec = vec + swap(vec, "core")
    vec = vec + swap(vec, "nbr")
    step = 1
    while step < sizes["rest"]:
        vec = vec + lax.ppermute(vec, "rest", [(i, i ^ step) for i in range(sizes["rest"])])
        step *= 2
    common = [vec[i * width : (i + 1) * width] for i in range(6)]
    split = vec[6 * width :]
    qkv_grad = spread_pieces(qkv_sum)
    return (
        block_out,
        input_grad,
        common[0],
        common[1],
        qkv_grad[:, :heads_width],
        split[:heads_width],
        qkv_grad[:, heads_width : 2 * heads_width],
        qkv_grad[:, 2 * heads_width :],
        split[heads_width : 2 * heads_width],
        spread_pieces(wout_sum),
        common[4],
        common[2],
        common[3],
        spread_pieces(up_sum),
        split[2 * heads_width :],
        spread_pieces(down_sum),
        common[5],
    )


def solution(mesh):
    n_dp, n_mp = mesh.shape["dp"], mesh.shape["mp"]
    names = ("rest", "nbr", "core", "mp")
    inner = Mesh(mesh.devices.reshape(n_dp // 4, 2, 2, n_mp), names)
    dp = ("rest", "nbr", "core")
    in_specs = (
        P(dp, "mp", None),
        P(dp),
        P(dp, "mp", None),
        P(),
        P(),
        P(None, "mp"),
        P("mp"),
        P(None, "mp"),
        P(None, "mp"),
        P("mp"),
        P("mp", None),
        P(),
        P(),
        P(),
        P(None, "mp"),
        P("mp"),
        P("mp", None),
        P(),
    )
    out_specs = (
        P(dp, "mp", None),
        P(dp, "mp", None),
        P(),
        P(),
        P(None, "mp"),
        P("mp"),
        P(None, "mp"),
        P(None, "mp"),
        P("mp"),
        P("mp", None),
        P(),
        P(),
        P(),
        P(None, "mp"),
        P("mp"),
        P("mp", None),
        P(),
    )
    return jax.shard_map(
        functools.partial(on_device, dict(inner.shape)),
        mesh=inner,
        in_specs=in_specs,
        out_specs=out_specs,
        check_vma=False,
    )
```

```python
import functools
import math

import jax
import jax.numpy as jnp
from jax import lax
from jax.experimental import pallas as pl
from jax.experimental.pallas import tpu as pltpu
from jax.sharding import Mesh
from jax.sharding import PartitionSpec as P

HEAD_DIM = 64
PAIR = 2 * HEAD_DIM
EPS = 1e-12
FILL = -1000000000.0
SCALE = 1.0 / math.sqrt(HEAD_DIM)
LOG2E = math.log2(math.e)
F32 = jnp.float32
BF16 = jnp.bfloat16
NT = (((1,), (1,)), ((), ()))
NN = (((1,), (0,)), ((), ()))
TN = (((0,), (0,)), ((), ()))


def mm(a, b, dims=NN):
    return lax.dot_general(a, b, dims, preferred_element_type=F32)


def key_mask(info, row, shape):
    seq = shape[0]
    slot = lax.broadcasted_iota(jnp.int32, shape, 0) + info[0]
    position = jnp.where(slot >= seq, slot - seq, slot)
    return position < info[1 + row]


def head_lanes(value, head):
    lane = lax.broadcasted_iota(jnp.int32, value.shape, 1)
    keep = lane < HEAD_DIM if head == 0 else lane >= HEAD_DIM
    return jnp.where(keep, value, jnp.zeros_like(value))


def attend_kernel(info, q_ref, k_ref, v_ref, o_ref, lse_ref):
    row = pl.program_id(0)
    q, k, v = q_ref[0], k_ref[0], v_ref[0]
    valid = key_mask(info, row, (k.shape[0], q.shape[0]))
    v_t = v.T
    parts = []
    for head in range(2):
        scores = mm(head_lanes(k, head), q, NT) * (SCALE * LOG2E)
        scores = jnp.where(valid, scores, FILL * LOG2E)
        top = jnp.max(scores, axis=0, keepdims=True)
        weight = jnp.exp2(scores - top)
        total = jnp.sum(weight, axis=0, keepdims=True)
        lse_ref[0, 0, head : head + 1, :] = top + jnp.log2(total)
        probs = (weight * (1.0 / total)).astype(BF16)
        parts.append(mm(v_t[head * HEAD_DIM : (head + 1) * HEAD_DIM], probs))
    o_ref[0] = jnp.concatenate(parts, axis=0).T.astype(BF16)


def attend_back_kernel(info, q_ref, k_ref, v_ref, do_ref, lse_ref, d_ref):
    row = pl.program_id(0)
    pair = pl.program_id(1)
    n_pairs = pl.num_programs(1)
    q, k, v, do = q_ref[0], k_ref[0], v_ref[0], do_ref[0]
    valid = key_mask(info, row, (k.shape[0], q.shape[0]))
    k_t = k.T
    dq_t, dk, dv = [], [], []
    for head in range(2):
        scores = mm(head_lanes(k, head), q, NT) * (SCALE * LOG2E)
        scores = jnp.where(valid, scores, FILL * LOG2E)
        probs = jnp.exp2(scores - lse_ref[0, 0, head : head + 1, :])
        dv.append(mm(probs.astype(BF16), do))
        dprobs = mm(head_lanes(v, head), do, NT)
        delta = jnp.sum(probs * dprobs, axis=0, keepdims=True)
        dscores = (probs * (dprobs - delta)).astype(BF16)
        dk.append(mm(dscores, q))
        dq_t.append(mm(k_t[head * HEAD_DIM : (head + 1) * HEAD_DIM], dscores))
    first = lax.broadcasted_iota(jnp.int32, dv[0].shape, 1) < HEAD_DIM
    dq = jnp.concatenate(dq_t, axis=0).T * SCALE

    def put(slot, value):
        start = pl.multiple_of((slot * n_pairs + pair) * PAIR, PAIR)
        d_ref[0, :, pl.ds(start, PAIR)] = value.astype(BF16)

    put(0, dq)
    put(1, jnp.where(first, dk[0], dk[1]) * SCALE)
    put(2, jnp.where(first, dv[0], dv[1]))


def attend_specs(seq, n_pairs):
    return [
        pl.BlockSpec((1, seq, PAIR), lambda r, p, info: (r, 0, p)),
        pl.BlockSpec((1, seq, PAIR), lambda r, p, info: (r, 0, n_pairs + p)),
        pl.BlockSpec((1, seq, PAIR), lambda r, p, info: (r, 0, 2 * n_pairs + p)),
    ]


VMEM_LIMIT = 50 * 1024 * 1024


def cost(micros):
    return pl.CostEstimate(flops=int(micros * 1.15e9), bytes_accessed=1000, transcendentals=0)


def attend(info, qkv):
    rows, seq, width = qkv.shape
    n_pairs = width // (3 * PAIR)
    return pl.pallas_call(
        attend_kernel,
        out_shape=(
            jax.ShapeDtypeStruct((rows, seq, n_pairs * PAIR), BF16),
            jax.ShapeDtypeStruct((rows, n_pairs, 2, seq), F32),
        ),
        grid_spec=pltpu.PrefetchScalarGridSpec(
            num_scalar_prefetch=1,
            grid=(rows, n_pairs),
            in_specs=attend_specs(seq, n_pairs),
            out_specs=(
                pl.BlockSpec((1, seq, PAIR), lambda r, p, info: (r, 0, p)),
                pl.BlockSpec((1, 1, 2, seq), lambda r, p, info: (r, p, 0, 0)),
            ),
        ),
        compiler_params=pltpu.CompilerParams(vmem_limit_bytes=VMEM_LIMIT),
        cost_estimate=cost(10),
        name="attend",
    )(info, qkv, qkv, qkv)


def attend_back(info, qkv, grad_mixed, lse):
    rows, seq, width = qkv.shape
    n_pairs = width // (3 * PAIR)
    return pl.pallas_call(
        attend_back_kernel,
        out_shape=jax.ShapeDtypeStruct((rows, seq, width), BF16),
        grid_spec=pltpu.PrefetchScalarGridSpec(
            num_scalar_prefetch=1,
            grid=(rows, n_pairs),
            in_specs=attend_specs(seq, n_pairs)
            + [
                pl.BlockSpec((1, seq, PAIR), lambda r, p, info: (r, 0, p)),
                pl.BlockSpec((1, 1, 2, seq), lambda r, p, info: (r, p, 0, 0)),
            ],
            out_specs=pl.BlockSpec((1, seq, width), lambda r, p, info: (r, 0, 0)),
        ),
        compiler_params=pltpu.CompilerParams(vmem_limit_bytes=VMEM_LIMIT),
        cost_estimate=cost(13),
        name="attend_back",
    )(info, qkv, qkv, qkv, grad_mixed, lse)


def ffn_kernel(mode, block, info, *refs):
    first, own = mode
    refs = list(refs)
    nm, nm_t, up = refs[:3]
    wa, wb, bu = refs[3:6]
    y_in, gnm_in = (None, None) if first else refs[6:8]
    y, gnm, keep, send, gbu = refs[-5:]
    step = pl.program_id(0)
    core = info[0]

    @pl.when(step == 0)
    def _():
        if first:
            y[...] = jnp.zeros_like(y)
            gnm[...] = jnp.zeros_like(gnm)
        else:
            y[...] = y_in[...]
            gnm[...] = gnm_in[...]

    x, g = nm[...], up[...]
    width = x.shape[1]
    per = width // block
    start = pl.multiple_of(lax.rem(step, per) * block, block)
    part = pl.ds(start, block)
    if own:
        w_up, w_down = wa[...], wb[...]
    else:
        w_up = jnp.where(core == 0, wa[:, part], wb[:, part])
        w_down = jnp.where(core == 0, wb[part, :], wa[part, :])
    hidden = mm(x, w_up) + bu[...]
    cdf = 0.5 * (1.0 + lax.erf(hidden * (1.0 / math.sqrt(2.0))))
    active = (hidden * cdf).astype(BF16)
    slope = cdf + hidden * jnp.exp(-0.5 * hidden * hidden) * (1.0 / math.sqrt(2.0 * math.pi))
    grad_hidden = (mm(g, w_down, NT) * slope).astype(BF16)
    gbu[...] = jnp.sum(grad_hidden.astype(F32), axis=0, keepdims=True)
    y[...] += mm(active, w_down)
    gnm[...] += mm(grad_hidden, w_up, NT)
    grad_down = mm(active, g, TN).astype(BF16)
    grad_up = mm(nm_t[...], grad_hidden).astype(BF16)

    @pl.when(core == 0)
    def _():
        keep[0, :, part] = grad_up
        send[0, part, :] = grad_down

    @pl.when(core != 0)
    def _():
        keep[0, part, :] = grad_down
        send[0, :, part] = grad_up


def ffn(core, nm, nm_t, up, wa, wb, bu, own, sums=None, block=256):
    tokens, width = nm.shape
    units = bu.shape[1]
    first = sums is None
    per = width // block
    whole = lambda shape: pl.BlockSpec(shape, lambda f, info: (0, 0))
    once = lambda shape: pl.BlockSpec(shape, lambda f, info: (0, 0), pipeline_mode=pl.Buffered(1))
    in_specs = [once((tokens, width)), once((width, tokens)), once((tokens, width))]
    if own:
        in_specs += [
            pl.BlockSpec((width, block), lambda f, info: (0, f)),
            pl.BlockSpec((block, width), lambda f, info: (f, 0)),
        ]
    else:
        in_specs += [once((width, width))] * 2
    in_specs += [pl.BlockSpec((1, block), lambda f, info: (0, f))]
    args = [nm, nm_t, up, wa, wb, bu]
    aliases = {}
    if not first:
        in_specs += [once((tokens, width))] * 2
        args += list(sums)
        aliases = {7: 0, 8: 1}
    grads = pl.BlockSpec((1, width, width), lambda f, info: (f // per, 0, 0))
    return pl.pallas_call(
        functools.partial(ffn_kernel, (first, own), block),
        out_shape=(
            jax.ShapeDtypeStruct((tokens, width), F32),
            jax.ShapeDtypeStruct((tokens, width), F32),
            jax.ShapeDtypeStruct((units // width, width, width), BF16),
            jax.ShapeDtypeStruct((units // width, width, width), BF16),
            jax.ShapeDtypeStruct((1, units), F32),
        ),
        grid_spec=pltpu.PrefetchScalarGridSpec(
            num_scalar_prefetch=1,
            grid=(units // block,),
            in_specs=in_specs,
            out_specs=(
                whole((tokens, width)),
                whole((tokens, width)),
                grads,
                grads,
                pl.BlockSpec((1, block), lambda f, info: (0, f)),
            ),
        ),
        input_output_aliases=aliases,
        compiler_params=pltpu.CompilerParams(vmem_limit_bytes=VMEM_LIMIT),
        cost_estimate=cost(22 if own else 15),
        name="ffn_own" if own else "ffn_other",
    )(core, *args)


def norm(values):
    average = jnp.mean(values, axis=-1, keepdims=True)
    centred = values - average
    inv = lax.rsqrt(jnp.mean(centred * centred, axis=-1, keepdims=True) + EPS)
    return centred * inv, inv


def norm_back(grad, unit, inv, gain):
    scaled = grad * gain
    return inv * (
        scaled
        - jnp.mean(scaled, axis=-1, keepdims=True)
        - unit * jnp.mean(scaled * unit, axis=-1, keepdims=True)
    )


def swap(value, axis):
    return lax.ppermute(value, axis, [(0, 1), (1, 0)])


def part(value, index, count):
    size = value.shape[0] // count
    return lax.dynamic_slice_in_dim(value, index * size, size, 0)


def join(index, mine, other):
    return jnp.where(index == 0, jnp.concatenate([mine, other]), jnp.concatenate([other, mine]))


def tie(*values):
    return lax.optimization_barrier(values)


def add_low(a, b):
    return (a.astype(F32) + b.astype(F32)).astype(BF16)


def ladder(sizes):
    steps = [("nbr", lax.axis_index("nbr"), [(0, 1), (1, 0)])]
    bit = 1
    while bit < sizes["rest"]:
        index = (lax.axis_index("rest") // bit) % 2
        steps.append(("rest", index, [(i, i ^ bit) for i in range(sizes["rest"])]))
        bit *= 2
    return steps


def halve(value, step):
    axis, index, perm = step
    got = lax.ppermute(part(value, 1 - index, 2), axis, perm)
    return add_low(part(value, index, 2), got)


def double(value, step):
    axis, index, perm = step
    return join(index, value, lax.ppermute(value, axis, perm))


class Chain:
    def __init__(self, value, moves):
        self.value, self.moves = value, list(moves)

    def go(self):
        if self.moves:
            self.value = self.moves.pop(0)(self.value)


def meet(chains, *values):
    tied = tie(*[c.value for c in chains], *values)
    for c, v in zip(chains, tied):
        c.value = v
    rest = tied[len(chains) :]
    return rest[0] if len(rest) == 1 else rest


def on_device(
    sizes,
    tokens,
    lengths,
    out_grad,
    ln1_gain,
    ln1_shift,
    w_query,
    b_query,
    w_key,
    w_value,
    b_value,
    w_out,
    b_out,
    ln2_gain,
    ln2_shift,
    w_up,
    b_up,
    w_down,
    b_down,
):
    side = lax.axis_index("mp")
    core = lax.axis_index("core")
    nbr = lax.axis_index("nbr")
    rows_dev, half, width = tokens.shape
    rows = rows_dev // 2
    seq = 2 * half
    total = rows * seq
    heads = w_query.shape[1]
    units = w_up.shape[1] // 2
    steps = ladder(sizes)

    def by_core(first, second):
        return jnp.where(core == 0, first, second)

    def take_rows(mine, got):
        return jnp.concatenate([part(mine, side, 2), got], axis=1).reshape(total, width)

    w_send = jnp.where(
        nbr == 0, by_core(w_query, w_value), by_core(w_key, w_out.T)
    )
    w_send, t_send = tie(w_send, part(tokens, 1 - side, 2))
    w_mine = swap(w_send, "mp")
    got_tokens = swap(t_send, "mp")
    bias_own = jnp.concatenate([b_query, b_value, b_up])
    w_mine, bias_own = tie(w_mine, bias_own)
    bias_oth = swap(bias_own, "mp")
    w_near = swap(w_mine, "nbr")
    w_pair = jnp.where(
        nbr == 0, jnp.concatenate([w_mine, w_near]), jnp.concatenate([w_near, w_mine])
    )
    w_cross = swap(w_pair, "core")
    up_halves = [w_up[:, :units], w_up[:, units:]]
    down_halves = [w_down[:units], w_down[units:]]
    f_send0 = part(by_core(up_halves[0], down_halves[0]), nbr, 2)
    f_send1 = by_core(up_halves[1], down_halves[1])
    g_send = part(out_grad, 1 - side, 2)
    got_tokens, f_send0, g_send = tie(got_tokens, f_send0, g_send)
    x_low = take_rows(tokens, got_tokens)
    f_mine0 = swap(f_send0, "mp")
    x = x_low.astype(F32)
    wqkv_own = jnp.concatenate([w_query, w_key, w_value], axis=1)
    info = jnp.concatenate([(side * half)[None].astype(jnp.int32), part(lengths, side, 2)])
    q_k = by_core(w_pair, w_cross)
    v_o = by_core(w_cross, w_pair)
    wqkv_oth = jnp.concatenate([q_k[:width], q_k[width:], v_o[:width]], axis=1)
    wout_t = v_o[width:]

    unit_in, inv_in = norm(x)
    normed_in = (unit_in * ln1_gain + ln1_shift).astype(BF16)

    def project(weight, bias):
        no_key = jnp.zeros((heads,), F32)
        full = jnp.concatenate([bias[:heads], no_key, bias[heads : 2 * heads]])
        return (mm(normed_in, weight) + full).astype(BF16).reshape(rows, seq, 3 * heads)

    qkv_own = project(wqkv_own, bias_own)
    qkv_oth = project(wqkv_oth, bias_oth)
    qkv_own, qkv_oth = tie(qkv_own, qkv_oth)
    mixed_own, lse_own = attend(info, qkv_own)
    qkv_oth, f_mine0, f_send1, mixed_own = tie(qkv_oth, f_mine0, f_send1, mixed_own)
    f_mine1 = swap(f_send1, "mp")
    got_grad = swap(g_send, "mp")
    f_half0 = join(nbr, f_mine0, swap(f_mine0, "nbr"))
    mixed_oth, lse_oth = attend(info, qkv_oth)
    mixed_oth, f_half0, got_grad = tie(mixed_oth, f_half0, got_grad)
    up = take_rows(out_grad, got_grad)
    f_cross0 = swap(f_half0, "core")
    mixed_own = mixed_own.reshape(total, heads)
    mixed_oth = mixed_oth.reshape(total, heads)
    residual = x + mm(mixed_own, w_out) + mm(mixed_oth, wout_t, NT) + b_out
    unit_mid, inv_mid = norm(residual)
    normed_mid = (unit_mid * ln2_gain + ln2_shift).astype(BF16)
    normed_mid_t = normed_mid.T
    bup_own = bias_own[2 * heads :][None]
    bup_oth = bias_oth[2 * heads :][None]
    core_info = core.astype(jnp.int32)[None]
    feed = functools.partial(ffn, core_info, normed_mid, normed_mid_t, up)

    y, gnm, f_keep0, f_give0, gbup0 = feed(f_half0, f_cross0, bup_oth[:, :units], False)
    f_keep0, f_give0 = f_keep0[0], f_give0[0]
    y, f_give0, f_mine1 = tie(y, f_give0, f_mine1)
    f_cross1 = swap(f_mine1, "core")
    f_swap0 = swap(f_give0, "core")
    y, gnm, f_keep1, f_give1, gbup1 = feed(f_mine1, f_cross1, bup_oth[:, units:], False, (y, gnm))
    f_keep1, f_give1 = f_keep1[0], f_give1[0]
    y, f_oth0, f_give1 = tie(y, add_low(f_keep0, f_swap0), f_give1)
    f_got0 = swap(f_oth0, "mp")
    f_swap1 = swap(f_give1, "core")
    y, gnm, f_keep_own, f_give_own, gbup_own = feed(w_up, w_down, bup_own, True, (y, gnm))
    gnm, f_got0, f_oth1, f_give_own = tie(gnm, f_got0, add_low(f_keep1, f_swap1), f_give_own)
    f_got1 = swap(f_oth1, "mp")
    f_own = add_low(f_keep_own, swap(f_give_own, "core"))

    up32 = up.astype(F32)
    gl2_gain = jnp.sum(gnm * unit_mid, axis=0)
    gl2_shift = jnp.sum(gnm, axis=0)
    grad_res = up32 + norm_back(gnm, unit_mid, inv_mid, ln2_gain)
    grad_res_low = grad_res.astype(BF16)
    gm_own = mm(grad_res_low, w_out, NT).astype(BF16).reshape(rows, seq, heads)
    gm_oth = mm(grad_res_low, wout_t).astype(BF16).reshape(rows, seq, heads)
    moves = [functools.partial(halve, step=step) for step in steps]
    moves += [functools.partial(double, step=step) for step in reversed(steps)]
    moves += [lambda v: (v, swap(v, "core"))]
    f0 = Chain(add_low(f_own[0], f_got0), moves)
    gm_oth = meet([f0], gm_oth)
    f0.go()
    d_oth = attend_back(info, qkv_oth, gm_oth, lse_oth).reshape(total, 3 * heads)
    d_oth, f_got1 = meet([f0], d_oth, f_got1)
    f1 = Chain(add_low(f_own[1], f_got1), moves)

    def core_sum(first, second):
        return add_low(by_core(first, second), swap(by_core(second, first), "core"))

    def attn_sum(d, mixed):
        g = mm(normed_in, d, TN).astype(BF16)
        o = mm(grad_res_low, mixed, TN).astype(BF16)
        return core_sum(g[:, : 2 * heads], jnp.concatenate([g[:, 2 * heads :], o], axis=1))

    a_oth = attn_sum(d_oth, mixed_oth)
    gm_own, a_oth = meet([f0, f1], gm_own, a_oth)
    a_got = swap(a_oth, "mp")
    f0.go()
    f1.go()
    d_own = attend_back(info, qkv_own, gm_own, lse_own).reshape(total, 3 * heads)
    d_own = meet([f0, f1], d_own)
    f0.go()
    a_own = attn_sum(d_own, mixed_own)
    d_own, a_own = meet([f0], d_own, a_own)
    f0.go()
    f1.go()
    grad_in = mm(d_own, wqkv_own, NT) + mm(d_oth, wqkv_oth, NT)
    gl1_gain = jnp.sum(grad_in * unit_in, axis=0)
    gl1_shift = jnp.sum(grad_in, axis=0)
    dx = (grad_res + norm_back(grad_in, unit_in, inv_in, ln1_gain)).reshape(rows, seq, width)

    def bias_sums(d, gbup):
        sums = jnp.sum(d.astype(F32), axis=0)
        return [sums[:heads], sums[2 * heads :]] + [g[0] for g in gbup]

    shared = [gl1_gain, gl1_shift, gl2_gain, gl2_shift, jnp.sum(grad_res, axis=0), jnp.sum(up32, axis=0)]
    mine = jnp.concatenate(shared + bias_sums(d_own, [gbup_own]))
    sent = jnp.concatenate(shared + bias_sums(d_oth, [gbup0, gbup1]))
    out = (residual + y + b_down).astype(BF16).reshape(rows, seq, width)
    mine, sent, a_got, out, dx = meet([f0, f1], mine, sent, a_got, out, dx)
    att = Chain(add_low(a_own, a_got), moves)
    vec_moves = [lambda v: v + swap(v, "core")]
    vec_moves += [lambda v, s=s: v + lax.ppermute(v, s[0], s[2]) for s in steps]
    out_got = swap(out[:, half:], "mp")
    dx_got = swap(dx[:, half:].astype(BF16), "mp")
    vec = Chain(mine + swap(sent, "mp"), vec_moves)
    chains = [att, f1, f0]
    for c in chains:
        c.go()
    while att.moves:
        meet([c for c in chains if c.moves] + [vec])
        for c in chains + [vec]:
            c.go()

    block_out = join(side, out[:, :half], out_got)
    input_grad = join(side, dx[:, :half], dx_got.astype(F32))
    common = [vec.value[i * width : (i + 1) * width] for i in range(6)]
    split = vec.value[6 * width :]
    up_sum = [by_core(*c.value).astype(F32) for c in (f0, f1)]
    down_sum = [by_core(*c.value[::-1]).astype(F32) for c in (f0, f1)]
    qk_sum = by_core(*att.value).astype(F32)
    vo_sum = by_core(*att.value[::-1]).astype(F32)
    return (
        block_out,
        input_grad,
        common[0],
        common[1],
        qk_sum[:, :heads],
        split[:heads],
        qk_sum[:, heads:],
        vo_sum[:, :heads],
        split[heads : 2 * heads],
        vo_sum[:, heads:].T,
        common[4],
        common[2],
        common[3],
        jnp.concatenate(up_sum, axis=1),
        split[2 * heads :],
        jnp.concatenate(down_sum, axis=0),
        common[5],
    )


def solution(mesh):
    n_dp, n_mp = mesh.shape["dp"], mesh.shape["mp"]
    names = ("rest", "nbr", "core", "mp")
    inner = Mesh(mesh.devices.reshape(n_dp // 4, 2, 2, n_mp), names)
    dp = ("rest", "nbr", "core")
    in_specs = (
        P(dp, "mp", None),
        P(dp),
        P(dp, "mp", None),
        P(),
        P(),
        P(None, "mp"),
        P("mp"),
        P(None, "mp"),
        P(None, "mp"),
        P("mp"),
        P("mp", None),
        P(),
        P(),
        P(),
        P(None, "mp"),
        P("mp"),
        P("mp", None),
        P(),
    )
    out_specs = (
        P(dp, "mp", None),
        P(dp, "mp", None),
        P(),
        P(),
        P(None, "mp"),
        P("mp"),
        P(None, "mp"),
        P(None, "mp"),
        P("mp"),
        P("mp", None),
        P(),
        P(),
        P(),
        P(None, "mp"),
        P("mp"),
        P("mp", None),
        P(),
    )
    return jax.shard_map(
        functools.partial(on_device, dict(inner.shape)),
        mesh=inner,
        in_specs=in_specs,
        out_specs=out_specs,
        check_vma=False,
    )
```

```python
import functools
import math

import jax
import jax.numpy as jnp
from jax import lax
from jax.experimental import pallas as pl
from jax.experimental.pallas import tpu as pltpu
from jax.sharding import Mesh
from jax.sharding import PartitionSpec as P

HEAD_DIM = 64
PAIR = 2 * HEAD_DIM
EPS = 1e-12
FILL = -1000000000.0
SCALE = 1.0 / math.sqrt(HEAD_DIM)
LOG2E = math.log2(math.e)
F32 = jnp.float32
BF16 = jnp.bfloat16
NT = (((1,), (1,)), ((), ()))
NN = (((1,), (0,)), ((), ()))
TN = (((0,), (0,)), ((), ()))


def mm(a, b, dims=NN):
    return lax.dot_general(a, b, dims, preferred_element_type=F32)


def key_mask(info, row, shape):
    seq = shape[0]
    slot = lax.broadcasted_iota(jnp.int32, shape, 0) + info[0]
    position = jnp.where(slot >= seq, slot - seq, slot)
    return position < info[3 + row]


def head_lanes(value, head):
    lane = lax.broadcasted_iota(jnp.int32, value.shape, 1)
    keep = lane < HEAD_DIM if head == 0 else lane >= HEAD_DIM
    return jnp.where(keep, value, jnp.zeros_like(value))


def attend_kernel(info, q_ref, k_ref, v_ref, o_ref, lse_ref):
    row = pl.program_id(0)
    q, k, v = q_ref[0], k_ref[0], v_ref[0]
    valid = key_mask(info, row, (k.shape[0], q.shape[0]))
    v_t = v.T
    parts = []
    for head in range(2):
        scores = mm(head_lanes(k, head), q, NT) * (SCALE * LOG2E)
        scores = jnp.where(valid, scores, FILL * LOG2E)
        top = jnp.max(scores, axis=0, keepdims=True)
        weight = jnp.exp2(scores - top)
        total = jnp.sum(weight, axis=0, keepdims=True)
        lse_ref[0, 0, head : head + 1, :] = top + jnp.log2(total)
        probs = (weight * (1.0 / total)).astype(BF16)
        parts.append(mm(v_t[head * HEAD_DIM : (head + 1) * HEAD_DIM], probs))
    o_ref[0] = jnp.concatenate(parts, axis=0).T.astype(BF16)


def attend_back_kernel(info, q_ref, k_ref, v_ref, do_ref, lse_ref, d_ref, sum_ref):
    row = pl.program_id(0)
    pair = pl.program_id(1)
    n_pairs = pl.num_programs(1)
    q, k, v, do = q_ref[0], k_ref[0], v_ref[0], do_ref[0]
    valid = key_mask(info, row, (k.shape[0], q.shape[0]))
    k_t = k.T
    dq_t, dk, dv = [], [], []
    for head in range(2):
        scores = mm(head_lanes(k, head), q, NT) * (SCALE * LOG2E)
        scores = jnp.where(valid, scores, FILL * LOG2E)
        probs = jnp.exp2(scores - lse_ref[0, 0, head : head + 1, :])
        dv.append(mm(probs.astype(BF16), do))
        dprobs = mm(head_lanes(v, head), do, NT)
        delta = jnp.sum(probs * dprobs, axis=0, keepdims=True)
        dscores = (probs * (dprobs - delta)).astype(BF16)
        dk.append(mm(dscores, q))
        dq_t.append(mm(k_t[head * HEAD_DIM : (head + 1) * HEAD_DIM], dscores))
    first = lax.broadcasted_iota(jnp.int32, dv[0].shape, 1) < HEAD_DIM
    dq = jnp.concatenate(dq_t, axis=0).T * SCALE

    def put(slot, value):
        start = pl.multiple_of((slot * n_pairs + pair) * PAIR, PAIR)
        low = value.astype(BF16)
        d_ref[0, :, pl.ds(start, PAIR)] = low
        sum_ref[0, :, pl.ds(start, PAIR)] = jnp.sum(low.astype(F32), axis=0, keepdims=True)

    put(0, dq)
    put(1, jnp.where(first, dk[0], dk[1]) * SCALE)
    put(2, jnp.where(first, dv[0], dv[1]))


def attend_specs(seq, n_pairs):
    return [
        pl.BlockSpec((1, seq, PAIR), lambda r, p, info: (r, 0, p)),
        pl.BlockSpec((1, seq, PAIR), lambda r, p, info: (r, 0, n_pairs + p)),
        pl.BlockSpec((1, seq, PAIR), lambda r, p, info: (r, 0, 2 * n_pairs + p)),
    ]


VMEM_LIMIT = 50 * 1024 * 1024


def cost(micros):
    return pl.CostEstimate(flops=int(micros * 1.15e9), bytes_accessed=1000, transcendentals=0)


def attend(info, qkv):
    rows, seq, width = qkv.shape
    n_pairs = width // (3 * PAIR)
    return pl.pallas_call(
        attend_kernel,
        out_shape=(
            jax.ShapeDtypeStruct((rows, seq, n_pairs * PAIR), BF16),
            jax.ShapeDtypeStruct((rows, n_pairs, 2, seq), F32),
        ),
        grid_spec=pltpu.PrefetchScalarGridSpec(
            num_scalar_prefetch=1,
            grid=(rows, n_pairs),
            in_specs=attend_specs(seq, n_pairs),
            out_specs=(
                pl.BlockSpec((1, seq, PAIR), lambda r, p, info: (r, 0, p)),
                pl.BlockSpec((1, 1, 2, seq), lambda r, p, info: (r, p, 0, 0)),
            ),
        ),
        compiler_params=pltpu.CompilerParams(vmem_limit_bytes=VMEM_LIMIT),
        cost_estimate=cost(10),
        name="attend",
    )(info, qkv, qkv, qkv)


def attend_back(info, qkv, grad_mixed, lse):
    rows, seq, width = qkv.shape
    n_pairs = width // (3 * PAIR)
    return pl.pallas_call(
        attend_back_kernel,
        out_shape=(
            jax.ShapeDtypeStruct((rows, seq, width), BF16),
            jax.ShapeDtypeStruct((rows, 1, width), F32),
        ),
        grid_spec=pltpu.PrefetchScalarGridSpec(
            num_scalar_prefetch=1,
            grid=(rows, n_pairs),
            in_specs=attend_specs(seq, n_pairs)
            + [
                pl.BlockSpec((1, seq, PAIR), lambda r, p, info: (r, 0, p)),
                pl.BlockSpec((1, 1, 2, seq), lambda r, p, info: (r, p, 0, 0)),
            ],
            out_specs=(
                pl.BlockSpec((1, seq, width), lambda r, p, info: (r, 0, 0)),
                pl.BlockSpec((1, 1, width), lambda r, p, info: (r, 0, 0)),
            ),
        ),
        compiler_params=pltpu.CompilerParams(vmem_limit_bytes=VMEM_LIMIT),
        cost_estimate=cost(13),
        name="attend_back",
    )(info, qkv, qkv, qkv, grad_mixed, lse)


def feed_kernel(first, own, info, *refs):
    refs = list(refs)
    nm, wa, wb, bu = refs[:4]
    refs = refs[4:]
    if own:
        wu, wd = refs[:2]
        refs = refs[2:]
    nt_hbm, up_hbm = refs[:2]
    refs = refs[2:]
    if not first:
        y_hbm, gnm_hbm = refs[:2]
        refs = refs[2:]
    y_out, gnm_out, keep, send, gbu, nt, up, y, gnm, hidden, sems = refs
    step = pl.program_id(0)
    last = pl.num_programs(0) - 1
    core = info[1]
    copy_up = pltpu.make_async_copy(up_hbm, up, sems.at[0])
    copies = [pltpu.make_async_copy(nt_hbm, nt, sems.at[1])]
    if not first:
        copies += [
            pltpu.make_async_copy(y_hbm, y, sems.at[2]),
            pltpu.make_async_copy(gnm_hbm, gnm, sems.at[3]),
        ]
    out_y = pltpu.make_async_copy(y, y_out, sems.at[4])
    out_gnm = pltpu.make_async_copy(gnm, gnm_out, sems.at[5])

    @pl.when(step == 0)
    def _():
        copy_up.start()
        for copy in copies:
            copy.start()

    def pick():
        w_up = jnp.where(core == 0, wa[...], wb[...])
        w_down = jnp.where(core == 0, wb[...], wa[...])
        if own:
            w_up = jnp.where(step == 0, w_up, wu[...])
            w_down = jnp.where(step == 0, w_down, wd[...])
        return w_up, w_down

    w_up, w_down = pick()
    hidden[...] = mm(nm[...], w_up) + bu[...]

    @pl.when(step == 0)
    def _():
        copy_up.wait()

    h = hidden[...]
    cdf = 0.5 * (1.0 + lax.erf(h * (1.0 / math.sqrt(2.0))))
    active = (h * cdf).astype(BF16)
    slope = cdf + h * jnp.exp(-0.5 * h * h) * (1.0 / math.sqrt(2.0 * math.pi))
    grad_hidden = (mm(up[...], w_down, NT) * slope).astype(BF16)
    gbu[...] = jnp.sum(grad_hidden.astype(F32), axis=0, keepdims=True)
    grad_down = mm(active, up[...], TN).astype(BF16)

    @pl.when(step == 0)
    def _():
        for copy in copies:
            copy.wait()

    if first:
        y[...] = mm(active, w_down)
        gnm[...] = mm(grad_hidden, w_up, NT)
    else:
        y[...] += mm(active, w_down)
        gnm[...] += mm(grad_hidden, w_up, NT)

    @pl.when(step == last)
    def _():
        out_y.start()
        out_gnm.start()

    grad_up = mm(nt[...], grad_hidden).astype(BF16)
    keep[0] = jnp.where(core == 0, grad_up, grad_down)
    send[0] = jnp.where(core == 0, grad_down, grad_up)

    @pl.when(step == last)
    def _():
        out_y.wait()
        out_gnm.wait()


def feed(info, nm, nt, up, wa, wb, bu, own=None, sums=None):
    tokens, width = nm.shape
    count = bu.shape[1] // width
    first = sums is None
    once = lambda shape: pl.BlockSpec(shape, lambda f, info: (0, 0), pipeline_mode=pl.Buffered(1))
    place = pl.BlockSpec(memory_space=pl.ANY)
    row = pl.BlockSpec((1, width), lambda f, info: (0, f))
    in_specs = [once((tokens, width)), once(wa.shape), once(wb.shape), row]
    args = [nm, wa, wb, bu]
    if own is not None:
        in_specs += [
            pl.BlockSpec((width, width), lambda f, info: (0, jnp.maximum(f - 1, 0))),
            pl.BlockSpec((width, width), lambda f, info: (jnp.maximum(f - 1, 0), 0)),
        ]
        args += list(own)
    in_specs += [place] * 2
    args += [nt, up]
    if not first:
        in_specs += [place] * 2
        args += list(sums)
    grads = pl.BlockSpec((1, width, width), lambda f, info: (f, 0, 0))
    return pl.pallas_call(
        functools.partial(feed_kernel, first, own is not None),
        out_shape=(
            shaped(tokens, width, dtype=F32),
            shaped(tokens, width, dtype=F32),
            shaped(count, width, width),
            shaped(count, width, width),
            shaped(1, count * width, dtype=F32),
        ),
        grid_spec=pltpu.PrefetchScalarGridSpec(
            num_scalar_prefetch=1,
            grid=(count,),
            in_specs=in_specs,
            out_specs=(place, place, grads, grads, row),
            scratch_shapes=[
                pltpu.VMEM((width, tokens), BF16),
                pltpu.VMEM((tokens, width), BF16),
                pltpu.VMEM((tokens, width), F32),
                pltpu.VMEM((tokens, width), F32),
                pltpu.VMEM((tokens, width), F32),
                pltpu.SemaphoreType.DMA((6,)),
            ],
        ),
        compiler_params=pltpu.CompilerParams(vmem_limit_bytes=VMEM_LIMIT),
        cost_estimate=cost(12 * count),
        name="feed_own" if own is not None else "feed_other",
    )(info, *args)


def norm(values):
    average = jnp.mean(values, axis=-1, keepdims=True)
    centred = values - average
    inv = lax.rsqrt(jnp.mean(centred * centred, axis=-1, keepdims=True) + EPS)
    return centred * inv, inv


def norm_back(grad, unit, inv, gain):
    scaled = grad * gain
    return inv * (
        scaled
        - jnp.mean(scaled, axis=-1, keepdims=True)
        - unit * jnp.mean(scaled * unit, axis=-1, keepdims=True)
    )


def stack(first, second):
    return jnp.concatenate([first, second], axis=0)


def row_grid(kernel, name, micros, rows, in_specs, out_shape, out_specs, args):
    return pl.pallas_call(
        kernel,
        out_shape=out_shape,
        grid_spec=pltpu.PrefetchScalarGridSpec(
            num_scalar_prefetch=1, grid=(rows,), in_specs=in_specs, out_specs=out_specs
        ),
        compiler_params=pltpu.CompilerParams(vmem_limit_bytes=VMEM_LIMIT),
        cost_estimate=cost(micros),
        name=name,
    )(*args)


def fixed(shape):
    return pl.BlockSpec(shape, lambda r, info: (0,) * len(shape))


def const(shape):
    return pl.BlockSpec(
        shape, lambda r, info: (0,) * len(shape), pipeline_mode=pl.Buffered(1)
    )


def per_row(*shape):
    return pl.BlockSpec((1,) + shape, lambda r, info: (r,) + (0,) * len(shape))


def kept_row(*shape):
    return pl.BlockSpec((1,) + shape, lambda r, info: (info[2] + r,) + (0,) * len(shape))


def shaped(*shape, dtype=BF16):
    return jax.ShapeDtypeStruct(shape, dtype)


def enter_kernel(info, tok, got, wq, wk, wv, bias, gain, shift, x_out, n_out, nt_out, qkv):
    heads = wq.shape[1]
    x = stack(tok[0], got[0])
    x_out[0] = x
    unit, _ = norm(x.astype(F32))
    normed = (unit * gain[...] + shift[...]).astype(BF16)
    n_out[0] = normed
    nt_out[...] = normed.T
    qkv[0, :, :heads] = (mm(normed, wq[...]) + bias[:, :heads]).astype(BF16)
    qkv[0, :, heads : 2 * heads] = mm(normed, wk[...]).astype(BF16)
    qkv[0, :, 2 * heads :] = (mm(normed, wv[...]) + bias[:, heads : 2 * heads]).astype(BF16)


def enter(info, tokens, got, wq, wk, wv, bias, gain, shift):
    rows, half, width = got.shape
    seq, heads = 2 * half, wq.shape[1]
    return row_grid(
        enter_kernel,
        "enter",
        0,
        rows,
        [kept_row(half, width), per_row(half, width)]
        + [const(wq.shape)] * 3
        + [const(bias.shape)]
        + [const((1, width))] * 2,
        (
            shaped(rows, seq, width),
            shaped(rows, seq, width),
            shaped(width, rows * seq),
            shaped(rows, seq, 3 * heads),
        ),
        (
            per_row(seq, width),
            per_row(seq, width),
            pl.BlockSpec((width, seq), lambda r, info: (0, r)),
            per_row(seq, 3 * heads),
        ),
        (info, tokens, got, wq, wk, wv, bias, gain[None], shift[None]),
    )


def other_heads_kernel(info, n, p0, p1, p2, p3, bias, qkv, w):
    heads = w.shape[1] // 3

    @pl.when(pl.program_id(0) == 0)
    def _():
        nbr, core = info[3 + pl.num_programs(0)], info[1]
        size = p0.shape[0]
        for index, piece in enumerate((p0, p1, p2, p3)):
            row = 1 - nbr if index >= 2 else nbr
            col = 1 - core if index % 2 else core
            start = pl.multiple_of((2 * row + col) * size, size)
            w[pl.ds(start, size), :] = piece[...]

    full = jnp.concatenate(
        [bias[:, :heads], jnp.zeros((1, heads), F32), bias[:, heads : 2 * heads]], axis=1
    )
    qkv[0] = (mm(n[0], w[...]) + full).astype(BF16)


def other_heads(info, n, pieces, bias):
    rows, seq, width = n.shape
    size, wide = pieces[0].shape
    return row_grid(
        other_heads_kernel,
        "other_heads",
        0,
        rows,
        [per_row(seq, width)] + [const((size, wide))] * 4 + [const(bias.shape)],
        (shaped(rows, seq, wide), shaped(width, wide)),
        (per_row(seq, wide), fixed((width, wide))),
        (info, n, *pieces, bias),
    )


def middle_kernel(
    info, x, m_own, m_oth, w_own, w_mine, w_cross, b_out, gain, shift, grad, got, res, nm, nm_t, up, w_oth
):
    @pl.when(pl.program_id(0) == 0)
    def _():
        size = w_mine.shape[0]
        w_oth[pl.ds(pl.multiple_of(info[1] * size, size), size), :] = w_mine[...]
        w_oth[pl.ds(pl.multiple_of((1 - info[1]) * size, size), size), :] = w_cross[...]

    attended = mm(m_own[0], w_own[...]) + mm(m_oth[0], w_oth[...])
    residual = x[0].astype(F32) + attended + b_out[...]
    res[0] = residual
    unit, _ = norm(residual)
    normed = (unit * gain[...] + shift[...]).astype(BF16)
    nm[0] = normed
    nm_t[...] = normed.T
    up[0] = stack(grad[0], got[0])


def middle(info, x, m_own, m_oth, w_own, w_mine, w_cross, b_out, gain, shift, grad, got):
    rows, seq, width = x.shape
    heads = w_own.shape[0]
    return row_grid(
        middle_kernel,
        "middle",
        0,
        rows,
        [per_row(seq, width), per_row(seq, heads), per_row(seq, heads)]
        + [const(w_own.shape), const(w_mine.shape), const(w_mine.shape)]
        + [const((1, width))] * 3
        + [kept_row(seq // 2, width), per_row(seq // 2, width)],
        (
            shaped(rows, seq, width, dtype=F32),
            shaped(rows, seq, width),
            shaped(width, rows * seq),
            shaped(rows, seq, width),
            shaped(heads, width),
        ),
        (
            per_row(seq, width),
            per_row(seq, width),
            pl.BlockSpec((width, seq), lambda r, info: (0, r)),
            per_row(seq, width),
            fixed((heads, width)),
        ),
        (info, x, m_own, m_oth, w_own, w_mine, w_cross, b_out[None], gain[None], shift[None], grad, got),
    )


def middle_back_kernel(
    info, gnm, res, y, up, gain, b_down, w_own, w_oth, keep, send, gres, glow_t, gm_own, gm_oth, sums
):
    half = keep.shape[1]
    residual, grad, upstream = res[0], gnm[0], up[0].astype(F32)
    out = (residual + y[0] + b_down[...]).astype(BF16)
    keep[0] = out[:half]
    send[0] = out[half:]
    unit, inv = norm(residual)
    total = upstream + norm_back(grad, unit, inv, gain[...])
    gres[0] = total
    low = total.astype(BF16)
    glow_t[...] = low.T
    gm_own[0] = mm(low, w_own[...], NT).astype(BF16)
    gm_oth[0] = mm(low, w_oth[...], NT).astype(BF16)

    @pl.when(pl.program_id(0) == 0)
    def _():
        sums[...] = jnp.zeros_like(sums)

    for index, value in enumerate((grad * unit, grad, total, upstream)):
        sums[index : index + 1, :] += jnp.sum(value, axis=0, keepdims=True)


def middle_back(info, gnm, res, y, up, gain, b_down, w_own, w_oth):
    rows, seq, width = res.shape
    heads = w_own.shape[0]
    row = per_row(seq, width)
    half = per_row(seq // 2, width)
    return row_grid(
        middle_back_kernel,
        "middle_back",
        0,
        rows,
        [row] * 4 + [const((1, width))] * 2 + [const((heads, width))] * 2,
        (
            shaped(rows, seq // 2, width),
            shaped(rows, seq // 2, width),
            shaped(rows, seq, width, dtype=F32),
            shaped(width, rows * seq),
            shaped(rows, seq, heads),
            shaped(rows, seq, heads),
            shaped(8, width, dtype=F32),
        ),
        (
            half,
            half,
            row,
            pl.BlockSpec((width, seq), lambda r, info: (0, r)),
            per_row(seq, heads),
            per_row(seq, heads),
            fixed((8, width)),
        ),
        (info, gnm, res, y, up, gain[None], b_down[None], w_own, w_oth),
    )


def weights_kernel(info, nt, d, glow_t, mixed, keep, send):
    heads = mixed.shape[1]
    g = mm(nt[...], d[...]).astype(BF16)
    o = mm(glow_t[...], mixed[...]).astype(BF16)
    cut = 2 * heads

    @pl.when(info[1] == 0)
    def _():
        keep[...] = g[:, :cut]
        send[:, :heads] = g[:, cut:]
        send[:, heads:] = o

    @pl.when(info[1] != 0)
    def _():
        send[...] = g[:, :cut]
        keep[:, :heads] = g[:, cut:]
        keep[:, heads:] = o


def weights(info, nt, d, glow_t, mixed, block=256):
    width, tokens = nt.shape
    heads = mixed.shape[1]
    part = pl.BlockSpec((block, tokens), lambda r, info: (r, 0))
    result = pl.BlockSpec((block, 2 * heads), lambda r, info: (r, 0))
    return row_grid(
        weights_kernel,
        "weights",
        0,
        width // block,
        [part, const(d.shape), part, const(mixed.shape)],
        (shaped(width, 2 * heads), shaped(width, 2 * heads)),
        (result, result),
        (info, nt, d, glow_t, mixed),
    )


def leave_kernel(info, d_own, d_oth, wq, wk, wv, w_oth, x, gres, gain, keep, send, sums):
    heads = wq.shape[1]
    half = keep.shape[1]
    grad = (
        mm(d_own[0, :, :heads], wq[...], NT)
        + mm(d_own[0, :, heads : 2 * heads], wk[...], NT)
        + mm(d_own[0, :, 2 * heads :], wv[...], NT)
        + mm(d_oth[0], w_oth[...], NT)
    )
    unit, inv = norm(x[0].astype(F32))
    total = gres[0] + norm_back(grad, unit, inv, gain[...])
    keep[0] = total[:half]
    send[0] = total[half:].astype(BF16)

    @pl.when(pl.program_id(0) == 0)
    def _():
        sums[...] = jnp.zeros_like(sums)

    for index, value in enumerate((grad * unit, grad)):
        sums[index : index + 1, :] += jnp.sum(value, axis=0, keepdims=True)


def leave(info, d_own, d_oth, wq, wk, wv, w_oth, x, gres, gain):
    rows, seq, width = x.shape
    row = per_row(seq, width)
    half = per_row(seq // 2, width)
    wide = per_row(seq, d_own.shape[2])
    return row_grid(
        leave_kernel,
        "leave",
        10,
        rows,
        [wide, wide]
        + [const(wq.shape)] * 3
        + [const(w_oth.shape), row, row, const((1, width))],
        (
            shaped(rows, seq // 2, width, dtype=F32),
            shaped(rows, seq // 2, width),
            shaped(8, width, dtype=F32),
        ),
        (half, half, fixed((8, width))),
        (info, d_own, d_oth, wq, wk, wv, w_oth, x, gres, gain[None]),
    )


def spread_kernel(info, mine, cross, q, k, v, o):
    heads = q.shape[1]

    def write(first, second):
        q[...] = first[:, :heads].astype(F32)
        k[...] = first[:, heads:].astype(F32)
        v[...] = second[:, :heads].astype(F32)
        o[...] = second[:, heads:].astype(F32).T

    @pl.when(info[1] == 0)
    def _():
        write(mine, cross)

    @pl.when(info[1] != 0)
    def _():
        write(cross, mine)


def spread(info, mine, cross, block=256):
    width, both = mine.shape
    heads = both // 2
    piece = pl.BlockSpec((block, both), lambda r, info: (r, 0))
    plain = pl.BlockSpec((block, heads), lambda r, info: (r, 0))
    return row_grid(
        spread_kernel,
        "spread",
        3,
        width // block,
        [piece, piece],
        (shaped(width, heads, dtype=F32),) * 3 + (shaped(heads, width, dtype=F32),),
        (plain,) * 3 + (pl.BlockSpec((heads, block), lambda r, info: (0, r)),),
        (info, mine, cross),
    )


def spread_feed_kernel(info, mine, near, cross, both, up, down):
    nbr, core = info[info.shape[0] - 1], info[1]
    here = pl.program_id(1) == nbr
    own = jnp.where(here, mine[...], near[...]).astype(F32)
    other = jnp.where(here, cross[...], both[...]).astype(F32)
    up[...] = jnp.where(core == 0, own, other)
    down[...] = jnp.where(core == 0, other, own)


def spread_feed(info, mine, near, cross, both):
    width = mine.shape[1]
    block = width // 2
    piece = pl.BlockSpec((block, width), lambda k, n, info: (k, 0))
    return pl.pallas_call(
        spread_feed_kernel,
        out_shape=(shaped(width, 2 * width, dtype=F32), shaped(2 * width, width, dtype=F32)),
        grid_spec=pltpu.PrefetchScalarGridSpec(
            num_scalar_prefetch=1,
            grid=(2, 2),
            in_specs=[piece] * 4,
            out_specs=(
                pl.BlockSpec((block, width), lambda k, n, info: (n, k)),
                pl.BlockSpec((block, width), lambda k, n, info: (2 * k + n, 0)),
            ),
        ),
        compiler_params=pltpu.CompilerParams(vmem_limit_bytes=VMEM_LIMIT),
        cost_estimate=cost(5),
        name="spread_feed",
    )(info, mine, near, cross, both)


def swap(value, axis):
    return lax.ppermute(value, axis, [(0, 1), (1, 0)])


def part(value, index, count):
    size = value.shape[0] // count
    return lax.dynamic_slice_in_dim(value, index * size, size, 0)


def half_of(value, index):
    if isinstance(value, tuple):
        return jnp.where(index == 0, *value)
    return part(value, index, 2)


def join(index, mine, other):
    return jnp.where(index == 0, jnp.concatenate([mine, other]), jnp.concatenate([other, mine]))


def tie(*values):
    return lax.optimization_barrier(values)


def add_low(*addends):
    return sum(addend.astype(F32) for addend in addends).astype(BF16)


def ladder(sizes):
    steps = [("nbr", lax.axis_index("nbr"), [(0, 1), (1, 0)])]
    bit = 1
    while bit < sizes["rest"]:
        index = (lax.axis_index("rest") // bit) % 2
        steps.append(("rest", index, [(i, i ^ bit) for i in range(sizes["rest"])]))
        bit *= 2
    return steps


def halve(step):
    axis, index, perm = step

    def start(value):
        sent, kept = [
            add_low(*[half_of(addend, which) for addend in value]) for which in (1 - index, index)
        ]
        return kept, lax.ppermute(sent, axis, perm)

    return start, lambda kept, got: (kept, got)


def double(step):
    axis, index, perm = step

    def start(value):
        if isinstance(value, tuple):
            value = add_low(*value)
        return value, lax.ppermute(value, axis, perm)

    return start, functools.partial(join, index)


def pair(axis):
    return lambda value: (value, swap(value, axis)), lambda *both: both


class Chain:
    def __init__(self, pending, finish, moves):
        self.pending, self.finish, self.moves = pending, finish, list(moves)

    def go(self):
        if self.finish is not None:
            value = self.finish(*self.pending)
            if self.moves:
                start, self.finish = self.moves.pop(0)
                self.pending = start(value)
            else:
                self.pending, self.finish = value, None


def meet(chains, *values):
    tree = [tuple(c.pending) for c in chains]
    tree, tied = lax.optimization_barrier((tree, list(values)))
    for c, pending in zip(chains, tree):
        c.pending = pending
    return tied[0] if len(tied) == 1 else tied


def on_device(
    sizes,
    tokens,
    lengths,
    out_grad,
    ln1_gain,
    ln1_shift,
    w_query,
    b_query,
    w_key,
    w_value,
    b_value,
    w_out,
    b_out,
    ln2_gain,
    ln2_shift,
    w_up,
    b_up,
    w_down,
    b_down,
):
    side = lax.axis_index("mp")
    core = lax.axis_index("core")
    nbr = lax.axis_index("nbr")
    rows_dev, half, width = tokens.shape
    rows = rows_dev // 2
    seq = 2 * half
    total = rows * seq
    heads = w_query.shape[1]
    units = w_up.shape[1] // 2
    steps = ladder(sizes)

    def by_core(first, second):
        return jnp.where(core == 0, first, second)

    def flat(value):
        return value.reshape(total, value.shape[-1])

    info = jnp.concatenate(
        [jnp.stack([side * half, core, side * rows]), part(lengths, side, 2), nbr[None]]
    ).astype(jnp.int32)

    quarter = 2 * nbr + core
    w_send = jnp.concatenate([part(w, quarter, 4) for w in (w_query, w_key, w_value)], axis=1)
    t_send = part(tokens, 1 - side, 2)
    got_tokens = swap(t_send, "mp")
    w_mine = swap(w_send, "mp")
    bias_own = jnp.concatenate([b_query, b_value, b_up])
    bias_oth = swap(bias_own, "mp")
    up_halves = [w_up[:, :units], w_up[:, units:]]
    down_halves = [w_down[:units], w_down[units:]]
    f_send0 = part(by_core(up_halves[0], down_halves[0]), nbr, 2)
    f_send1 = by_core(up_halves[1], down_halves[1])
    g_send = part(out_grad, 1 - side, 2)
    o_send = part(w_out, core, 2)
    got_tokens, f_send0, f_send1, g_send, o_send = tie(
        got_tokens, f_send0, f_send1, g_send, o_send
    )
    x, normed_in, nt, qkv_own = enter(
        info, tokens, got_tokens, w_query, w_key, w_value, bias_own[None], ln1_gain, ln1_shift
    )
    f_mine0 = swap(f_send0, "mp")
    o_mine = swap(o_send, "mp")
    qkv_own, w_mine, bias_oth = tie(qkv_own, w_mine, bias_oth)
    w_near = swap(w_mine, "nbr")
    mixed_own, lse_own = attend(info, qkv_own)
    mixed_own, w_near, g_send = tie(mixed_own, w_near, g_send)
    pieces = (w_mine, swap(w_mine, "core"), w_near, swap(w_near, "core"))
    got_grad = swap(g_send, "mp")
    qkv_oth, wqkv_oth = other_heads(info, normed_in, pieces, bias_oth[None])
    qkv_oth, f_mine0, f_send1, o_mine = tie(qkv_oth, f_mine0, f_send1, o_mine)
    f_half0 = join(nbr, f_mine0, swap(f_mine0, "nbr"))
    f_mine1 = swap(f_send1, "mp")
    mixed_oth, lse_oth = attend(info, qkv_oth)
    mixed_oth, f_half0, got_grad = tie(mixed_oth, f_half0, got_grad)
    f_cross0 = swap(f_half0, "core")
    residual, nm, nm_t, up, wout_oth = middle(
        info, x, mixed_own, mixed_oth, w_out, o_mine, swap(o_mine, "core"),
        b_out, ln2_gain, ln2_shift, out_grad, got_grad,
    )
    bup_own = bias_own[2 * heads :][None]
    bup_oth = bias_oth[2 * heads :][None]
    args = (info, flat(nm), nm_t, flat(up))
    y, gnm, f_keep0, f_give0, gbup0 = feed(*args, f_half0, f_cross0, bup_oth[:, :units])
    y, f_give0, f_mine1 = tie(y, f_give0[0], f_mine1)
    f_swap0, f_cross1 = swap(f_give0, "core"), swap(f_mine1, "core")
    y, f_oth0, f_cross1 = tie(y, add_low(f_keep0[0], f_swap0), f_cross1)
    f_got0 = swap(f_oth0, "mp")
    bup_rest = jnp.concatenate([bup_oth[:, units:], bup_own], axis=1)
    y, gnm, f_keep, f_give, gbup_rest = feed(
        *args, f_mine1, f_cross1, bup_rest, own=(w_up, w_down), sums=(y, gnm)
    )
    gbup1, gbup_own = gbup_rest[:, :units], gbup_rest[:, units:]
    gnm, f_give, f_got0 = tie(gnm, f_give, f_got0)
    f_swap = swap(f_give, "core")
    out_keep, out_send, grad_res, glow_t, gm_own, gm_oth, mid_sums = middle_back(
        info, gnm.reshape(rows, seq, width), residual, y.reshape(rows, seq, width), up,
        ln2_gain, b_down, w_out, wout_oth,
    )
    gm_oth, f_swap = tie(gm_oth, f_swap)
    f_got1 = swap(add_low(f_keep[0], f_swap[0]), "mp")
    halving = [halve(step) for step in steps]
    moves = halving + [double(step) for step in reversed(steps)] + [pair("core")]
    last = (lambda v: (v, swap(v, "nbr"), swap(v, "core")), lambda *three: three)
    feed_moves = moves[1:-2] + [last]
    keep_both = lambda *both: both
    f0 = Chain((f_keep[1], f_swap[1], f_got0), keep_both, halving[:1])
    f0.go()
    d_oth, bias_sum_oth = attend_back(info, qkv_oth, gm_oth, lse_oth)
    d_oth = meet([f0], d_oth)
    a_keep, a_give = weights(info, nt, flat(d_oth), glow_t, flat(mixed_oth))
    a_give, f_got1 = tie(a_give, f_got1)
    f1 = Chain((f_keep[2], f_swap[2], f_got1), keep_both, halving[:1])
    f1.go()
    gm_own, a_oth = tie(gm_own, add_low(a_keep, swap(a_give, "core")))
    a_got0 = swap(a_oth[: width // 2], "mp")
    d_own, bias_sum_own = attend_back(info, qkv_own, gm_own, lse_own)
    d_own, a_got0, a_last = meet([f1], d_own, a_got0, a_oth[width // 2 :])
    a_got1 = swap(a_last, "mp")
    both = tuple(zip(f0.pending, f1.pending))
    feed_sum = Chain(both, keep_both, feed_moves)
    feed_sum.go()
    a_keep, a_give = weights(info, nt, flat(d_own), glow_t, flat(mixed_own))
    a_give, a_keep, a_got1 = meet([feed_sum], a_give, a_keep, a_got1)
    d_own, a_swap = tie(d_own, swap(a_give, "core"))
    a_own = add_low(a_keep, a_swap)
    att = Chain((a_own, (a_got0, a_got1)), keep_both, moves)
    att.go()
    feed_sum.go()
    out_got = swap(out_send, "mp")
    dx_keep, dx_send, end_sums = leave(
        info, d_own, d_oth, w_query, w_key, w_value, wqkv_oth, x, grad_res, ln1_gain
    )
    dx_send, end_sums = meet([att, feed_sum], dx_send, end_sums)

    def bias_sums(d, gbup):
        sums = jnp.sum(d, axis=(0, 1))
        return [sums[:heads], sums[2 * heads :]] + [g[0] for g in gbup]

    shared = [end_sums[0], end_sums[1]] + [mid_sums[i] for i in range(4)]
    mine = jnp.concatenate(shared + bias_sums(bias_sum_own, [gbup_own]))
    sent = jnp.concatenate(shared + bias_sums(bias_sum_oth, [gbup0, gbup1]))
    along = steps[:1] + [("core", None, [(0, 1), (1, 0)])] + steps[1:][::-1]
    vec_moves = [(lambda v, s=s: (v, lax.ppermute(v, s[0], s[2])), jnp.add) for s in along]
    vec = Chain((mine, swap(sent, "mp")), jnp.add, vec_moves)
    att.go()
    feed_sum.go()
    stage = 1
    while att.moves:
        stage += 1
        live = [c for c in (att, vec) if c.finish is not None]
        if feed_sum.moves:
            live += [feed_sum]
        if stage == 2:
            out_got, dx_send = meet(live, out_got, dx_send)
            dx_got = swap(dx_send, "mp")
            block_out = join(side, out_keep, out_got)
        elif len(att.moves) == 2:
            dx_got = meet(live + [feed_sum], dx_got)
            input_grad = join(side, dx_keep, dx_got.astype(F32))
            f_pieces = feed_sum.pending + (swap(feed_sum.pending[1], "core"),)
        elif len(att.moves) == 1:
            up_sum, down_sum = spread_feed(info, *f_pieces)
            up_sum, down_sum, block_out, input_grad = meet(
                live, up_sum, down_sum, block_out, input_grad
            )
        else:
            meet(live)
        for c in live:
            c.go()
    while vec.finish is not None:
        vec.go()

    common = [vec.pending[i * width : (i + 1) * width] for i in range(6)]
    split = vec.pending[6 * width :]
    q_sum, k_sum, v_sum, o_sum = spread(info, *att.pending)
    return (
        block_out,
        input_grad,
        common[0],
        common[1],
        q_sum,
        split[:heads],
        k_sum,
        v_sum,
        split[heads : 2 * heads],
        o_sum,
        common[4],
        common[2],
        common[3],
        up_sum,
        split[2 * heads :],
        down_sum,
        common[5],
    )


def solution(mesh):
    n_dp, n_mp = mesh.shape["dp"], mesh.shape["mp"]
    names = ("rest", "nbr", "core", "mp")
    inner = Mesh(mesh.devices.reshape(n_dp // 4, 2, 2, n_mp), names)
    dp = ("rest", "nbr", "core")
    in_specs = (
        P(dp, "mp", None),
        P(dp),
        P(dp, "mp", None),
        P(),
        P(),
        P(None, "mp"),
        P("mp"),
        P(None, "mp"),
        P(None, "mp"),
        P("mp"),
        P("mp", None),
        P(),
        P(),
        P(),
        P(None, "mp"),
        P("mp"),
        P("mp", None),
        P(),
    )
    out_specs = (
        P(dp, "mp", None),
        P(dp, "mp", None),
        P(),
        P(),
        P(None, "mp"),
        P("mp"),
        P(None, "mp"),
        P(None, "mp"),
        P("mp"),
        P("mp", None),
        P(),
        P(),
        P(),
        P(None, "mp"),
        P("mp"),
        P("mp", None),
        P(),
    )
    return jax.shard_map(
        functools.partial(on_device, dict(inner.shape)),
        mesh=inner,
        in_specs=in_specs,
        out_specs=out_specs,
        check_vma=False,
    )
```

```python
import functools
import math

import jax
import jax.numpy as jnp
from jax import lax
from jax.experimental import pallas as pl
from jax.experimental.pallas import tpu as pltpu
from jax.sharding import Mesh
from jax.sharding import PartitionSpec as P

HEAD_DIM = 64
PAIR = 2 * HEAD_DIM
EPS = 1e-12
FILL = -1000000000.0
SCALE = 1.0 / math.sqrt(HEAD_DIM)
LOG2E = math.log2(math.e)
F32 = jnp.float32
BF16 = jnp.bfloat16
NT = (((1,), (1,)), ((), ()))
NN = (((1,), (0,)), ((), ()))
TN = (((0,), (0,)), ((), ()))


def mm(a, b, dims=NN):
    return lax.dot_general(a, b, dims, preferred_element_type=F32)


def key_mask(info, row, shape):
    seq = shape[0]
    slot = lax.broadcasted_iota(jnp.int32, shape, 0) + info[0]
    position = jnp.where(slot >= seq, slot - seq, slot)
    return position < info[3 + row]


def head_lanes(value, head):
    lane = lax.broadcasted_iota(jnp.int32, value.shape, 1)
    keep = lane < HEAD_DIM if head == 0 else lane >= HEAD_DIM
    return jnp.where(keep, value, jnp.zeros_like(value))


def attend_kernel(info, q_ref, k_ref, v_ref, o_ref, lse_ref):
    row = pl.program_id(0)
    q, k, v = q_ref[0], k_ref[0], v_ref[0]
    valid = key_mask(info, row, (k.shape[0], q.shape[0]))
    v_t = v.T
    seq = k.shape[0]
    both = mm(jnp.concatenate([head_lanes(k, 0), head_lanes(k, 1)], axis=0), q, NT)
    parts = []
    for head in range(2):
        scores = both[head * seq : (head + 1) * seq] * (SCALE * LOG2E)
        scores = jnp.where(valid, scores, FILL * LOG2E)
        top = jnp.max(scores, axis=0, keepdims=True)
        weight = jnp.exp2(scores - top)
        total = jnp.sum(weight, axis=0, keepdims=True)
        lse_ref[0, 0, head : head + 1, :] = top + jnp.log2(total)
        probs = (weight * (1.0 / total)).astype(BF16)
        parts.append(mm(v_t[head * HEAD_DIM : (head + 1) * HEAD_DIM], probs))
    o_ref[0] = jnp.concatenate(parts, axis=0).T.astype(BF16)


def attend_back_kernel(info, q_ref, k_ref, v_ref, do_ref, lse_ref, d_ref, sum_ref):
    row = pl.program_id(0)
    pair = pl.program_id(1)
    n_pairs = pl.num_programs(1)
    q, k, v, do = q_ref[0], k_ref[0], v_ref[0], do_ref[0]
    valid = key_mask(info, row, (k.shape[0], q.shape[0]))
    k_t = k.T
    dq_t, dk, dv = [], [], []
    for head in range(2):
        scores = mm(head_lanes(k, head), q, NT) * (SCALE * LOG2E)
        scores = jnp.where(valid, scores, FILL * LOG2E)
        probs = jnp.exp2(scores - lse_ref[0, 0, head : head + 1, :])
        dv.append(mm(probs.astype(BF16), do))
        dprobs = mm(head_lanes(v, head), do, NT)
        delta = jnp.sum(probs * dprobs, axis=0, keepdims=True)
        dscores = (probs * (dprobs - delta)).astype(BF16)
        dk.append(mm(dscores, q))
        dq_t.append(mm(k_t[head * HEAD_DIM : (head + 1) * HEAD_DIM], dscores))
    first = lax.broadcasted_iota(jnp.int32, dv[0].shape, 1) < HEAD_DIM
    dq = jnp.concatenate(dq_t, axis=0).T * SCALE

    def put(slot, value):
        start = pl.multiple_of((slot * n_pairs + pair) * PAIR, PAIR)
        low = value.astype(BF16)
        d_ref[0, :, pl.ds(start, PAIR)] = low
        sum_ref[0, :, pl.ds(start, PAIR)] = jnp.sum(low.astype(F32), axis=0, keepdims=True)

    put(0, dq)
    put(1, jnp.where(first, dk[0], dk[1]) * SCALE)
    put(2, jnp.where(first, dv[0], dv[1]))


def attend_specs(seq, n_pairs):
    return [
        pl.BlockSpec((1, seq, PAIR), lambda r, p, info: (r, 0, p)),
        pl.BlockSpec((1, seq, PAIR), lambda r, p, info: (r, 0, n_pairs + p)),
        pl.BlockSpec((1, seq, PAIR), lambda r, p, info: (r, 0, 2 * n_pairs + p)),
    ]


VMEM_LIMIT = 50 * 1024 * 1024


def cost(micros):
    return pl.CostEstimate(flops=int(micros * 1.15e9), bytes_accessed=1000, transcendentals=0)


def attend(info, qkv):
    rows, seq, width = qkv.shape
    n_pairs = width // (3 * PAIR)
    return pl.pallas_call(
        attend_kernel,
        out_shape=(
            jax.ShapeDtypeStruct((rows, seq, n_pairs * PAIR), BF16),
            jax.ShapeDtypeStruct((rows, n_pairs, 2, seq), F32),
        ),
        grid_spec=pltpu.PrefetchScalarGridSpec(
            num_scalar_prefetch=1,
            grid=(rows, n_pairs),
            in_specs=attend_specs(seq, n_pairs),
            out_specs=(
                pl.BlockSpec((1, seq, PAIR), lambda r, p, info: (r, 0, p)),
                pl.BlockSpec((1, 1, 2, seq), lambda r, p, info: (r, p, 0, 0)),
            ),
        ),
        compiler_params=pltpu.CompilerParams(vmem_limit_bytes=VMEM_LIMIT),
        cost_estimate=cost(10),
        name="attend",
    )(info, qkv, qkv, qkv)


def attend_back(info, qkv, grad_mixed, lse):
    rows, seq, width = qkv.shape
    n_pairs = width // (3 * PAIR)
    return pl.pallas_call(
        attend_back_kernel,
        out_shape=(
            jax.ShapeDtypeStruct((rows, seq, width), BF16),
            jax.ShapeDtypeStruct((rows, 1, width), F32),
        ),
        grid_spec=pltpu.PrefetchScalarGridSpec(
            num_scalar_prefetch=1,
            grid=(rows, n_pairs),
            in_specs=attend_specs(seq, n_pairs)
            + [
                pl.BlockSpec((1, seq, PAIR), lambda r, p, info: (r, 0, p)),
                pl.BlockSpec((1, 1, 2, seq), lambda r, p, info: (r, p, 0, 0)),
            ],
            out_specs=(
                pl.BlockSpec((1, seq, width), lambda r, p, info: (r, 0, 0)),
                pl.BlockSpec((1, 1, width), lambda r, p, info: (r, 0, 0)),
            ),
        ),
        compiler_params=pltpu.CompilerParams(vmem_limit_bytes=VMEM_LIMIT),
        cost_estimate=cost(13),
        name="attend_back",
    )(info, qkv, qkv, qkv, grad_mixed, lse)


def feed_kernel(first, own, info, *refs):
    refs = list(refs)
    nm, wa, wb, bu = refs[:4]
    refs = refs[4:]
    if own:
        wu, wd = refs[:2]
        refs = refs[2:]
    nt_hbm, up_hbm = refs[:2]
    refs = refs[2:]
    if not first:
        y_hbm, gnm_hbm = refs[:2]
        refs = refs[2:]
    y_out, gnm_out, keep, send, gbu, nt, up, y, gnm, hidden, sems = refs
    step = pl.program_id(0)
    last = pl.num_programs(0) - 1
    core = info[1]
    copy_up = pltpu.make_async_copy(up_hbm, up, sems.at[0])
    copies = [pltpu.make_async_copy(nt_hbm, nt, sems.at[1])]
    if not first:
        copies += [
            pltpu.make_async_copy(y_hbm, y, sems.at[2]),
            pltpu.make_async_copy(gnm_hbm, gnm, sems.at[3]),
        ]
    out_y = pltpu.make_async_copy(y, y_out, sems.at[4])
    out_gnm = pltpu.make_async_copy(gnm, gnm_out, sems.at[5])

    @pl.when(step == 0)
    def _():
        copy_up.start()
        for copy in copies:
            copy.start()

    def pick():
        w_up = jnp.where(core == 0, wa[...], wb[...])
        w_down = jnp.where(core == 0, wb[...], wa[...])
        if own:
            w_up = jnp.where(step == 0, w_up, wu[...])
            w_down = jnp.where(step == 0, w_down, wd[...])
        return w_up, w_down

    w_up, w_down = pick()
    hidden[...] = mm(nm[...], w_up) + bu[...]

    @pl.when(step == 0)
    def _():
        copy_up.wait()

    h = hidden[...]
    cdf = 0.5 * (1.0 + lax.erf(h * (1.0 / math.sqrt(2.0))))
    active = (h * cdf).astype(BF16)
    slope = cdf + h * jnp.exp(-0.5 * h * h) * (1.0 / math.sqrt(2.0 * math.pi))
    grad_hidden = (mm(up[...], w_down, NT) * slope).astype(BF16)
    gbu[...] = jnp.sum(grad_hidden.astype(F32), axis=0, keepdims=True)
    grad_down = mm(active, up[...], TN).astype(BF16)

    @pl.when(step == 0)
    def _():
        for copy in copies:
            copy.wait()

    if first:
        y[...] = mm(active, w_down)
        gnm[...] = mm(grad_hidden, w_up, NT)
    else:
        y[...] += mm(active, w_down)
        gnm[...] += mm(grad_hidden, w_up, NT)

    @pl.when(step == last)
    def _():
        out_y.start()
        out_gnm.start()

    grad_up = mm(nt[...], grad_hidden).astype(BF16)
    keep[0] = jnp.where(core == 0, grad_up, grad_down)
    send[0] = jnp.where(core == 0, grad_down, grad_up)

    @pl.when(step == last)
    def _():
        out_y.wait()
        out_gnm.wait()


def feed(info, nm, nt, up, wa, wb, bu, own=None, sums=None):
    tokens, width = nm.shape
    count = bu.shape[1] // width
    first = sums is None
    once = lambda shape: pl.BlockSpec(shape, lambda f, info: (0, 0), pipeline_mode=pl.Buffered(1))
    place = pl.BlockSpec(memory_space=pl.ANY)
    row = pl.BlockSpec((1, width), lambda f, info: (0, f))
    in_specs = [once((tokens, width)), once(wa.shape), once(wb.shape), row]
    args = [nm, wa, wb, bu]
    if own is not None:
        in_specs += [
            pl.BlockSpec((width, width), lambda f, info: (0, jnp.maximum(f - 1, 0))),
            pl.BlockSpec((width, width), lambda f, info: (jnp.maximum(f - 1, 0), 0)),
        ]
        args += list(own)
    in_specs += [place] * 2
    args += [nt, up]
    if not first:
        in_specs += [place] * 2
        args += list(sums)
    grads = pl.BlockSpec((1, width, width), lambda f, info: (f, 0, 0))
    return pl.pallas_call(
        functools.partial(feed_kernel, first, own is not None),
        out_shape=(
            shaped(tokens, width, dtype=F32),
            shaped(tokens, width, dtype=F32),
            shaped(count, width, width),
            shaped(count, width, width),
            shaped(1, count * width, dtype=F32),
        ),
        grid_spec=pltpu.PrefetchScalarGridSpec(
            num_scalar_prefetch=1,
            grid=(count,),
            in_specs=in_specs,
            out_specs=(place, place, grads, grads, row),
            scratch_shapes=[
                pltpu.VMEM((width, tokens), BF16),
                pltpu.VMEM((tokens, width), BF16),
                pltpu.VMEM((tokens, width), F32),
                pltpu.VMEM((tokens, width), F32),
                pltpu.VMEM((tokens, width), F32),
                pltpu.SemaphoreType.DMA((6,)),
            ],
        ),
        compiler_params=pltpu.CompilerParams(vmem_limit_bytes=VMEM_LIMIT),
        cost_estimate=cost(12 * count),
        name="feed_own" if own is not None else "feed_other",
    )(info, *args)


def norm(values):
    average = jnp.mean(values, axis=-1, keepdims=True)
    centred = values - average
    inv = lax.rsqrt(jnp.mean(centred * centred, axis=-1, keepdims=True) + EPS)
    return centred * inv, inv


def norm_back(grad, unit, inv, gain):
    scaled = grad * gain
    return inv * (
        scaled
        - jnp.mean(scaled, axis=-1, keepdims=True)
        - unit * jnp.mean(scaled * unit, axis=-1, keepdims=True)
    )


def stack(first, second):
    return jnp.concatenate([first, second], axis=0)


def row_grid(kernel, name, micros, rows, in_specs, out_shape, out_specs, args):
    return pl.pallas_call(
        kernel,
        out_shape=out_shape,
        grid_spec=pltpu.PrefetchScalarGridSpec(
            num_scalar_prefetch=1, grid=(rows,), in_specs=in_specs, out_specs=out_specs
        ),
        compiler_params=pltpu.CompilerParams(vmem_limit_bytes=VMEM_LIMIT),
        cost_estimate=cost(micros),
        name=name,
    )(*args)


def fixed(shape):
    return pl.BlockSpec(shape, lambda r, info: (0,) * len(shape))


def const(shape):
    return pl.BlockSpec(
        shape, lambda r, info: (0,) * len(shape), pipeline_mode=pl.Buffered(1)
    )


def per_row(*shape):
    return pl.BlockSpec((1,) + shape, lambda r, info: (r,) + (0,) * len(shape))


def kept_row(*shape):
    return pl.BlockSpec((1,) + shape, lambda r, info: (info[2] + r,) + (0,) * len(shape))


def shaped(*shape, dtype=BF16):
    return jax.ShapeDtypeStruct(shape, dtype)


def enter_kernel(info, tok, got, wq, wk, wv, bias, gain, shift, x_out, n_out, nt_out, qkv):
    heads = wq.shape[1]
    x = stack(tok[0], got[0])
    x_out[0] = x
    unit, _ = norm(x.astype(F32))
    normed = (unit * gain[...] + shift[...]).astype(BF16)
    n_out[0] = normed
    nt_out[...] = normed.T
    qkv[0, :, :heads] = (mm(normed, wq[...]) + bias[:, :heads]).astype(BF16)
    qkv[0, :, heads : 2 * heads] = mm(normed, wk[...]).astype(BF16)
    qkv[0, :, 2 * heads :] = (mm(normed, wv[...]) + bias[:, heads : 2 * heads]).astype(BF16)


def enter(info, tokens, got, wq, wk, wv, bias, gain, shift):
    rows, half, width = got.shape
    seq, heads = 2 * half, wq.shape[1]
    return row_grid(
        enter_kernel,
        "enter",
        0,
        rows,
        [kept_row(half, width), per_row(half, width)]
        + [const(wq.shape)] * 3
        + [const(bias.shape)]
        + [const((1, width))] * 2,
        (
            shaped(rows, seq, width),
            shaped(rows, seq, width),
            shaped(width, rows * seq),
            shaped(rows, seq, 3 * heads),
        ),
        (
            per_row(seq, width),
            per_row(seq, width),
            pl.BlockSpec((width, seq), lambda r, info: (0, r)),
            per_row(seq, 3 * heads),
        ),
        (info, tokens, got, wq, wk, wv, bias, gain[None], shift[None]),
    )


def other_heads_kernel(info, n, p0, p1, p2, p3, bias, qkv, w):
    heads = w.shape[1] // 3

    @pl.when(pl.program_id(0) == 0)
    def _():
        nbr, core = info[3 + pl.num_programs(0)], info[1]
        size = p0.shape[0]
        for index, piece in enumerate((p0, p1, p2, p3)):
            row = 1 - nbr if index >= 2 else nbr
            col = 1 - core if index % 2 else core
            start = pl.multiple_of((2 * row + col) * size, size)
            w[pl.ds(start, size), :] = piece[...]

    full = jnp.concatenate(
        [bias[:, :heads], jnp.zeros((1, heads), F32), bias[:, heads : 2 * heads]], axis=1
    )
    qkv[0] = (mm(n[0], w[...]) + full).astype(BF16)


def other_heads(info, n, pieces, bias):
    rows, seq, width = n.shape
    size, wide = pieces[0].shape
    return row_grid(
        other_heads_kernel,
        "other_heads",
        0,
        rows,
        [per_row(seq, width)] + [const((size, wide))] * 4 + [const(bias.shape)],
        (shaped(rows, seq, wide), shaped(width, wide)),
        (per_row(seq, wide), fixed((width, wide))),
        (info, n, *pieces, bias),
    )


def middle_kernel(
    info, x, m_own, m_oth, w_own, w_mine, w_cross, b_out, gain, shift, grad, got, res, nm, nm_t, up, w_oth
):
    @pl.when(pl.program_id(0) == 0)
    def _():
        size = w_mine.shape[0]
        w_oth[pl.ds(pl.multiple_of(info[1] * size, size), size), :] = w_mine[...]
        w_oth[pl.ds(pl.multiple_of((1 - info[1]) * size, size), size), :] = w_cross[...]

    attended = mm(m_own[0], w_own[...]) + mm(m_oth[0], w_oth[...])
    residual = x[0].astype(F32) + attended + b_out[...]
    res[0] = residual
    unit, _ = norm(residual)
    normed = (unit * gain[...] + shift[...]).astype(BF16)
    nm[0] = normed
    nm_t[...] = normed.T
    up[0] = stack(grad[0], got[0])


def middle(info, x, m_own, m_oth, w_own, w_mine, w_cross, b_out, gain, shift, grad, got):
    rows, seq, width = x.shape
    heads = w_own.shape[0]
    return row_grid(
        middle_kernel,
        "middle",
        0,
        rows,
        [per_row(seq, width), per_row(seq, heads), per_row(seq, heads)]
        + [const(w_own.shape), const(w_mine.shape), const(w_mine.shape)]
        + [const((1, width))] * 3
        + [kept_row(seq // 2, width), per_row(seq // 2, width)],
        (
            shaped(rows, seq, width, dtype=F32),
            shaped(rows, seq, width),
            shaped(width, rows * seq),
            shaped(rows, seq, width),
            shaped(heads, width),
        ),
        (
            per_row(seq, width),
            per_row(seq, width),
            pl.BlockSpec((width, seq), lambda r, info: (0, r)),
            per_row(seq, width),
            fixed((heads, width)),
        ),
        (info, x, m_own, m_oth, w_own, w_mine, w_cross, b_out[None], gain[None], shift[None], grad, got),
    )


def middle_back_kernel(
    info, gnm, res, y, up, gain, b_down, w_own, w_oth, keep, send, gres, glow_t, gm_own, gm_oth, sums
):
    half = keep.shape[1]
    residual, grad, upstream = res[0], gnm[0], up[0].astype(F32)
    out = (residual + y[0] + b_down[...]).astype(BF16)
    keep[0] = out[:half]
    send[0] = out[half:]
    unit, inv = norm(residual)
    total = upstream + norm_back(grad, unit, inv, gain[...])
    gres[0] = total
    low = total.astype(BF16)
    glow_t[...] = low.T
    gm_own[0] = mm(low, w_own[...], NT).astype(BF16)
    gm_oth[0] = mm(low, w_oth[...], NT).astype(BF16)

    @pl.when(pl.program_id(0) == 0)
    def _():
        sums[...] = jnp.zeros_like(sums)

    for index, value in enumerate((grad * unit, grad, total, upstream)):
        sums[index : index + 1, :] += jnp.sum(value, axis=0, keepdims=True)


def middle_back(info, gnm, res, y, up, gain, b_down, w_own, w_oth):
    rows, seq, width = res.shape
    heads = w_own.shape[0]
    row = per_row(seq, width)
    half = per_row(seq // 2, width)
    return row_grid(
        middle_back_kernel,
        "middle_back",
        0,
        rows,
        [row] * 4 + [const((1, width))] * 2 + [const((heads, width))] * 2,
        (
            shaped(rows, seq // 2, width),
            shaped(rows, seq // 2, width),
            shaped(rows, seq, width, dtype=F32),
            shaped(width, rows * seq),
            shaped(rows, seq, heads),
            shaped(rows, seq, heads),
            shaped(8, width, dtype=F32),
        ),
        (
            half,
            half,
            row,
            pl.BlockSpec((width, seq), lambda r, info: (0, r)),
            per_row(seq, heads),
            per_row(seq, heads),
            fixed((8, width)),
        ),
        (info, gnm, res, y, up, gain[None], b_down[None], w_own, w_oth),
    )


def weights_kernel(info, nt, d, glow_t, mixed, keep, send):
    heads = mixed.shape[1]
    g = mm(nt[...], d[...]).astype(BF16)
    o = mm(glow_t[...], mixed[...]).astype(BF16)
    cut = 2 * heads

    @pl.when(info[1] == 0)
    def _():
        keep[...] = g[:, :cut]
        send[:, :heads] = g[:, cut:]
        send[:, heads:] = o

    @pl.when(info[1] != 0)
    def _():
        send[...] = g[:, :cut]
        keep[:, :heads] = g[:, cut:]
        keep[:, heads:] = o


def weights(info, nt, d, glow_t, mixed, block=256):
    width, tokens = nt.shape
    heads = mixed.shape[1]
    part = pl.BlockSpec((block, tokens), lambda r, info: (r, 0))
    result = pl.BlockSpec((block, 2 * heads), lambda r, info: (r, 0))
    return row_grid(
        weights_kernel,
        "weights",
        0,
        width // block,
        [part, const(d.shape), part, const(mixed.shape)],
        (shaped(width, 2 * heads), shaped(width, 2 * heads)),
        (result, result),
        (info, nt, d, glow_t, mixed),
    )


def leave_kernel(info, d_own, d_oth, wq, wk, wv, w_oth, x, gres, gain, keep, send, sums):
    heads = wq.shape[1]
    half = keep.shape[1]
    grad = (
        mm(d_own[0, :, :heads], wq[...], NT)
        + mm(d_own[0, :, heads : 2 * heads], wk[...], NT)
        + mm(d_own[0, :, 2 * heads :], wv[...], NT)
        + mm(d_oth[0], w_oth[...], NT)
    )
    unit, inv = norm(x[0].astype(F32))
    total = gres[0] + norm_back(grad, unit, inv, gain[...])
    keep[0] = total[:half]
    send[0] = total[half:].astype(BF16)

    @pl.when(pl.program_id(0) == 0)
    def _():
        sums[...] = jnp.zeros_like(sums)

    for index, value in enumerate((grad * unit, grad)):
        sums[index : index + 1, :] += jnp.sum(value, axis=0, keepdims=True)


def leave(info, d_own, d_oth, wq, wk, wv, w_oth, x, gres, gain):
    rows, seq, width = x.shape
    row = per_row(seq, width)
    half = per_row(seq // 2, width)
    wide = per_row(seq, d_own.shape[2])
    return row_grid(
        leave_kernel,
        "leave",
        10,
        rows,
        [wide, wide]
        + [const(wq.shape)] * 3
        + [const(w_oth.shape), row, row, const((1, width))],
        (
            shaped(rows, seq // 2, width, dtype=F32),
            shaped(rows, seq // 2, width),
            shaped(8, width, dtype=F32),
        ),
        (half, half, fixed((8, width))),
        (info, d_own, d_oth, wq, wk, wv, w_oth, x, gres, gain[None]),
    )


def spread_kernel(info, mine, cross, q, k, v, o):
    heads = q.shape[1]

    def write(first, second):
        q[...] = first[:, :heads].astype(F32)
        k[...] = first[:, heads:].astype(F32)
        v[...] = second[:, :heads].astype(F32)
        o[...] = second[:, heads:].astype(F32).T

    @pl.when(info[1] == 0)
    def _():
        write(mine, cross)

    @pl.when(info[1] != 0)
    def _():
        write(cross, mine)


def spread(info, mine, cross, block=256):
    width, both = mine.shape
    heads = both // 2
    piece = pl.BlockSpec((block, both), lambda r, info: (r, 0))
    plain = pl.BlockSpec((block, heads), lambda r, info: (r, 0))
    return row_grid(
        spread_kernel,
        "spread",
        3,
        width // block,
        [piece, piece],
        (shaped(width, heads, dtype=F32),) * 3 + (shaped(heads, width, dtype=F32),),
        (plain,) * 3 + (pl.BlockSpec((heads, block), lambda r, info: (0, r)),),
        (info, mine, cross),
    )


def spread_feed_kernel(info, *refs):
    nbr, core = info[info.shape[0] - 1], info[1]
    up, down = refs[-2:]
    here = pl.program_id(1) == nbr
    for chunk in range(2):
        mine, near, cross, both = refs[4 * chunk : 4 * chunk + 4]

        @pl.when(pl.program_id(0) == chunk)
        def _():
            own = jnp.where(here, mine[...], near[...]).astype(F32)
            other = jnp.where(here, cross[...], both[...]).astype(F32)
            up[...] = jnp.where(core == 0, own, other)
            down[...] = jnp.where(core == 0, other, own)


def spread_feed(info, pieces):
    block, width = pieces[0].shape
    once = pl.BlockSpec((block, width), lambda k, n, info: (0, 0), pipeline_mode=pl.Buffered(1))
    return pl.pallas_call(
        spread_feed_kernel,
        out_shape=(shaped(width, 2 * width, dtype=F32), shaped(2 * width, width, dtype=F32)),
        grid_spec=pltpu.PrefetchScalarGridSpec(
            num_scalar_prefetch=1,
            grid=(2, 2),
            in_specs=[once] * 8,
            out_specs=(
                pl.BlockSpec((block, width), lambda k, n, info: (n, k)),
                pl.BlockSpec((block, width), lambda k, n, info: (2 * k + n, 0)),
            ),
        ),
        compiler_params=pltpu.CompilerParams(vmem_limit_bytes=VMEM_LIMIT),
        cost_estimate=cost(5),
        name="spread_feed",
    )(info, *pieces)


def swap(value, axis):
    return lax.ppermute(value, axis, [(0, 1), (1, 0)])


def part(value, index, count):
    size = value.shape[0] // count
    return lax.dynamic_slice_in_dim(value, index * size, size, 0)


class Rows:
    def __init__(self, array, matrix=None, start=0, size=None):
        self.array, self.matrix, self.start = array, matrix, start
        self.size = array.shape[-2] if size is None else size

    def half(self, index):
        size = self.size // 2
        return Rows(self.array, self.matrix, self.start + index * size, size)

    def read(self):
        if self.matrix is None:
            return lax.dynamic_slice_in_dim(self.array, self.start, self.size, 0)
        shape = (1, self.size, self.array.shape[-1])
        return lax.dynamic_slice(self.array, (self.matrix, self.start, 0), shape)[0]


class Stacked:
    def __init__(self, upper, lower):
        self.upper, self.lower = upper, lower

    def half(self, index):
        return Rows(jnp.where(index == 0, self.upper, self.lower))


def total_low(addends):
    return add_low(*[addend.read() for addend in addends])


def join(index, mine, other):
    return jnp.where(index == 0, jnp.concatenate([mine, other]), jnp.concatenate([other, mine]))


def tie(*values):
    return lax.optimization_barrier(values)


def add_low(*addends):
    return sum(addend.astype(F32) for addend in addends).astype(BF16)


def ladder(sizes):
    steps = [("nbr", lax.axis_index("nbr"), [(0, 1), (1, 0)])]
    bit = 1
    while bit < sizes["rest"]:
        index = (lax.axis_index("rest") // bit) % 2
        steps.append(("rest", index, [(i, i ^ bit) for i in range(sizes["rest"])]))
        bit *= 2
    return steps


def halve(step):
    axis, index, perm = step

    def prepare(addends):
        sent = total_low([a.half(1 - index) for a in addends])
        return sent, tuple(a.half(index) for a in addends)

    return (
        prepare,
        lambda sent: (lax.ppermute(sent, axis, perm),),
        lambda kept, got: kept + (Rows(got),),
    )


def double(step):
    axis, index, perm = step

    def prepare(value):
        if isinstance(value, tuple):
            value = total_low(value)
        return value, value

    return prepare, lambda sent: (lax.ppermute(sent, axis, perm),), functools.partial(join, index)


def twice(value):
    return value, value


def to_pair(axis):
    return twice, lambda sent: (swap(sent, axis),), lambda value, got: (value, got)


def to_three():
    return (
        twice,
        lambda sent: (swap(sent, "nbr"), swap(sent, "core")),
        lambda value, near, cross: (value, near, cross),
    )


def add_over(axis, perm):
    return twice, lambda sent: (lax.ppermute(sent, axis, perm),), jnp.add


class Chain:
    def __init__(self, value, moves, behind=()):
        self.value, self.finish, self.moves, self.flying = value, None, list(moves), ()
        self.go(behind)

    def go(self, behind=(), values=()):
        if self.finish is not None:
            self.value, self.finish = self.finish(self.value, *self.flying), None
            self.flying = ()
        if self.moves:
            prepare, launch, self.finish = self.moves.pop(0)
            sent, self.value = prepare(self.value)
            if behind or values:
                sent, values = meet(behind, sent, list(values))
            self.flying = launch(sent)
        return values

    @property
    def done(self):
        return self.finish is None


def meet(chains, *values):
    flying, tied = lax.optimization_barrier(([c.flying for c in chains], list(values)))
    for c, transfers in zip(chains, flying):
        c.flying = tuple(transfers)
    return tied[0] if len(tied) == 1 else tied


def on_device(
    sizes,
    tokens,
    lengths,
    out_grad,
    ln1_gain,
    ln1_shift,
    w_query,
    b_query,
    w_key,
    w_value,
    b_value,
    w_out,
    b_out,
    ln2_gain,
    ln2_shift,
    w_up,
    b_up,
    w_down,
    b_down,
):
    side = lax.axis_index("mp")
    core = lax.axis_index("core")
    nbr = lax.axis_index("nbr")
    rows_dev, half, width = tokens.shape
    rows = rows_dev // 2
    seq = 2 * half
    total = rows * seq
    heads = w_query.shape[1]
    units = w_up.shape[1] // 2
    steps = ladder(sizes)

    def by_core(first, second):
        return jnp.where(core == 0, first, second)

    def flat(value):
        return value.reshape(total, value.shape[-1])

    info = jnp.concatenate(
        [jnp.stack([side * half, core, side * rows]), part(lengths, side, 2), nbr[None]]
    ).astype(jnp.int32)

    quarter = 2 * nbr + core
    w_send = jnp.concatenate([part(w, quarter, 4) for w in (w_query, w_key, w_value)], axis=1)
    t_send = part(tokens, 1 - side, 2)
    got_tokens = swap(t_send, "mp")
    w_mine = swap(w_send, "mp")
    bias_own = jnp.concatenate([b_query, b_value, b_up])
    bias_oth = swap(bias_own, "mp")
    up_halves = [w_up[:, :units], w_up[:, units:]]
    down_halves = [w_down[:units], w_down[units:]]
    f_send0 = part(by_core(up_halves[0], down_halves[0]), nbr, 2)
    f_send1 = by_core(up_halves[1], down_halves[1])
    g_send = part(out_grad, 1 - side, 2)
    o_send = part(w_out, core, 2)
    got_tokens, f_send0, f_send1, g_send, o_send = tie(
        got_tokens, f_send0, f_send1, g_send, o_send
    )
    x, normed_in, nt, qkv_own = enter(
        info, tokens, got_tokens, w_query, w_key, w_value, bias_own[None], ln1_gain, ln1_shift
    )
    f_mine0 = swap(f_send0, "mp")
    o_mine = swap(o_send, "mp")
    qkv_own, w_mine, bias_oth = tie(qkv_own, w_mine, bias_oth)
    w_near = swap(w_mine, "nbr")
    mixed_own, lse_own = attend(info, qkv_own)
    mixed_own, w_near, g_send = tie(mixed_own, w_near, g_send)
    pieces = (w_mine, swap(w_mine, "core"), w_near, swap(w_near, "core"))
    got_grad = swap(g_send, "mp")
    qkv_oth, wqkv_oth = other_heads(info, normed_in, pieces, bias_oth[None])
    qkv_oth, f_mine0, f_send1, o_mine = tie(qkv_oth, f_mine0, f_send1, o_mine)
    f_half0 = join(nbr, f_mine0, swap(f_mine0, "nbr"))
    f_mine1 = swap(f_send1, "mp")
    mixed_oth, lse_oth = attend(info, qkv_oth)
    mixed_oth, f_half0, got_grad = tie(mixed_oth, f_half0, got_grad)
    f_cross0 = swap(f_half0, "core")
    residual, nm, nm_t, up, wout_oth = middle(
        info, x, mixed_own, mixed_oth, w_out, o_mine, swap(o_mine, "core"),
        b_out, ln2_gain, ln2_shift, out_grad, got_grad,
    )
    bup_own = bias_own[2 * heads :][None]
    bup_oth = bias_oth[2 * heads :][None]
    args = (info, flat(nm), nm_t, flat(up))
    y, gnm, f_keep0, f_give0, gbup0 = feed(*args, f_half0, f_cross0, bup_oth[:, :units])
    y, f_give0, f_mine1 = tie(y, f_give0[0], f_mine1)
    f_swap0, f_cross1 = swap(f_give0, "core"), swap(f_mine1, "core")
    y, f_oth0, f_cross1 = tie(y, add_low(f_keep0[0], f_swap0), f_cross1)
    f_got0 = swap(f_oth0, "mp")
    bup_rest = jnp.concatenate([bup_oth[:, units:], bup_own], axis=1)
    y, gnm, f_keep, f_give, gbup_rest = feed(
        *args, f_mine1, f_cross1, bup_rest, own=(w_up, w_down), sums=(y, gnm)
    )
    gbup1, gbup_own = gbup_rest[:, :units], gbup_rest[:, units:]
    gnm, f_give, f_got0 = tie(gnm, f_give, f_got0)
    f_swap = swap(f_give, "core")
    out_keep, out_send, grad_res, glow_t, gm_own, gm_oth, mid_sums = middle_back(
        info, gnm.reshape(rows, seq, width), residual, y.reshape(rows, seq, width), up,
        ln2_gain, b_down, w_out, wout_oth,
    )
    gm_oth, f_swap = tie(gm_oth, f_swap)
    f_got1 = swap(add_low(f_keep[0], f_swap[0]), "mp")
    halving = [halve(step) for step in steps]
    doubling = [double(step) for step in reversed(steps)]
    feed_moves = halving + doubling[:-1] + [to_three()]
    att_moves = halving + doubling + [to_pair("core")]
    f0 = Chain((Rows(f_keep, 1), Rows(f_swap, 1), Rows(f_got0)), feed_moves)
    d_oth, bias_sum_oth = attend_back(info, qkv_oth, gm_oth, lse_oth)
    d_oth = meet([f0], d_oth)
    f0.go()
    a_keep, a_give = weights(info, nt, flat(d_oth), glow_t, flat(mixed_oth))
    a_give, f_got1 = meet([f0], a_give, f_got1)
    f1 = Chain((Rows(f_keep, 2), Rows(f_swap, 2), Rows(f_got1)), feed_moves)
    gm_own, a_oth = tie(gm_own, add_low(a_keep, swap(a_give, "core")))
    a_got0 = swap(a_oth[: width // 2], "mp")
    f0.go()
    d_own, bias_sum_own = attend_back(info, qkv_own, gm_own, lse_own)
    d_own, a_got0, a_last = meet([f0, f1], d_own, a_got0, a_oth[width // 2 :])
    a_got1 = swap(a_last, "mp")
    f1.go()
    f0.go()
    a_keep, a_give = weights(info, nt, flat(d_own), glow_t, flat(mixed_own))
    a_give, a_got1 = meet([f0, f1], a_give, a_got1)
    a_swap = swap(a_give, "core")
    d_own, a_swap = tie(d_own, a_swap)
    att = Chain((Rows(a_keep), Rows(a_swap), Stacked(a_got0, a_got1)), att_moves)
    f1.go()
    f0.go()
    out_got = swap(out_send, "mp")
    dx_keep, dx_send, end_sums = leave(
        info, d_own, d_oth, w_query, w_key, w_value, wqkv_oth, x, grad_res, ln1_gain
    )
    dx_send, end_sums = att.go((f0, f1), (dx_send, end_sums))
    f1.go()
    f0.go()

    def bias_sums(d, gbup):
        sums = jnp.sum(d, axis=(0, 1))
        return [sums[:heads], sums[2 * heads :]] + [g[0] for g in gbup]

    def small_sums(end_sums):
        shared = [end_sums[0], end_sums[1]] + [mid_sums[i] for i in range(4)]
        mine = jnp.concatenate(shared + bias_sums(bias_sum_own, [gbup_own]))
        sent = jnp.concatenate(shared + bias_sums(bias_sum_oth, [gbup0, gbup1]))
        parts = swap(mine, "core"), swap(sent, "mp"), cross(sent)
        return mine, parts

    def cross(value):
        return lax.ppermute(value, ("core", "mp"), [(i, 3 - i) for i in range(4)])

    waits = {f0: 1, f1: 1}
    pieces = {}
    vec = None
    stage = 1
    while att.moves:
        stage += 1
        live = [c for c in (vec,) if c is not None and not c.done]
        for c in (f1, f0):
            if not c.done and (c.moves or waits[c] == 0 or len(att.moves) == 1):
                live.append(c)
            elif not c.done:
                waits[c] -= 1
        if stage == 2:
            out_got, dx_send, end_sums = att.go(live, (out_got, dx_send, end_sums))
            dx_got = swap(dx_send, "mp")
            mine, others = small_sums(end_sums)
        elif vec is None:
            (others,) = att.go(live, (others,))
            along = steps[1:2] + steps[:1] + steps[2:]
            vec = Chain(
                (mine + others[1]) + (others[0] + others[2]),
                [add_over(axis, perm) for axis, _, perm in along],
            )
        elif len(att.moves) == 2:
            (dx_got,) = att.go(live, (dx_got,))
        elif len(att.moves) == 1:
            up_sum, down_sum = spread_feed(info, pieces[f0] + pieces[f1])
            up_sum, out_got, dx_got = tie(up_sum, out_got, dx_got)
            block_out = join(side, out_keep, out_got)
            input_grad = join(side, dx_keep, dx_got.astype(F32))
            up_sum, down_sum, block_out, input_grad = att.go(
                live, (up_sum, down_sum, block_out, input_grad)
            )
        else:
            att.go(live)
        for c in live:
            c.go()
            if c in waits and c.done:
                pieces[c] = c.value + (swap(c.value[1], "core"),)
    while not vec.done:
        vec.go()

    common = [vec.value[i * width : (i + 1) * width] for i in range(6)]
    split = vec.value[6 * width :]
    att.go()
    q_sum, k_sum, v_sum, o_sum = spread(info, *att.value)
    return (
        block_out,
        input_grad,
        common[0],
        common[1],
        q_sum,
        split[:heads],
        k_sum,
        v_sum,
        split[heads : 2 * heads],
        o_sum,
        common[4],
        common[2],
        common[3],
        up_sum,
        split[2 * heads :],
        down_sum,
        common[5],
    )


def solution(mesh):
    n_dp, n_mp = mesh.shape["dp"], mesh.shape["mp"]
    names = ("rest", "nbr", "core", "mp")
    inner = Mesh(mesh.devices.reshape(n_dp // 4, 2, 2, n_mp), names)
    dp = ("rest", "nbr", "core")
    in_specs = (
        P(dp, "mp", None),
        P(dp),
        P(dp, "mp", None),
        P(),
        P(),
        P(None, "mp"),
        P("mp"),
        P(None, "mp"),
        P(None, "mp"),
        P("mp"),
        P("mp", None),
        P(),
        P(),
        P(),
        P(None, "mp"),
        P("mp"),
        P("mp", None),
        P(),
    )
    out_specs = (
        P(dp, "mp", None),
        P(dp, "mp", None),
        P(),
        P(),
        P(None, "mp"),
        P("mp"),
        P(None, "mp"),
        P(None, "mp"),
        P("mp"),
        P("mp", None),
        P(),
        P(),
        P(),
        P(None, "mp"),
        P("mp"),
        P("mp", None),
        P(),
    )
    return jax.shard_map(
        functools.partial(on_device, dict(inner.shape)),
        mesh=inner,
        in_specs=in_specs,
        out_specs=out_specs,
        check_vma=False,
    )
```

```python
import functools
import math

import jax
import jax.numpy as jnp
from jax import lax
from jax.experimental import pallas as pl
from jax.experimental.pallas import tpu as pltpu
from jax.sharding import Mesh
from jax.sharding import PartitionSpec as P

HEAD_DIM = 64
PAIR = 2 * HEAD_DIM
EPS = 1e-12
FILL = -1000000000.0
SCALE = 1.0 / math.sqrt(HEAD_DIM)
LOG2E = math.log2(math.e)
F32 = jnp.float32
BF16 = jnp.bfloat16
NT = (((1,), (1,)), ((), ()))
NN = (((1,), (0,)), ((), ()))
TN = (((0,), (0,)), ((), ()))


def mm(a, b, dims=NN):
    return lax.dot_general(a, b, dims, preferred_element_type=F32)


def key_mask(info, row, shape):
    seq = shape[0]
    slot = lax.broadcasted_iota(jnp.int32, shape, 0) + info[0]
    position = jnp.where(slot >= seq, slot - seq, slot)
    return position < info[3 + row]


def head_lanes(value, head):
    lane = lax.broadcasted_iota(jnp.int32, value.shape, 1)
    keep = lane < HEAD_DIM if head == 0 else lane >= HEAD_DIM
    return jnp.where(keep, value, jnp.zeros_like(value))


def attend_kernel(info, q_ref, k_ref, v_ref, o_ref, lse_ref):
    row = pl.program_id(0)
    q, k, v = q_ref[0], k_ref[0], v_ref[0]
    valid = key_mask(info, row, (k.shape[0], q.shape[0]))
    v_t = v.T
    seq = k.shape[0]
    both = mm(jnp.concatenate([head_lanes(k, 0), head_lanes(k, 1)], axis=0), q, NT)
    parts = []
    for head in range(2):
        scores = both[head * seq : (head + 1) * seq] * (SCALE * LOG2E)
        scores = jnp.where(valid, scores, FILL * LOG2E)
        top = jnp.max(scores, axis=0, keepdims=True)
        weight = jnp.exp2(scores - top)
        total = jnp.sum(weight, axis=0, keepdims=True)
        lse_ref[0, 0, head : head + 1, :] = top + jnp.log2(total)
        probs = (weight * (1.0 / total)).astype(BF16)
        parts.append(mm(v_t[head * HEAD_DIM : (head + 1) * HEAD_DIM], probs))
    o_ref[0] = jnp.concatenate(parts, axis=0).T.astype(BF16)


def attend_back_kernel(info, q_ref, k_ref, v_ref, do_ref, lse_ref, d_ref, sum_ref):
    row = pl.program_id(0)
    pair = pl.program_id(1)
    n_pairs = pl.num_programs(1)
    q, k, v, do = q_ref[0], k_ref[0], v_ref[0], do_ref[0]
    valid = key_mask(info, row, (k.shape[0], q.shape[0]))
    k_t = k.T
    dq_t, dk, dv = [], [], []
    for head in range(2):
        scores = mm(head_lanes(k, head), q, NT) * (SCALE * LOG2E)
        scores = jnp.where(valid, scores, FILL * LOG2E)
        probs = jnp.exp2(scores - lse_ref[0, 0, head : head + 1, :])
        dv.append(mm(probs.astype(BF16), do))
        dprobs = mm(head_lanes(v, head), do, NT)
        delta = jnp.sum(probs * dprobs, axis=0, keepdims=True)
        dscores = (probs * (dprobs - delta)).astype(BF16)
        dk.append(mm(dscores, q))
        dq_t.append(mm(k_t[head * HEAD_DIM : (head + 1) * HEAD_DIM], dscores))
    first = lax.broadcasted_iota(jnp.int32, dv[0].shape, 1) < HEAD_DIM
    dq = jnp.concatenate(dq_t, axis=0).T * SCALE

    def put(slot, value):
        start = pl.multiple_of((slot * n_pairs + pair) * PAIR, PAIR)
        low = value.astype(BF16)
        d_ref[0, :, pl.ds(start, PAIR)] = low
        sum_ref[0, :, pl.ds(start, PAIR)] = jnp.sum(low.astype(F32), axis=0, keepdims=True)

    put(0, dq)
    put(1, jnp.where(first, dk[0], dk[1]) * SCALE)
    put(2, jnp.where(first, dv[0], dv[1]))


def attend_specs(seq, n_pairs):
    return [
        pl.BlockSpec((1, seq, PAIR), lambda r, p, info: (r, 0, p)),
        pl.BlockSpec((1, seq, PAIR), lambda r, p, info: (r, 0, n_pairs + p)),
        pl.BlockSpec((1, seq, PAIR), lambda r, p, info: (r, 0, 2 * n_pairs + p)),
    ]


MIB = 1024 * 1024
VMEM_MIB = {"enter": 50, "middle": 50, "middle_back": 50, "leave": 50}


def cost(micros):
    return pl.CostEstimate(flops=int(micros * 1.15e9), bytes_accessed=1000, transcendentals=0)


def attend(info, qkv):
    rows, seq, width = qkv.shape
    n_pairs = width // (3 * PAIR)
    return pl.pallas_call(
        attend_kernel,
        out_shape=(
            jax.ShapeDtypeStruct((rows, seq, n_pairs * PAIR), BF16),
            jax.ShapeDtypeStruct((rows, n_pairs, 2, seq), F32),
        ),
        grid_spec=pltpu.PrefetchScalarGridSpec(
            num_scalar_prefetch=1,
            grid=(rows, n_pairs),
            in_specs=attend_specs(seq, n_pairs),
            out_specs=(
                pl.BlockSpec((1, seq, PAIR), lambda r, p, info: (r, 0, p)),
                pl.BlockSpec((1, 1, 2, seq), lambda r, p, info: (r, p, 0, 0)),
            ),
        ),
        compiler_params=pltpu.CompilerParams(vmem_limit_bytes=20 * MIB),
        cost_estimate=cost(10),
        name="attend",
    )(info, qkv, qkv, qkv)


def attend_back(info, qkv, grad_mixed, lse):
    rows, seq, width = qkv.shape
    n_pairs = width // (3 * PAIR)
    return pl.pallas_call(
        attend_back_kernel,
        out_shape=(
            jax.ShapeDtypeStruct((rows, seq, width), BF16),
            jax.ShapeDtypeStruct((rows, 1, width), F32),
        ),
        grid_spec=pltpu.PrefetchScalarGridSpec(
            num_scalar_prefetch=1,
            grid=(rows, n_pairs),
            in_specs=attend_specs(seq, n_pairs)
            + [
                pl.BlockSpec((1, seq, PAIR), lambda r, p, info: (r, 0, p)),
                pl.BlockSpec((1, 1, 2, seq), lambda r, p, info: (r, p, 0, 0)),
            ],
            out_specs=(
                pl.BlockSpec((1, seq, width), lambda r, p, info: (r, 0, 0)),
                pl.BlockSpec((1, 1, width), lambda r, p, info: (r, 0, 0)),
            ),
        ),
        compiler_params=pltpu.CompilerParams(vmem_limit_bytes=24 * MIB),
        cost_estimate=cost(13),
        name="attend_back",
    )(info, qkv, qkv, qkv, grad_mixed, lse)


def feed_kernel(first, own, info, *refs):
    refs = list(refs)
    nm, wa, wb, bu = refs[:4]
    refs = refs[4:]
    if own:
        wu, wd = refs[:2]
        refs = refs[2:]
    nt_hbm, up_hbm = refs[:2]
    refs = refs[2:]
    if not first:
        y_hbm, gnm_hbm = refs[:2]
        refs = refs[2:]
    y_out, gnm_out, keep, send, gbu, nt, up, y, gnm, sems = refs
    step = pl.program_id(0)
    last = pl.num_programs(0) - 1
    core = info[1]
    copies = [
        pltpu.make_async_copy(up_hbm, up, sems.at[0]),
        pltpu.make_async_copy(nt_hbm, nt, sems.at[1]),
    ]
    if not first:
        copies += [
            pltpu.make_async_copy(y_hbm, y, sems.at[2]),
            pltpu.make_async_copy(gnm_hbm, gnm, sems.at[3]),
        ]
    out_y = pltpu.make_async_copy(y, y_out, sems.at[4])
    out_gnm = pltpu.make_async_copy(gnm, gnm_out, sems.at[5])

    @pl.when(step == 0)
    def _():
        for copy in copies:
            copy.start()
        for copy in copies:
            copy.wait()

    w_up = jnp.where(core == 0, wa[...], wb[...])
    w_down = jnp.where(core == 0, wb[...], wa[...])
    if own:
        w_up = jnp.where(step == 0, w_up, wu[...])
        w_down = jnp.where(step == 0, w_down, wd[...])
    h = mm(nm[...], w_up) + bu[...]
    cdf = 0.5 * (1.0 + lax.erf(h * (1.0 / math.sqrt(2.0))))
    active = (h * cdf).astype(BF16)
    slope = cdf + h * jnp.exp(-0.5 * h * h) * (1.0 / math.sqrt(2.0 * math.pi))
    grad_hidden = (mm(up[...], w_down, NT) * slope).astype(BF16)
    gbu[...] = jnp.sum(grad_hidden.astype(F32), axis=0, keepdims=True)
    if first:
        y[...] = mm(active, w_down)
        gnm[...] = mm(grad_hidden, w_up, NT)
    else:
        y[...] += mm(active, w_down)
        gnm[...] += mm(grad_hidden, w_up, NT)
    grad_down = mm(active, up[...], TN).astype(BF16)

    @pl.when(step == last)
    def _():
        out_y.start()
        out_gnm.start()

    grad_up = mm(nt[...], grad_hidden).astype(BF16)
    keep[0] = jnp.where(core == 0, grad_up, grad_down)
    send[0] = jnp.where(core == 0, grad_down, grad_up)

    @pl.when(step == last)
    def _():
        out_y.wait()
        out_gnm.wait()


def feed(info, nm, nt, up, wa, wb, bu, own=None, sums=None):
    tokens, width = nm.shape
    count = bu.shape[1] // width
    first = sums is None
    once = lambda shape: pl.BlockSpec(shape, lambda f, info: (0, 0), pipeline_mode=pl.Buffered(1))
    place = pl.BlockSpec(memory_space=pl.ANY)
    row = pl.BlockSpec((1, width), lambda f, info: (0, f))
    in_specs = [once((tokens, width)), once(wa.shape), once(wb.shape), row]
    args = [nm, wa, wb, bu]
    if own is not None:
        in_specs += [
            pl.BlockSpec((width, width), lambda f, info: (0, jnp.maximum(f - 1, 0))),
            pl.BlockSpec((width, width), lambda f, info: (jnp.maximum(f - 1, 0), 0)),
        ]
        args += list(own)
    in_specs += [place] * 2
    args += [nt, up]
    if not first:
        in_specs += [place] * 2
        args += list(sums)
    grads = pl.BlockSpec((1, width, width), lambda f, info: (f, 0, 0))
    return pl.pallas_call(
        functools.partial(feed_kernel, first, own is not None),
        out_shape=(
            shaped(tokens, width, dtype=F32),
            shaped(tokens, width, dtype=F32),
            shaped(count, width, width),
            shaped(count, width, width),
            shaped(1, count * width, dtype=F32),
        ),
        grid_spec=pltpu.PrefetchScalarGridSpec(
            num_scalar_prefetch=1,
            grid=(count,),
            in_specs=in_specs,
            out_specs=(place, place, grads, grads, row),
            scratch_shapes=[
                pltpu.VMEM((width, tokens), BF16),
                pltpu.VMEM((tokens, width), BF16),
                pltpu.VMEM((tokens, width), F32),
                pltpu.VMEM((tokens, width), F32),
                pltpu.SemaphoreType.DMA((6,)),
            ],
        ),
        compiler_params=pltpu.CompilerParams(vmem_limit_bytes=40 * MIB),
        cost_estimate=cost(12 * count),
        name="feed_own" if own is not None else "feed_other",
    )(info, *args)


def norm(values):
    average = jnp.mean(values, axis=-1, keepdims=True)
    centred = values - average
    inv = lax.rsqrt(jnp.mean(centred * centred, axis=-1, keepdims=True) + EPS)
    return centred * inv, inv


def norm_back(grad, unit, inv, gain):
    scaled = grad * gain
    return inv * (
        scaled
        - jnp.mean(scaled, axis=-1, keepdims=True)
        - unit * jnp.mean(scaled * unit, axis=-1, keepdims=True)
    )


def stack(first, second):
    return jnp.concatenate([first, second], axis=0)


def row_grid(kernel, name, micros, rows, in_specs, out_shape, out_specs, args):
    return pl.pallas_call(
        kernel,
        out_shape=out_shape,
        grid_spec=pltpu.PrefetchScalarGridSpec(
            num_scalar_prefetch=1, grid=(rows,), in_specs=in_specs, out_specs=out_specs
        ),
        compiler_params=pltpu.CompilerParams(vmem_limit_bytes=VMEM_MIB.get(name, 28) * MIB),
        cost_estimate=cost(micros),
        name=name,
    )(*args)


def fixed(shape):
    return pl.BlockSpec(shape, lambda r, info: (0,) * len(shape))


def const(shape):
    return pl.BlockSpec(
        shape, lambda r, info: (0,) * len(shape), pipeline_mode=pl.Buffered(1)
    )


def per_row(*shape):
    return pl.BlockSpec((1,) + shape, lambda r, info: (r,) + (0,) * len(shape))


def kept_row(*shape):
    return pl.BlockSpec((1,) + shape, lambda r, info: (info[2] + r,) + (0,) * len(shape))


def shaped(*shape, dtype=BF16):
    return jax.ShapeDtypeStruct(shape, dtype)


def enter_kernel(info, tok, got, wq, wk, wv, bias, gain, shift, x_out, n_out, nt_out, qkv):
    heads = wq.shape[1]
    x = stack(tok[0], got[0])
    x_out[0] = x
    unit, _ = norm(x.astype(F32))
    normed = (unit * gain[...] + shift[...]).astype(BF16)
    n_out[0] = normed
    nt_out[...] = normed.T
    qkv[0, :, :heads] = (mm(normed, wq[...]) + bias[:, :heads]).astype(BF16)
    qkv[0, :, heads : 2 * heads] = mm(normed, wk[...]).astype(BF16)
    qkv[0, :, 2 * heads :] = (mm(normed, wv[...]) + bias[:, heads : 2 * heads]).astype(BF16)


def enter(info, tokens, got, wq, wk, wv, bias, gain, shift):
    rows, half, width = got.shape
    seq, heads = 2 * half, wq.shape[1]
    return row_grid(
        enter_kernel,
        "enter",
        0,
        rows,
        [kept_row(half, width), per_row(half, width)]
        + [const(wq.shape)] * 3
        + [const(bias.shape)]
        + [const((1, width))] * 2,
        (
            shaped(rows, seq, width),
            shaped(rows, seq, width),
            shaped(width, rows * seq),
            shaped(rows, seq, 3 * heads),
        ),
        (
            per_row(seq, width),
            per_row(seq, width),
            pl.BlockSpec((width, seq), lambda r, info: (0, r)),
            per_row(seq, 3 * heads),
        ),
        (info, tokens, got, wq, wk, wv, bias, gain[None], shift[None]),
    )


def other_heads_kernel(info, n, p0, p1, p2, p3, bias, qkv, w):
    heads = w.shape[1] // 3

    @pl.when(pl.program_id(0) == 0)
    def _():
        nbr, core = info[3 + pl.num_programs(0)], info[1]
        size = p0.shape[0]
        for index, piece in enumerate((p0, p1, p2, p3)):
            row = 1 - nbr if index >= 2 else nbr
            col = 1 - core if index % 2 else core
            start = pl.multiple_of((2 * row + col) * size, size)
            w[pl.ds(start, size), :] = piece[...]

    full = jnp.concatenate(
        [bias[:, :heads], jnp.zeros((1, heads), F32), bias[:, heads : 2 * heads]], axis=1
    )
    qkv[0] = (mm(n[0], w[...]) + full).astype(BF16)


def other_heads(info, n, pieces, bias):
    rows, seq, width = n.shape
    size, wide = pieces[0].shape
    return row_grid(
        other_heads_kernel,
        "other_heads",
        0,
        rows,
        [per_row(seq, width)] + [const((size, wide))] * 4 + [const(bias.shape)],
        (shaped(rows, seq, wide), shaped(width, wide)),
        (per_row(seq, wide), fixed((width, wide))),
        (info, n, *pieces, bias),
    )


def middle_kernel(
    info, x, m_own, m_oth, w_own, w_mine, w_cross, b_out, gain, shift, grad, got, res, nm, nm_t, up, w_oth
):
    @pl.when(pl.program_id(0) == 0)
    def _():
        size = w_mine.shape[0]
        w_oth[pl.ds(pl.multiple_of(info[1] * size, size), size), :] = w_mine[...]
        w_oth[pl.ds(pl.multiple_of((1 - info[1]) * size, size), size), :] = w_cross[...]

    attended = mm(m_own[0], w_own[...]) + mm(m_oth[0], w_oth[...])
    residual = x[0].astype(F32) + attended + b_out[...]
    res[0] = residual
    unit, _ = norm(residual)
    normed = (unit * gain[...] + shift[...]).astype(BF16)
    nm[0] = normed
    nm_t[...] = normed.T
    up[0] = stack(grad[0], got[0])


def middle(info, x, m_own, m_oth, w_own, w_mine, w_cross, b_out, gain, shift, grad, got):
    rows, seq, width = x.shape
    heads = w_own.shape[0]
    return row_grid(
        middle_kernel,
        "middle",
        0,
        rows,
        [per_row(seq, width), per_row(seq, heads), per_row(seq, heads)]
        + [const(w_own.shape), const(w_mine.shape), const(w_mine.shape)]
        + [const((1, width))] * 3
        + [kept_row(seq // 2, width), per_row(seq // 2, width)],
        (
            shaped(rows, seq, width, dtype=F32),
            shaped(rows, seq, width),
            shaped(width, rows * seq),
            shaped(rows, seq, width),
            shaped(heads, width),
        ),
        (
            per_row(seq, width),
            per_row(seq, width),
            pl.BlockSpec((width, seq), lambda r, info: (0, r)),
            per_row(seq, width),
            fixed((heads, width)),
        ),
        (info, x, m_own, m_oth, w_own, w_mine, w_cross, b_out[None], gain[None], shift[None], grad, got),
    )


def middle_back_kernel(
    info, gnm, res, y, up, gain, b_down, w_own, w_oth, keep, send, gres, glow_t, gm_own, gm_oth, sums
):
    half = keep.shape[1]
    residual, grad, upstream = res[0], gnm[0], up[0].astype(F32)
    out = (residual + y[0] + b_down[...]).astype(BF16)
    keep[0] = out[:half]
    send[0] = out[half:]
    unit, inv = norm(residual)
    total = upstream + norm_back(grad, unit, inv, gain[...])
    gres[0] = total
    low = total.astype(BF16)
    glow_t[...] = low.T
    gm_own[0] = mm(low, w_own[...], NT).astype(BF16)
    gm_oth[0] = mm(low, w_oth[...], NT).astype(BF16)

    @pl.when(pl.program_id(0) == 0)
    def _():
        sums[...] = jnp.zeros_like(sums)

    for index, value in enumerate((grad * unit, grad, total, upstream)):
        sums[index : index + 1, :] += jnp.sum(value, axis=0, keepdims=True)


def middle_back(info, gnm, res, y, up, gain, b_down, w_own, w_oth):
    rows, seq, width = res.shape
    heads = w_own.shape[0]
    row = per_row(seq, width)
    half = per_row(seq // 2, width)
    return row_grid(
        middle_back_kernel,
        "middle_back",
        0,
        rows,
        [row] * 4 + [const((1, width))] * 2 + [const((heads, width))] * 2,
        (
            shaped(rows, seq // 2, width),
            shaped(rows, seq // 2, width),
            shaped(rows, seq, width, dtype=F32),
            shaped(width, rows * seq),
            shaped(rows, seq, heads),
            shaped(rows, seq, heads),
            shaped(8, width, dtype=F32),
        ),
        (
            half,
            half,
            row,
            pl.BlockSpec((width, seq), lambda r, info: (0, r)),
            per_row(seq, heads),
            per_row(seq, heads),
            fixed((8, width)),
        ),
        (info, gnm, res, y, up, gain[None], b_down[None], w_own, w_oth),
    )


def weights_kernel(info, nt, d, glow_t, mixed, keep, send):
    heads = mixed.shape[1]
    g = mm(nt[...], d[...]).astype(BF16)
    o = mm(glow_t[...], mixed[...]).astype(BF16)
    cut = 2 * heads

    @pl.when(info[1] == 0)
    def _():
        keep[...] = g[:, :cut]
        send[:, :heads] = g[:, cut:]
        send[:, heads:] = o

    @pl.when(info[1] != 0)
    def _():
        send[...] = g[:, :cut]
        keep[:, :heads] = g[:, cut:]
        keep[:, heads:] = o


def weights(info, nt, d, glow_t, mixed, block=256):
    width, tokens = nt.shape
    heads = mixed.shape[1]
    part = pl.BlockSpec((block, tokens), lambda r, info: (r, 0))
    result = pl.BlockSpec((block, 2 * heads), lambda r, info: (r, 0))
    return row_grid(
        weights_kernel,
        "weights",
        0,
        width // block,
        [part, const(d.shape), part, const(mixed.shape)],
        (shaped(width, 2 * heads), shaped(width, 2 * heads)),
        (result, result),
        (info, nt, d, glow_t, mixed),
    )


def leave_kernel(info, d_own, d_oth, wq, wk, wv, w_oth, x, gres, gain, keep, send, sums):
    heads = wq.shape[1]
    half = keep.shape[1]
    grad = (
        mm(d_own[0, :, :heads], wq[...], NT)
        + mm(d_own[0, :, heads : 2 * heads], wk[...], NT)
        + mm(d_own[0, :, 2 * heads :], wv[...], NT)
        + mm(d_oth[0], w_oth[...], NT)
    )
    unit, inv = norm(x[0].astype(F32))
    total = gres[0] + norm_back(grad, unit, inv, gain[...])
    keep[0] = total[:half]
    send[0] = total[half:].astype(BF16)

    @pl.when(pl.program_id(0) == 0)
    def _():
        sums[...] = jnp.zeros_like(sums)

    for index, value in enumerate((grad * unit, grad)):
        sums[index : index + 1, :] += jnp.sum(value, axis=0, keepdims=True)


def leave(info, d_own, d_oth, wq, wk, wv, w_oth, x, gres, gain):
    rows, seq, width = x.shape
    row = per_row(seq, width)
    half = per_row(seq // 2, width)
    wide = per_row(seq, d_own.shape[2])
    return row_grid(
        leave_kernel,
        "leave",
        10,
        rows,
        [wide, wide]
        + [const(wq.shape)] * 3
        + [const(w_oth.shape), row, row, const((1, width))],
        (
            shaped(rows, seq // 2, width, dtype=F32),
            shaped(rows, seq // 2, width),
            shaped(8, width, dtype=F32),
        ),
        (half, half, fixed((8, width))),
        (info, d_own, d_oth, wq, wk, wv, w_oth, x, gres, gain[None]),
    )


def spread_kernel(info, mine, near, cross, both, q, k, v, o):
    heads = q.shape[1]
    here = pl.program_id(0) == info[info.shape[0] - 1]
    own = jnp.where(here, mine[...], near[...]).astype(F32)
    other = jnp.where(here, cross[...], both[...]).astype(F32)

    def write(first, second):
        q[...] = first[:, :heads]
        k[...] = first[:, heads:]
        v[...] = second[:, :heads]
        o[...] = second[:, heads:].T

    @pl.when(info[1] == 0)
    def _():
        write(own, other)

    @pl.when(info[1] != 0)
    def _():
        write(other, own)


def spread(info, *pieces):
    block, both = pieces[0].shape
    heads = both // 2
    plain = pl.BlockSpec((block, heads), lambda n, info: (n, 0))
    return row_grid(
        spread_kernel,
        "spread",
        3,
        2,
        [const((block, both))] * 4,
        (shaped(2 * block, heads, dtype=F32),) * 3 + (shaped(heads, 2 * block, dtype=F32),),
        (plain,) * 3 + (pl.BlockSpec((heads, block), lambda n, info: (0, n)),),
        (info, *pieces),
    )


def spread_feed_kernel(info, *refs):
    nbr, core = info[info.shape[0] - 1], info[1]
    up, down = refs[-2:]
    here = pl.program_id(1) == nbr
    for chunk in range(2):
        mine, near, cross, both = refs[4 * chunk : 4 * chunk + 4]

        @pl.when(pl.program_id(0) == chunk)
        def _():
            own = jnp.where(here, mine[...], near[...]).astype(F32)
            other = jnp.where(here, cross[...], both[...]).astype(F32)
            up[...] = jnp.where(core == 0, own, other)
            down[...] = jnp.where(core == 0, other, own)


def spread_feed(info, pieces):
    block, width = pieces[0].shape
    once = pl.BlockSpec((block, width), lambda k, n, info: (0, 0), pipeline_mode=pl.Buffered(1))
    return pl.pallas_call(
        spread_feed_kernel,
        out_shape=(shaped(width, 2 * width, dtype=F32), shaped(2 * width, width, dtype=F32)),
        grid_spec=pltpu.PrefetchScalarGridSpec(
            num_scalar_prefetch=1,
            grid=(2, 2),
            in_specs=[once] * 8,
            out_specs=(
                pl.BlockSpec((block, width), lambda k, n, info: (n, k)),
                pl.BlockSpec((block, width), lambda k, n, info: (2 * k + n, 0)),
            ),
        ),
        compiler_params=pltpu.CompilerParams(vmem_limit_bytes=24 * MIB),
        cost_estimate=cost(5),
        name="spread_feed",
    )(info, *pieces)


def swap(value, axis):
    return lax.ppermute(value, axis, [(0, 1), (1, 0)])


def part(value, index, count):
    size = value.shape[0] // count
    return lax.dynamic_slice_in_dim(value, index * size, size, 0)


class Rows:
    def __init__(self, array, matrix=None, start=0, size=None):
        self.array, self.matrix, self.start = array, matrix, start
        self.size = array.shape[-2] if size is None else size

    def half(self, index):
        size = self.size // 2
        return Rows(self.array, self.matrix, self.start + index * size, size)

    def read(self):
        if self.matrix is None:
            return lax.dynamic_slice_in_dim(self.array, self.start, self.size, 0)
        shape = (1, self.size, self.array.shape[-1])
        return lax.dynamic_slice(self.array, (self.matrix, self.start, 0), shape)[0]


class Either:
    def __init__(self, index, first, second):
        self.index, self.first, self.second = index, first, second

    def half(self, index):
        return Either(self.index, self.first.half(index), self.second.half(index))

    def read(self):
        return jnp.where(self.index == 0, self.first.read(), self.second.read())


class Stacked:
    def __init__(self, upper, lower):
        self.upper, self.lower = Rows(upper), Rows(lower)

    def half(self, index):
        return Either(index, self.upper, self.lower)


def total_low(addends):
    return add_low(*[addend.read() for addend in addends])


def join(index, mine, other):
    return jnp.where(index == 0, jnp.concatenate([mine, other]), jnp.concatenate([other, mine]))


def tie(*values):
    return lax.optimization_barrier(values)


def add_low(*addends):
    return sum(addend.astype(F32) for addend in addends).astype(BF16)


def ladder(sizes):
    steps = [("nbr", lax.axis_index("nbr"), [(0, 1), (1, 0)])]
    bit = 1
    while bit < sizes["rest"]:
        index = (lax.axis_index("rest") // bit) % 2
        steps.append(("rest", index, [(i, i ^ bit) for i in range(sizes["rest"])]))
        bit *= 2
    return steps


def halve(step):
    axis, index, perm = step

    def prepare(addends):
        sent = total_low([a.half(1 - index) for a in addends])
        return sent, tuple(a.half(index) for a in addends)

    return (
        prepare,
        lambda sent: (lax.ppermute(sent, axis, perm),),
        lambda kept, got: kept + (Rows(got),),
    )


def double(step):
    axis, index, perm = step

    def prepare(value):
        if isinstance(value, tuple):
            value = total_low(value)
        return value, value

    return prepare, lambda sent: (lax.ppermute(sent, axis, perm),), functools.partial(join, index)


def twice(value):
    return value, value


def to_pair(axis):
    return (
        lambda three: (three[1], three),
        lambda sent: (swap(sent, axis),),
        lambda three, got: three + (got,),
    )


def to_three():
    return (
        twice,
        lambda sent: (swap(sent, "nbr"), swap(sent, "core")),
        lambda value, near, cross: (value, near, cross),
    )


def add_over(axis, perm):
    return twice, lambda sent: (lax.ppermute(sent, axis, perm),), jnp.add


class Chain:
    def __init__(self, value, moves, behind=()):
        self.value, self.finish, self.moves, self.flying = value, None, list(moves), ()
        self.go(behind)

    def go(self, behind=(), values=()):
        if self.finish is not None:
            self.value, self.finish = self.finish(self.value, *self.flying), None
            self.flying = ()
        if self.moves:
            prepare, launch, self.finish = self.moves.pop(0)
            sent, self.value = prepare(self.value)
            if behind or values:
                sent, values = meet(behind, sent, list(values))
            self.flying = launch(sent)
        return values

    @property
    def done(self):
        return self.finish is None


def meet(chains, *values):
    flying, tied = lax.optimization_barrier(([c.flying for c in chains], list(values)))
    for c, transfers in zip(chains, flying):
        c.flying = tuple(transfers)
    return tied[0] if len(tied) == 1 else tied


def on_device(
    sizes,
    tokens,
    lengths,
    out_grad,
    ln1_gain,
    ln1_shift,
    w_query,
    b_query,
    w_key,
    w_value,
    b_value,
    w_out,
    b_out,
    ln2_gain,
    ln2_shift,
    w_up,
    b_up,
    w_down,
    b_down,
):
    side = lax.axis_index("mp")
    core = lax.axis_index("core")
    nbr = lax.axis_index("nbr")
    rows_dev, half, width = tokens.shape
    rows = rows_dev // 2
    seq = 2 * half
    total = rows * seq
    heads = w_query.shape[1]
    units = w_up.shape[1] // 2
    steps = ladder(sizes)

    def by_core(first, second):
        return jnp.where(core == 0, first, second)

    def flat(value):
        return value.reshape(total, value.shape[-1])

    info = jnp.concatenate(
        [jnp.stack([side * half, core, side * rows]), part(lengths, side, 2), nbr[None]]
    ).astype(jnp.int32)

    quarter = 2 * nbr + core
    w_send = jnp.concatenate([part(w, quarter, 4) for w in (w_query, w_key, w_value)], axis=1)
    t_send = part(tokens, 1 - side, 2)
    got_tokens = swap(t_send, "mp")
    w_mine = swap(w_send, "mp")
    bias_own = jnp.concatenate([b_query, b_value, b_up])
    bias_oth = swap(bias_own, "mp")
    up_halves = [w_up[:, :units], w_up[:, units:]]
    down_halves = [w_down[:units], w_down[units:]]
    f_send0 = part(by_core(up_halves[0], down_halves[0]), nbr, 2)
    f_send1 = by_core(up_halves[1], down_halves[1])
    g_send = part(out_grad, 1 - side, 2)
    o_send = part(w_out, core, 2)
    got_tokens, f_send0, f_send1, g_send, o_send = tie(
        got_tokens, f_send0, f_send1, g_send, o_send
    )
    x, normed_in, nt, qkv_own = enter(
        info, tokens, got_tokens, w_query, w_key, w_value, bias_own[None], ln1_gain, ln1_shift
    )
    f_mine0 = swap(f_send0, "mp")
    o_mine = swap(o_send, "mp")
    qkv_own, w_mine, bias_oth = tie(qkv_own, w_mine, bias_oth)
    w_near = swap(w_mine, "nbr")
    mixed_own, lse_own = attend(info, qkv_own)
    mixed_own, w_near, g_send = tie(mixed_own, w_near, g_send)
    pieces = (w_mine, swap(w_mine, "core"), w_near, swap(w_near, "core"))
    got_grad = swap(g_send, "mp")
    qkv_oth, wqkv_oth = other_heads(info, normed_in, pieces, bias_oth[None])
    qkv_oth, f_mine0, f_send1, o_mine = tie(qkv_oth, f_mine0, f_send1, o_mine)
    f_half0 = join(nbr, f_mine0, swap(f_mine0, "nbr"))
    f_mine1 = swap(f_send1, "mp")
    mixed_oth, lse_oth = attend(info, qkv_oth)
    mixed_oth, f_half0, got_grad = tie(mixed_oth, f_half0, got_grad)
    f_cross0 = swap(f_half0, "core")
    residual, nm, nm_t, up, wout_oth = middle(
        info, x, mixed_own, mixed_oth, w_out, o_mine, swap(o_mine, "core"),
        b_out, ln2_gain, ln2_shift, out_grad, got_grad,
    )
    bup_own = bias_own[2 * heads :][None]
    bup_oth = bias_oth[2 * heads :][None]
    args = (info, flat(nm), nm_t, flat(up))
    y, gnm, f_keep0, f_give0, gbup0 = feed(*args, f_half0, f_cross0, bup_oth[:, :units])
    y, f_give0, f_mine1 = tie(y, f_give0[0], f_mine1)
    f_swap0, f_cross1 = swap(f_give0, "core"), swap(f_mine1, "core")
    y, f_oth0, f_cross1 = tie(y, add_low(f_keep0[0], f_swap0), f_cross1)
    f_got0 = swap(f_oth0, "mp")
    bup_rest = jnp.concatenate([bup_oth[:, units:], bup_own], axis=1)
    y, gnm, f_keep, f_give, gbup_rest = feed(
        *args, f_mine1, f_cross1, bup_rest, own=(w_up, w_down), sums=(y, gnm)
    )
    gbup1, gbup_own = gbup_rest[:, :units], gbup_rest[:, units:]
    gnm, f_give, f_got0 = tie(gnm, f_give, f_got0)
    f_swap = swap(f_give, "core")
    out_keep, out_send, grad_res, glow_t, gm_own, gm_oth, mid_sums = middle_back(
        info, gnm.reshape(rows, seq, width), residual, y.reshape(rows, seq, width), up,
        ln2_gain, b_down, w_out, wout_oth,
    )
    gm_oth, f_swap = tie(gm_oth, f_swap)
    f_got1 = swap(add_low(f_keep[0], f_swap[0]), "mp")
    halving = [halve(step) for step in steps]
    doubling = [double(step) for step in reversed(steps)]
    feed_moves = halving + doubling[:-1] + [to_three()]
    att_moves = feed_moves + [to_pair("core")]
    f0 = Chain((Rows(f_keep, 1), Rows(f_swap, 1), Rows(f_got0)), feed_moves)
    d_oth, bias_sum_oth = attend_back(info, qkv_oth, gm_oth, lse_oth)
    d_oth = meet([f0], d_oth)
    f0.go()
    a_keep, a_give = weights(info, nt, flat(d_oth), glow_t, flat(mixed_oth))
    a_give, f_got1 = meet([f0], a_give, f_got1)
    f1 = Chain((Rows(f_keep, 2), Rows(f_swap, 2), Rows(f_got1)), feed_moves)
    gm_own, a_oth = tie(gm_own, add_low(a_keep, swap(a_give, "core")))
    a_got0 = swap(a_oth[: width // 2], "mp")
    f0.go()
    d_own, bias_sum_own = attend_back(info, qkv_own, gm_own, lse_own)
    d_own, a_got0, a_last = meet([f0, f1], d_own, a_got0, a_oth[width // 2 :])
    a_got1 = swap(a_last, "mp")
    f1.go()
    f0.go()
    a_keep, a_give = weights(info, nt, flat(d_own), glow_t, flat(mixed_own))
    a_give, a_got1 = meet([f0, f1], a_give, a_got1)
    a_swap = swap(a_give, "core")
    d_own, a_swap = tie(d_own, a_swap)
    att = Chain((Rows(a_keep), Rows(a_swap), Stacked(a_got0, a_got1)), att_moves)
    f1.go()
    f0.go()
    out_got = swap(out_send, "mp")
    dx_keep, dx_send, end_sums = leave(
        info, d_own, d_oth, w_query, w_key, w_value, wqkv_oth, x, grad_res, ln1_gain
    )
    dx_send, end_sums = att.go((f0, f1), (dx_send, end_sums))
    f1.go()
    f0.go()

    def bias_sums(d, gbup):
        sums = jnp.sum(d, axis=(0, 1))
        return [sums[:heads], sums[2 * heads :]] + [g[0] for g in gbup]

    def small_sums(end_sums):
        shared = [end_sums[0], end_sums[1]] + [mid_sums[i] for i in range(4)]
        mine = jnp.concatenate(shared + bias_sums(bias_sum_own, [gbup_own]))
        sent = jnp.concatenate(shared + bias_sums(bias_sum_oth, [gbup0, gbup1]))
        parts = swap(mine, "core"), swap(sent, "mp"), cross(sent)
        return [mine] + list(parts)

    def cross(value):
        return lax.ppermute(value, ("core", "mp"), [(i, 3 - i) for i in range(4)])

    terms = small_sums(end_sums)
    waits = {f0: 1, f1: 1}
    pieces = {}
    vec = dx_got = None
    stage = 1
    while att.moves:
        stage += 1
        live = [c for c in (vec,) if c is not None and not c.done]
        for c in (f1, f0):
            if not c.done and (c.moves or waits[c] == 0 or len(att.moves) == 1):
                live.append(c)
            elif not c.done:
                waits[c] -= 1
        if vec is None:
            out_got, terms = att.go(live, (out_got, terms))
            vec = Chain(
                (terms[0] + terms[2]) + (terms[1] + terms[3]),
                [add_over(axis, perm) for axis, _, perm in steps],
            )
        elif dx_got is None:
            (dx_send,) = att.go(live, (dx_send,))
            dx_got = swap(dx_send, "mp")
        elif len(att.moves) == 3:
            (out_got,) = att.go(live, (out_got,))
            block_out = join(side, out_keep, out_got)
        elif len(att.moves) == 2:
            live = [c for c in live if c is not vec]
            dx_got, block_out = att.go(live, (dx_got, block_out))
        elif len(att.moves) == 1:
            up_sum, down_sum = spread_feed(info, pieces[f0] + pieces[f1])
            up_sum, dx_got = tie(up_sum, dx_got)
            input_grad = join(side, dx_keep, dx_got.astype(F32))
            up_sum, down_sum, block_out, input_grad = att.go(
                live, (up_sum, down_sum, block_out, input_grad)
            )
        else:
            att.go(live)
        for c in live:
            c.go()
            if c in waits and c.done:
                pieces[c] = c.value + (swap(c.value[1], "core"),)
    while not vec.done:
        vec.go()

    common = [vec.value[i * width : (i + 1) * width] for i in range(6)]
    split = vec.value[6 * width :]
    att.go()
    q_sum, k_sum, v_sum, o_sum = spread(info, *att.value)
    return (
        block_out,
        input_grad,
        common[0],
        common[1],
        q_sum,
        split[:heads],
        k_sum,
        v_sum,
        split[heads : 2 * heads],
        o_sum,
        common[4],
        common[2],
        common[3],
        up_sum,
        split[2 * heads :],
        down_sum,
        common[5],
    )


def solution(mesh):
    n_dp, n_mp = mesh.shape["dp"], mesh.shape["mp"]
    names = ("rest", "nbr", "core", "mp")
    inner = Mesh(mesh.devices.reshape(n_dp // 4, 2, 2, n_mp), names)
    dp = ("rest", "nbr", "core")
    in_specs = (
        P(dp, "mp", None),
        P(dp),
        P(dp, "mp", None),
        P(),
        P(),
        P(None, "mp"),
        P("mp"),
        P(None, "mp"),
        P(None, "mp"),
        P("mp"),
        P("mp", None),
        P(),
        P(),
        P(),
        P(None, "mp"),
        P("mp"),
        P("mp", None),
        P(),
    )
    out_specs = (
        P(dp, "mp", None),
        P(dp, "mp", None),
        P(),
        P(),
        P(None, "mp"),
        P("mp"),
        P(None, "mp"),
        P(None, "mp"),
        P("mp"),
        P("mp", None),
        P(),
        P(),
        P(),
        P(None, "mp"),
        P("mp"),
        P("mp", None),
        P(),
    )
    return jax.shard_map(
        functools.partial(on_device, dict(inner.shape)),
        mesh=inner,
        in_specs=in_specs,
        out_specs=out_specs,
        check_vma=False,
    )
```

```python
import functools
import math

import jax
import jax.numpy as jnp
from jax import lax
from jax.experimental import pallas as pl
from jax.experimental.pallas import tpu as pltpu
from jax.sharding import Mesh
from jax.sharding import PartitionSpec as P

HEAD_DIM = 64
PAIR = 2 * HEAD_DIM
EPS = 1e-12
FILL = -1000000000.0
SCALE = 1.0 / math.sqrt(HEAD_DIM)
LOG2E = math.log2(math.e)
F32 = jnp.float32
BF16 = jnp.bfloat16
NT = (((1,), (1,)), ((), ()))
NN = (((1,), (0,)), ((), ()))
TN = (((0,), (0,)), ((), ()))


def mm(a, b, dims=NN):
    return lax.dot_general(a, b, dims, preferred_element_type=F32)


def key_mask(info, row, shape):
    seq = shape[0]
    slot = lax.broadcasted_iota(jnp.int32, shape, 0) + info[0]
    position = jnp.where(slot >= seq, slot - seq, slot)
    return position < info[3 + row]


def head_lanes(value, head):
    lane = lax.broadcasted_iota(jnp.int32, value.shape, 1)
    keep = lane < HEAD_DIM if head == 0 else lane >= HEAD_DIM
    return jnp.where(keep, value, jnp.zeros_like(value))


def attend_kernel(info, q_ref, k_ref, v_ref, o_ref, lse_ref):
    row = pl.program_id(0)
    q, k, v = q_ref[0], k_ref[0], v_ref[0]
    valid = key_mask(info, row, (k.shape[0], q.shape[0]))
    v_t = v.T
    seq = k.shape[0]
    both = mm(jnp.concatenate([head_lanes(k, 0), head_lanes(k, 1)], axis=0), q, NT)
    parts = []
    for head in range(2):
        scores = both[head * seq : (head + 1) * seq] * (SCALE * LOG2E)
        scores = jnp.where(valid, scores, FILL * LOG2E)
        top = jnp.max(scores, axis=0, keepdims=True)
        weight = jnp.exp2(scores - top)
        total = jnp.sum(weight, axis=0, keepdims=True)
        lse_ref[0, 0, head : head + 1, :] = top + jnp.log2(total)
        probs = (weight * (1.0 / total)).astype(BF16)
        parts.append(mm(v_t[head * HEAD_DIM : (head + 1) * HEAD_DIM], probs))
    o_ref[0] = jnp.concatenate(parts, axis=0).T.astype(BF16)


def attend_back_kernel(info, q_ref, k_ref, v_ref, do_ref, lse_ref, d_ref, sum_ref):
    row = pl.program_id(0)
    pair = pl.program_id(1)
    n_pairs = pl.num_programs(1)
    q, k, v, do = q_ref[0], k_ref[0], v_ref[0], do_ref[0]
    valid = key_mask(info, row, (k.shape[0], q.shape[0]))
    k_t = k.T
    dq_t, dk, dv = [], [], []
    for head in range(2):
        scores = mm(head_lanes(k, head), q, NT) * (SCALE * LOG2E)
        scores = jnp.where(valid, scores, FILL * LOG2E)
        probs = jnp.exp2(scores - lse_ref[0, 0, head : head + 1, :])
        dv.append(mm(probs.astype(BF16), do))
        dprobs = mm(head_lanes(v, head), do, NT)
        delta = jnp.sum(probs * dprobs, axis=0, keepdims=True)
        dscores = (probs * (dprobs - delta)).astype(BF16)
        dk.append(mm(dscores, q))
        dq_t.append(mm(k_t[head * HEAD_DIM : (head + 1) * HEAD_DIM], dscores))
    first = lax.broadcasted_iota(jnp.int32, dv[0].shape, 1) < HEAD_DIM
    dq = jnp.concatenate(dq_t, axis=0).T * SCALE

    def put(slot, value):
        start = pl.multiple_of((slot * n_pairs + pair) * PAIR, PAIR)
        low = value.astype(BF16)
        d_ref[0, :, pl.ds(start, PAIR)] = low
        sum_ref[0, :, pl.ds(start, PAIR)] = jnp.sum(low.astype(F32), axis=0, keepdims=True)

    put(0, dq)
    put(1, jnp.where(first, dk[0], dk[1]) * SCALE)
    put(2, jnp.where(first, dv[0], dv[1]))


def attend_specs(seq, n_pairs):
    return [
        pl.BlockSpec((1, seq, PAIR), lambda r, p, info: (r, 0, p)),
        pl.BlockSpec((1, seq, PAIR), lambda r, p, info: (r, 0, n_pairs + p)),
        pl.BlockSpec((1, seq, PAIR), lambda r, p, info: (r, 0, 2 * n_pairs + p)),
    ]


MIB = 1024 * 1024
VMEM_MIB = {"enter": 50, "middle": 50, "middle_back": 50, "leave": 50}


def cost(micros):
    return pl.CostEstimate(flops=int(micros * 1.15e9), bytes_accessed=1000, transcendentals=0)


def attend(info, qkv):
    rows, seq, width = qkv.shape
    n_pairs = width // (3 * PAIR)
    return pl.pallas_call(
        attend_kernel,
        out_shape=(
            jax.ShapeDtypeStruct((rows, seq, n_pairs * PAIR), BF16),
            jax.ShapeDtypeStruct((rows, n_pairs, 2, seq), F32),
        ),
        grid_spec=pltpu.PrefetchScalarGridSpec(
            num_scalar_prefetch=1,
            grid=(rows, n_pairs),
            in_specs=attend_specs(seq, n_pairs),
            out_specs=(
                pl.BlockSpec((1, seq, PAIR), lambda r, p, info: (r, 0, p)),
                pl.BlockSpec((1, 1, 2, seq), lambda r, p, info: (r, p, 0, 0)),
            ),
        ),
        compiler_params=pltpu.CompilerParams(vmem_limit_bytes=20 * MIB),
        cost_estimate=cost(10),
        name="attend",
    )(info, qkv, qkv, qkv)


def attend_back(info, qkv, grad_mixed, lse):
    rows, seq, width = qkv.shape
    n_pairs = width // (3 * PAIR)
    return pl.pallas_call(
        attend_back_kernel,
        out_shape=(
            jax.ShapeDtypeStruct((rows, seq, width), BF16),
            jax.ShapeDtypeStruct((rows, 1, width), F32),
        ),
        grid_spec=pltpu.PrefetchScalarGridSpec(
            num_scalar_prefetch=1,
            grid=(rows, n_pairs),
            in_specs=attend_specs(seq, n_pairs)
            + [
                pl.BlockSpec((1, seq, PAIR), lambda r, p, info: (r, 0, p)),
                pl.BlockSpec((1, 1, 2, seq), lambda r, p, info: (r, p, 0, 0)),
            ],
            out_specs=(
                pl.BlockSpec((1, seq, width), lambda r, p, info: (r, 0, 0)),
                pl.BlockSpec((1, 1, width), lambda r, p, info: (r, 0, 0)),
            ),
        ),
        compiler_params=pltpu.CompilerParams(vmem_limit_bytes=24 * MIB),
        cost_estimate=cost(13),
        name="attend_back",
    )(info, qkv, qkv, qkv, grad_mixed, lse)


def feed_kernel(first, own, info, *refs):
    refs = list(refs)
    nm, wa0, wa1, wb0, wb1, bu = refs[:6]
    refs = refs[6:]
    if own:
        wu, wd = refs[:2]
        refs = refs[2:]
    nt_hbm, up_hbm = refs[:2]
    refs = refs[2:]
    if not first:
        y_hbm, gnm_hbm = refs[:2]
        refs = refs[2:]
    y_out, gnm_out, keep, send, gbu, nt, up, y, gnm, sems = refs
    step = pl.program_id(0)
    last = pl.num_programs(0) - 1
    core = info[1]
    copies = [
        pltpu.make_async_copy(up_hbm, up, sems.at[0]),
        pltpu.make_async_copy(nt_hbm, nt, sems.at[1]),
    ]
    if not first:
        copies += [
            pltpu.make_async_copy(y_hbm, y, sems.at[2]),
            pltpu.make_async_copy(gnm_hbm, gnm, sems.at[3]),
        ]
    out_y = pltpu.make_async_copy(y, y_out, sems.at[4])
    out_gnm = pltpu.make_async_copy(gnm, gnm_out, sems.at[5])

    @pl.when(step == 0)
    def _():
        for copy in copies:
            copy.start()
        for copy in copies:
            copy.wait()

    def whole(low, high):
        ends = low[...], high[...]
        if not own:
            flip = info[info.shape[0] - 1] != 0
            ends = jnp.where(flip, *ends[::-1]), jnp.where(flip, *ends)
        return jnp.concatenate(ends, axis=0)

    piece_a, piece_b = whole(wa0, wa1), whole(wb0, wb1)
    w_up = jnp.where(core == 0, piece_a, piece_b)
    w_down = jnp.where(core == 0, piece_b, piece_a)
    if own:
        w_up = jnp.where(step == 0, w_up, wu[...])
        w_down = jnp.where(step == 0, w_down, wd[...])
    h = mm(nm[...], w_up) + bu[...]
    cdf = 0.5 * (1.0 + lax.erf(h * (1.0 / math.sqrt(2.0))))
    active = (h * cdf).astype(BF16)
    slope = cdf + h * jnp.exp(-0.5 * h * h) * (1.0 / math.sqrt(2.0 * math.pi))
    grad_hidden = (mm(up[...], w_down, NT) * slope).astype(BF16)
    gbu[...] = jnp.sum(grad_hidden.astype(F32), axis=0, keepdims=True)
    if first:
        y[...] = mm(active, w_down)
        gnm[...] = mm(grad_hidden, w_up, NT)
    else:
        y[...] += mm(active, w_down)
        gnm[...] += mm(grad_hidden, w_up, NT)
    grad_down = mm(active, up[...], TN).astype(BF16)

    @pl.when(step == last)
    def _():
        out_y.start()
        out_gnm.start()

    grad_up = mm(nt[...], grad_hidden).astype(BF16)
    keep[0] = jnp.where(core == 0, grad_up, grad_down)
    send[0] = jnp.where(core == 0, grad_down, grad_up)

    @pl.when(step == last)
    def _():
        out_y.wait()
        out_gnm.wait()


def feed(info, nm, nt, up, wa, wb, bu, own=None, sums=None):
    tokens, width = nm.shape
    count = bu.shape[1] // width
    first = sums is None
    once = lambda shape: pl.BlockSpec(shape, lambda f, info: (0, 0), pipeline_mode=pl.Buffered(1))
    place = pl.BlockSpec(memory_space=pl.ANY)
    row = pl.BlockSpec((1, width), lambda f, info: (0, f))
    in_specs = [once((tokens, width))] + [once(wa[0].shape)] * 4 + [row]
    args = [nm, *wa, *wb, bu]
    if own is not None:
        in_specs += [
            pl.BlockSpec((width, width), lambda f, info: (0, jnp.maximum(f - 1, 0))),
            pl.BlockSpec((width, width), lambda f, info: (jnp.maximum(f - 1, 0), 0)),
        ]
        args += list(own)
    in_specs += [place] * 2
    args += [nt, up]
    if not first:
        in_specs += [place] * 2
        args += list(sums)
    grads = pl.BlockSpec((1, width, width), lambda f, info: (f, 0, 0))
    return pl.pallas_call(
        functools.partial(feed_kernel, first, own is not None),
        out_shape=(
            shaped(tokens, width, dtype=F32),
            shaped(tokens, width, dtype=F32),
            shaped(count, width, width),
            shaped(count, width, width),
            shaped(1, count * width, dtype=F32),
        ),
        grid_spec=pltpu.PrefetchScalarGridSpec(
            num_scalar_prefetch=1,
            grid=(count,),
            in_specs=in_specs,
            out_specs=(place, place, grads, grads, row),
            scratch_shapes=[
                pltpu.VMEM((width, tokens), BF16),
                pltpu.VMEM((tokens, width), BF16),
                pltpu.VMEM((tokens, width), F32),
                pltpu.VMEM((tokens, width), F32),
                pltpu.SemaphoreType.DMA((6,)),
            ],
        ),
        compiler_params=pltpu.CompilerParams(vmem_limit_bytes=46 * MIB),
        cost_estimate=cost(12 * count),
        name="feed_own" if own is not None else "feed_other",
    )(info, *args)


def norm(values):
    average = jnp.mean(values, axis=-1, keepdims=True)
    centred = values - average
    inv = lax.rsqrt(jnp.mean(centred * centred, axis=-1, keepdims=True) + EPS)
    return centred * inv, inv


def norm_back(grad, unit, inv, gain):
    scaled = grad * gain
    return inv * (
        scaled
        - jnp.mean(scaled, axis=-1, keepdims=True)
        - unit * jnp.mean(scaled * unit, axis=-1, keepdims=True)
    )


def stack(first, second):
    return jnp.concatenate([first, second], axis=0)


def row_grid(kernel, name, micros, rows, in_specs, out_shape, out_specs, args):
    return pl.pallas_call(
        kernel,
        out_shape=out_shape,
        grid_spec=pltpu.PrefetchScalarGridSpec(
            num_scalar_prefetch=1, grid=(rows,), in_specs=in_specs, out_specs=out_specs
        ),
        compiler_params=pltpu.CompilerParams(vmem_limit_bytes=VMEM_MIB.get(name, 28) * MIB),
        cost_estimate=cost(micros),
        name=name,
    )(*args)


def fixed(shape):
    return pl.BlockSpec(shape, lambda r, info: (0,) * len(shape))


def const(shape):
    return pl.BlockSpec(
        shape, lambda r, info: (0,) * len(shape), pipeline_mode=pl.Buffered(1)
    )


def per_row(*shape):
    return pl.BlockSpec((1,) + shape, lambda r, info: (r,) + (0,) * len(shape))


def kept_row(*shape):
    return pl.BlockSpec((1,) + shape, lambda r, info: (info[2] + r,) + (0,) * len(shape))


def shaped(*shape, dtype=BF16):
    return jax.ShapeDtypeStruct(shape, dtype)


def enter_kernel(info, tok, got, wq, wk, wv, bias, gain, shift, x_out, n_out, nt_out, qkv):
    heads = wq.shape[1]
    x = stack(tok[0], got[0])
    x_out[0] = x
    unit, _ = norm(x.astype(F32))
    normed = (unit * gain[...] + shift[...]).astype(BF16)
    n_out[0] = normed
    nt_out[...] = normed.T
    qkv[0, :, :heads] = (mm(normed, wq[...]) + bias[:, :heads]).astype(BF16)
    qkv[0, :, heads : 2 * heads] = mm(normed, wk[...]).astype(BF16)
    qkv[0, :, 2 * heads :] = (mm(normed, wv[...]) + bias[:, heads : 2 * heads]).astype(BF16)


def enter(info, tokens, got, wq, wk, wv, bias, gain, shift):
    rows, half, width = got.shape
    seq, heads = 2 * half, wq.shape[1]
    return row_grid(
        enter_kernel,
        "enter",
        0,
        rows,
        [kept_row(half, width), per_row(half, width)]
        + [const(wq.shape)] * 3
        + [const(bias.shape)]
        + [const((1, width))] * 2,
        (
            shaped(rows, seq, width),
            shaped(rows, seq, width),
            shaped(width, rows * seq),
            shaped(rows, seq, 3 * heads),
        ),
        (
            per_row(seq, width),
            per_row(seq, width),
            pl.BlockSpec((width, seq), lambda r, info: (0, r)),
            per_row(seq, 3 * heads),
        ),
        (info, tokens, got, wq, wk, wv, bias, gain[None], shift[None]),
    )


def other_heads_kernel(info, n, p0, p1, p2, p3, bias, qkv, w):
    heads = w.shape[1] // 3

    @pl.when(pl.program_id(0) == 0)
    def _():
        nbr, core = info[3 + pl.num_programs(0)], info[1]
        size = p0.shape[0]
        for index, piece in enumerate((p0, p1, p2, p3)):
            row = 1 - nbr if index >= 2 else nbr
            col = 1 - core if index % 2 else core
            start = pl.multiple_of((2 * row + col) * size, size)
            w[pl.ds(start, size), :] = piece[...]

    full = jnp.concatenate(
        [bias[:, :heads], jnp.zeros((1, heads), F32), bias[:, heads : 2 * heads]], axis=1
    )
    qkv[0] = (mm(n[0], w[...]) + full).astype(BF16)


def other_heads(info, n, pieces, bias):
    rows, seq, width = n.shape
    size, wide = pieces[0].shape
    return row_grid(
        other_heads_kernel,
        "other_heads",
        0,
        rows,
        [per_row(seq, width)] + [const((size, wide))] * 4 + [const(bias.shape)],
        (shaped(rows, seq, wide), shaped(width, wide)),
        (per_row(seq, wide), fixed((width, wide))),
        (info, n, *pieces, bias),
    )


def middle_kernel(
    info, x, m_own, m_oth, w_own, w_mine, w_cross, b_out, gain, shift, grad, got, res, nm, nm_t, up, w_oth
):
    @pl.when(pl.program_id(0) == 0)
    def _():
        size = w_mine.shape[0]
        w_oth[pl.ds(pl.multiple_of(info[1] * size, size), size), :] = w_mine[...]
        w_oth[pl.ds(pl.multiple_of((1 - info[1]) * size, size), size), :] = w_cross[...]

    attended = mm(m_own[0], w_own[...]) + mm(m_oth[0], w_oth[...])
    residual = x[0].astype(F32) + attended + b_out[...]
    res[0] = residual
    unit, _ = norm(residual)
    normed = (unit * gain[...] + shift[...]).astype(BF16)
    nm[0] = normed
    nm_t[...] = normed.T
    up[0] = stack(grad[0], got[0])


def middle(info, x, m_own, m_oth, w_own, w_mine, w_cross, b_out, gain, shift, grad, got):
    rows, seq, width = x.shape
    heads = w_own.shape[0]
    return row_grid(
        middle_kernel,
        "middle",
        0,
        rows,
        [per_row(seq, width), per_row(seq, heads), per_row(seq, heads)]
        + [const(w_own.shape), const(w_mine.shape), const(w_mine.shape)]
        + [const((1, width))] * 3
        + [kept_row(seq // 2, width), per_row(seq // 2, width)],
        (
            shaped(rows, seq, width, dtype=F32),
            shaped(rows, seq, width),
            shaped(width, rows * seq),
            shaped(rows, seq, width),
            shaped(heads, width),
        ),
        (
            per_row(seq, width),
            per_row(seq, width),
            pl.BlockSpec((width, seq), lambda r, info: (0, r)),
            per_row(seq, width),
            fixed((heads, width)),
        ),
        (info, x, m_own, m_oth, w_own, w_mine, w_cross, b_out[None], gain[None], shift[None], grad, got),
    )


def middle_back_kernel(
    info, gnm, res, y, up, gain, b_down, w_own, w_oth, keep, send, gres, glow_t, gm_own, gm_oth, sums
):
    half = keep.shape[1]
    residual, grad, upstream = res[0], gnm[0], up[0].astype(F32)
    out = (residual + y[0] + b_down[...]).astype(BF16)
    keep[0] = out[:half]
    send[0] = out[half:]
    unit, inv = norm(residual)
    total = upstream + norm_back(grad, unit, inv, gain[...])
    gres[0] = total
    low = total.astype(BF16)
    glow_t[...] = low.T
    gm_own[0] = mm(low, w_own[...], NT).astype(BF16)
    gm_oth[0] = mm(low, w_oth[...], NT).astype(BF16)

    @pl.when(pl.program_id(0) == 0)
    def _():
        sums[...] = jnp.zeros_like(sums)

    for index, value in enumerate((grad * unit, grad, total, upstream)):
        sums[index : index + 1, :] += jnp.sum(value, axis=0, keepdims=True)


def middle_back(info, gnm, res, y, up, gain, b_down, w_own, w_oth):
    rows, seq, width = res.shape
    heads = w_own.shape[0]
    row = per_row(seq, width)
    half = per_row(seq // 2, width)
    return row_grid(
        middle_back_kernel,
        "middle_back",
        0,
        rows,
        [row] * 4 + [const((1, width))] * 2 + [const((heads, width))] * 2,
        (
            shaped(rows, seq // 2, width),
            shaped(rows, seq // 2, width),
            shaped(rows, seq, width, dtype=F32),
            shaped(width, rows * seq),
            shaped(rows, seq, heads),
            shaped(rows, seq, heads),
            shaped(8, width, dtype=F32),
        ),
        (
            half,
            half,
            row,
            pl.BlockSpec((width, seq), lambda r, info: (0, r)),
            per_row(seq, heads),
            per_row(seq, heads),
            fixed((8, width)),
        ),
        (info, gnm, res, y, up, gain[None], b_down[None], w_own, w_oth),
    )


def weights_kernel(info, nt, d, glow_t, mixed, keep, send):
    heads = mixed.shape[1]
    g = mm(nt[...], d[...]).astype(BF16)
    o = mm(glow_t[...], mixed[...]).astype(BF16)
    cut = 2 * heads

    @pl.when(info[1] == 0)
    def _():
        keep[...] = g[:, :cut]
        send[:, :heads] = g[:, cut:]
        send[:, heads:] = o

    @pl.when(info[1] != 0)
    def _():
        send[...] = g[:, :cut]
        keep[:, :heads] = g[:, cut:]
        keep[:, heads:] = o


def weights(info, nt, d, glow_t, mixed, block=256):
    width, tokens = nt.shape
    heads = mixed.shape[1]
    part = pl.BlockSpec((block, tokens), lambda r, info: (r, 0))
    result = pl.BlockSpec((block, 2 * heads), lambda r, info: (r, 0))
    return row_grid(
        weights_kernel,
        "weights",
        0,
        width // block,
        [part, const(d.shape), part, const(mixed.shape)],
        (shaped(width, 2 * heads), shaped(width, 2 * heads)),
        (result, result),
        (info, nt, d, glow_t, mixed),
    )


def leave_kernel(info, d_own, d_oth, wq, wk, wv, w_oth, x, gres, gain, keep, send, sums):
    heads = wq.shape[1]
    half = keep.shape[1]
    grad = (
        mm(d_own[0, :, :heads], wq[...], NT)
        + mm(d_own[0, :, heads : 2 * heads], wk[...], NT)
        + mm(d_own[0, :, 2 * heads :], wv[...], NT)
        + mm(d_oth[0], w_oth[...], NT)
    )
    unit, inv = norm(x[0].astype(F32))
    total = gres[0] + norm_back(grad, unit, inv, gain[...])
    keep[0] = total[:half]
    send[0] = total[half:].astype(BF16)

    @pl.when(pl.program_id(0) == 0)
    def _():
        sums[...] = jnp.zeros_like(sums)

    for index, value in enumerate((grad * unit, grad)):
        sums[index : index + 1, :] += jnp.sum(value, axis=0, keepdims=True)


def leave(info, d_own, d_oth, wq, wk, wv, w_oth, x, gres, gain):
    rows, seq, width = x.shape
    row = per_row(seq, width)
    half = per_row(seq // 2, width)
    wide = per_row(seq, d_own.shape[2])
    return row_grid(
        leave_kernel,
        "leave",
        10,
        rows,
        [wide, wide]
        + [const(wq.shape)] * 3
        + [const(w_oth.shape), row, row, const((1, width))],
        (
            shaped(rows, seq // 2, width, dtype=F32),
            shaped(rows, seq // 2, width),
            shaped(8, width, dtype=F32),
        ),
        (half, half, fixed((8, width))),
        (info, d_own, d_oth, wq, wk, wv, w_oth, x, gres, gain[None]),
    )


def spread_kernel(info, mine, near, cross, both, q, k, v, o):
    heads = q.shape[1]
    here = pl.program_id(0) == info[info.shape[0] - 1]
    own = jnp.where(here, mine[...], near[...]).astype(F32)
    other = jnp.where(here, cross[...], both[...]).astype(F32)

    def write(first, second):
        q[...] = first[:, :heads]
        k[...] = first[:, heads:]
        v[...] = second[:, :heads]
        o[...] = second[:, heads:].T

    @pl.when(info[1] == 0)
    def _():
        write(own, other)

    @pl.when(info[1] != 0)
    def _():
        write(other, own)


def spread(info, *pieces):
    block, both = pieces[0].shape
    heads = both // 2
    plain = pl.BlockSpec((block, heads), lambda n, info: (n, 0))
    return row_grid(
        spread_kernel,
        "spread",
        3,
        2,
        [const((block, both))] * 4,
        (shaped(2 * block, heads, dtype=F32),) * 3 + (shaped(heads, 2 * block, dtype=F32),),
        (plain,) * 3 + (pl.BlockSpec((heads, block), lambda n, info: (0, n)),),
        (info, *pieces),
    )


def spread_feed_kernel(info, *refs):
    nbr, core = info[info.shape[0] - 1], info[1]
    up, down = refs[-2:]
    here = pl.program_id(1) == nbr
    for chunk in range(2):
        mine, near, cross, both = refs[4 * chunk : 4 * chunk + 4]

        @pl.when(pl.program_id(0) == chunk)
        def _():
            own = jnp.where(here, mine[...], near[...]).astype(F32)
            other = jnp.where(here, cross[...], both[...]).astype(F32)
            up[...] = jnp.where(core == 0, own, other)
            down[...] = jnp.where(core == 0, other, own)


def spread_feed(info, pieces):
    block, width = pieces[0].shape
    once = pl.BlockSpec((block, width), lambda k, n, info: (0, 0), pipeline_mode=pl.Buffered(1))
    return pl.pallas_call(
        spread_feed_kernel,
        out_shape=(shaped(width, 2 * width, dtype=F32), shaped(2 * width, width, dtype=F32)),
        grid_spec=pltpu.PrefetchScalarGridSpec(
            num_scalar_prefetch=1,
            grid=(2, 2),
            in_specs=[once] * 8,
            out_specs=(
                pl.BlockSpec((block, width), lambda k, n, info: (n, k)),
                pl.BlockSpec((block, width), lambda k, n, info: (2 * k + n, 0)),
            ),
        ),
        compiler_params=pltpu.CompilerParams(vmem_limit_bytes=24 * MIB),
        cost_estimate=cost(5),
        name="spread_feed",
    )(info, *pieces)


def swap(value, axis):
    return lax.ppermute(value, axis, [(0, 1), (1, 0)])


def part(value, index, count):
    size = value.shape[0] // count
    return lax.dynamic_slice_in_dim(value, index * size, size, 0)


class Rows:
    def __init__(self, array, matrix=None, start=0, size=None):
        self.array, self.matrix, self.start = array, matrix, start
        self.size = array.shape[-2] if size is None else size

    def half(self, index):
        size = self.size // 2
        return Rows(self.array, self.matrix, self.start + index * size, size)

    def read(self):
        if self.matrix is None:
            return lax.dynamic_slice_in_dim(self.array, self.start, self.size, 0)
        shape = (1, self.size, self.array.shape[-1])
        return lax.dynamic_slice(self.array, (self.matrix, self.start, 0), shape)[0]


class Either:
    def __init__(self, index, first, second):
        self.index, self.first, self.second = index, first, second

    def half(self, index):
        return Either(self.index, self.first.half(index), self.second.half(index))

    def read(self):
        return jnp.where(self.index == 0, self.first.read(), self.second.read())


class Stacked:
    def __init__(self, upper, lower):
        self.upper, self.lower = Rows(upper), Rows(lower)

    def half(self, index):
        return Either(index, self.upper, self.lower)


def total_low(addends):
    return add_low(*[addend.read() for addend in addends])


def join(index, mine, other):
    return jnp.where(index == 0, jnp.concatenate([mine, other]), jnp.concatenate([other, mine]))


def tie(*values):
    return lax.optimization_barrier(values)


def add_low(*addends):
    return sum(addend.astype(F32) for addend in addends).astype(BF16)


def ladder(sizes):
    steps = [("nbr", lax.axis_index("nbr"), [(0, 1), (1, 0)])]
    bit = 1
    while bit < sizes["rest"]:
        index = (lax.axis_index("rest") // bit) % 2
        steps.append(("rest", index, [(i, i ^ bit) for i in range(sizes["rest"])]))
        bit *= 2
    return steps


def halve(step):
    axis, index, perm = step

    def prepare(addends):
        sent = total_low([a.half(1 - index) for a in addends])
        return sent, tuple(a.half(index) for a in addends)

    return (
        prepare,
        lambda sent: (lax.ppermute(sent, axis, perm),),
        lambda kept, got: kept + (Rows(got),),
    )


def double(step):
    axis, index, perm = step

    def prepare(value):
        if isinstance(value, tuple):
            value = total_low(value)
        return value, value

    return prepare, lambda sent: (lax.ppermute(sent, axis, perm),), functools.partial(join, index)


def twice(value):
    return value, value


def to_pair(axis):
    return (
        lambda three: (three[1], three),
        lambda sent: (swap(sent, axis),),
        lambda three, got: three + (got,),
    )


def to_three():
    return (
        twice,
        lambda sent: (swap(sent, "nbr"), swap(sent, "core")),
        lambda value, near, cross: (value, near, cross),
    )


def add_over(axis, perm):
    return twice, lambda sent: (lax.ppermute(sent, axis, perm),), jnp.add


class Chain:
    def __init__(self, value, moves, behind=()):
        self.value, self.finish, self.moves, self.flying = value, None, list(moves), ()
        self.go(behind)

    def go(self, behind=(), values=()):
        if self.finish is not None:
            self.value, self.finish = self.finish(self.value, *self.flying), None
            self.flying = ()
        if self.moves:
            prepare, launch, self.finish = self.moves.pop(0)
            sent, self.value = prepare(self.value)
            if behind or values:
                sent, values = meet(behind, sent, list(values))
            self.flying = launch(sent)
        return values

    @property
    def done(self):
        return self.finish is None


def meet(chains, *values):
    flying, tied = lax.optimization_barrier(([c.flying for c in chains], list(values)))
    for c, transfers in zip(chains, flying):
        c.flying = tuple(transfers)
    return tied[0] if len(tied) == 1 else tied


def on_device(
    sizes,
    tokens,
    lengths,
    out_grad,
    ln1_gain,
    ln1_shift,
    w_query,
    b_query,
    w_key,
    w_value,
    b_value,
    w_out,
    b_out,
    ln2_gain,
    ln2_shift,
    w_up,
    b_up,
    w_down,
    b_down,
):
    side = lax.axis_index("mp")
    core = lax.axis_index("core")
    nbr = lax.axis_index("nbr")
    rows_dev, half, width = tokens.shape
    rows = rows_dev // 2
    seq = 2 * half
    total = rows * seq
    heads = w_query.shape[1]
    units = w_up.shape[1] // 2
    steps = ladder(sizes)

    def by_core(first, second):
        return jnp.where(core == 0, first, second)

    def flat(value):
        return value.reshape(total, value.shape[-1])

    info = jnp.concatenate(
        [jnp.stack([side * half, core, side * rows]), part(lengths, side, 2), nbr[None]]
    ).astype(jnp.int32)

    quarter = 2 * nbr + core
    w_send = jnp.concatenate([part(w, quarter, 4) for w in (w_query, w_key, w_value)], axis=1)
    t_send = part(tokens, 1 - side, 2)
    got_tokens = swap(t_send, "mp")
    w_mine = swap(w_send, "mp")
    bias_own = jnp.concatenate([b_query, b_value, b_up])
    bias_oth = swap(bias_own, "mp")
    up_halves = [w_up[:, :units], w_up[:, units:]]
    down_halves = [w_down[:units], w_down[units:]]
    f_send0 = part(by_core(up_halves[0], down_halves[0]), nbr, 2)
    f_whole1 = by_core(up_halves[1], down_halves[1])
    f_send1, f_send2 = f_whole1[: units // 2], f_whole1[units // 2 :]
    g_send = part(out_grad, 1 - side, 2)
    o_send = part(w_out, core, 2)
    got_tokens, f_send0, f_send1, f_send2, g_send, o_send = tie(
        got_tokens, f_send0, f_send1, f_send2, g_send, o_send
    )
    x, normed_in, nt, qkv_own = enter(
        info, tokens, got_tokens, w_query, w_key, w_value, bias_own[None], ln1_gain, ln1_shift
    )
    f_mine0 = swap(f_send0, "mp")
    o_mine = swap(o_send, "mp")
    qkv_own, w_mine, bias_oth = tie(qkv_own, w_mine, bias_oth)
    w_near = swap(w_mine, "nbr")
    mixed_own, lse_own = attend(info, qkv_own)
    mixed_own, w_near, g_send = tie(mixed_own, w_near, g_send)
    pieces = (w_mine, swap(w_mine, "core"), w_near, swap(w_near, "core"))
    got_grad = swap(g_send, "mp")
    qkv_oth, wqkv_oth = other_heads(info, normed_in, pieces, bias_oth[None])
    qkv_oth, f_mine0, f_send1, o_mine = tie(qkv_oth, f_mine0, f_send1, o_mine)
    f_near0 = swap(f_mine0, "nbr")
    f_mine1 = swap(f_send1, "mp")
    mixed_oth, lse_oth = attend(info, qkv_oth)
    mixed_oth, f_near0, got_grad = tie(mixed_oth, f_near0, got_grad)
    f_cross0 = swap(f_mine0, "core"), swap(f_near0, "core")
    residual, nm, nm_t, up, wout_oth = middle(
        info, x, mixed_own, mixed_oth, w_out, o_mine, swap(o_mine, "core"),
        b_out, ln2_gain, ln2_shift, out_grad, got_grad,
    )
    nm, f_mine1, f_send2 = tie(nm, f_mine1, f_send2)
    f_mine2 = swap(f_send2, "mp")
    bup_own = bias_own[2 * heads :][None]
    bup_oth = bias_oth[2 * heads :][None]
    args = (info, flat(nm), nm_t, flat(up))
    y, gnm, f_keep0, f_give0, gbup0 = feed(
        *args, (f_mine0, f_near0), f_cross0, bup_oth[:, :units]
    )
    f_cross1 = swap(f_mine1, "core")
    y, f_give0, f_mine2, f_cross1 = tie(y, f_give0[0], f_mine2, f_cross1)
    f_swap0, f_cross2 = swap(f_give0, "core"), swap(f_mine2, "core")
    y, f_oth0, f_cross2 = tie(y, add_low(f_keep0[0], f_swap0), f_cross2)
    f_got0 = swap(f_oth0, "mp")
    bup_rest = jnp.concatenate([bup_oth[:, units:], bup_own], axis=1)
    y, gnm, f_keep, f_give, gbup_rest = feed(
        *args, (f_mine1, f_mine2), (f_cross1, f_cross2), bup_rest, own=(w_up, w_down), sums=(y, gnm)
    )
    gbup1, gbup_own = gbup_rest[:, :units], gbup_rest[:, units:]
    gnm, f_give, f_got0 = tie(gnm, f_give, f_got0)
    f_swap = swap(f_give, "core")
    out_keep, out_send, grad_res, glow_t, gm_own, gm_oth, mid_sums = middle_back(
        info, gnm.reshape(rows, seq, width), residual, y.reshape(rows, seq, width), up,
        ln2_gain, b_down, w_out, wout_oth,
    )
    gm_oth, f_swap = tie(gm_oth, f_swap)
    f_got1 = swap(add_low(f_keep[0], f_swap[0]), "mp")
    halving = [halve(step) for step in steps]
    doubling = [double(step) for step in reversed(steps)]
    feed_moves = halving + doubling[:-1] + [to_three()]
    att_moves = feed_moves + [to_pair("core")]
    f0 = Chain((Rows(f_keep, 1), Rows(f_swap, 1), Rows(f_got0)), feed_moves)
    d_oth, bias_sum_oth = attend_back(info, qkv_oth, gm_oth, lse_oth)
    d_oth = meet([f0], d_oth)
    f0.go()
    a_keep, a_give = weights(info, nt, flat(d_oth), glow_t, flat(mixed_oth))
    a_give, f_got1 = meet([f0], a_give, f_got1)
    f1 = Chain((Rows(f_keep, 2), Rows(f_swap, 2), Rows(f_got1)), feed_moves)
    gm_own, a_oth = tie(gm_own, add_low(a_keep, swap(a_give, "core")))
    a_got0 = swap(a_oth[: width // 2], "mp")
    f0.go()
    d_own, bias_sum_own = attend_back(info, qkv_own, gm_own, lse_own)
    d_own, a_got0, a_last = meet([f0, f1], d_own, a_got0, a_oth[width // 2 :])
    a_got1 = swap(a_last, "mp")
    f1.go()
    f0.go()
    a_keep, a_give = weights(info, nt, flat(d_own), glow_t, flat(mixed_own))
    a_give, a_got1 = meet([f0, f1], a_give, a_got1)
    a_swap = swap(a_give, "core")
    d_own, a_swap = tie(d_own, a_swap)
    att = Chain((Rows(a_keep), Rows(a_swap), Stacked(a_got0, a_got1)), att_moves)
    f1.go()
    f0.go()
    out_got = swap(out_send, "mp")
    dx_keep, dx_send, end_sums = leave(
        info, d_own, d_oth, w_query, w_key, w_value, wqkv_oth, x, grad_res, ln1_gain
    )
    dx_send, end_sums = att.go((f0, f1), (dx_send, end_sums))
    f1.go()
    f0.go()

    def bias_sums(d, gbup):
        sums = jnp.sum(d, axis=(0, 1))
        return [sums[:heads], sums[2 * heads :]] + [g[0] for g in gbup]

    def small_sums(end_sums):
        shared = [end_sums[0], end_sums[1]] + [mid_sums[i] for i in range(4)]
        mine = jnp.concatenate(shared + bias_sums(bias_sum_own, [gbup_own]))
        sent = jnp.concatenate(shared + bias_sums(bias_sum_oth, [gbup0, gbup1]))
        parts = swap(mine, "core"), swap(sent, "mp"), cross(sent)
        return [mine] + list(parts)

    def cross(value):
        return lax.ppermute(value, ("core", "mp"), [(i, 3 - i) for i in range(4)])

    terms = small_sums(end_sums)
    waits = {f0: 1, f1: 1}
    pieces = {}
    vec = dx_got = None
    stage = 1
    while att.moves:
        stage += 1
        live = [c for c in (vec,) if c is not None and not c.done]
        for c in (f1, f0):
            if not c.done and (c.moves or waits[c] == 0 or len(att.moves) == 1):
                live.append(c)
            elif not c.done:
                waits[c] -= 1
        if vec is None:
            out_got, terms = att.go(live, (out_got, terms))
            vec = Chain(
                (terms[0] + terms[2]) + (terms[1] + terms[3]),
                [add_over(axis, perm) for axis, _, perm in steps],
            )
        elif dx_got is None:
            (dx_send,) = att.go(live, (dx_send,))
            dx_got = swap(dx_send, "mp")
        elif len(att.moves) == 3:
            (out_got,) = att.go(live, (out_got,))
            block_out = join(side, out_keep, out_got)
        elif len(att.moves) == 2:
            live = [c for c in live if c is not vec]
            dx_got, block_out = att.go(live, (dx_got, block_out))
        elif len(att.moves) == 1:
            up_sum, down_sum = spread_feed(info, pieces[f0] + pieces[f1])
            up_sum, dx_got = tie(up_sum, dx_got)
            input_grad = join(side, dx_keep, dx_got.astype(F32))
            up_sum, down_sum, block_out, input_grad = att.go(
                live, (up_sum, down_sum, block_out, input_grad)
            )
        else:
            att.go(live)
        for c in live:
            c.go()
            if c in waits and c.done:
                pieces[c] = c.value + (swap(c.value[1], "core"),)
    while not vec.done:
        vec.go()

    common = [vec.value[i * width : (i + 1) * width] for i in range(6)]
    split = vec.value[6 * width :]
    att.go()
    q_sum, k_sum, v_sum, o_sum = spread(info, *att.value)
    return (
        block_out,
        input_grad,
        common[0],
        common[1],
        q_sum,
        split[:heads],
        k_sum,
        v_sum,
        split[heads : 2 * heads],
        o_sum,
        common[4],
        common[2],
        common[3],
        up_sum,
        split[2 * heads :],
        down_sum,
        common[5],
    )


def solution(mesh):
    n_dp, n_mp = mesh.shape["dp"], mesh.shape["mp"]
    names = ("rest", "nbr", "core", "mp")
    inner = Mesh(mesh.devices.reshape(n_dp // 4, 2, 2, n_mp), names)
    dp = ("rest", "nbr", "core")
    in_specs = (
        P(dp, "mp", None),
        P(dp),
        P(dp, "mp", None),
        P(),
        P(),
        P(None, "mp"),
        P("mp"),
        P(None, "mp"),
        P(None, "mp"),
        P("mp"),
        P("mp", None),
        P(),
        P(),
        P(),
        P(None, "mp"),
        P("mp"),
        P("mp", None),
        P(),
    )
    out_specs = (
        P(dp, "mp", None),
        P(dp, "mp", None),
        P(),
        P(),
        P(None, "mp"),
        P("mp"),
        P(None, "mp"),
        P(None, "mp"),
        P("mp"),
        P("mp", None),
        P(),
        P(),
        P(),
        P(None, "mp"),
        P("mp"),
        P("mp", None),
        P(),
    )
    return jax.shard_map(
        functools.partial(on_device, dict(inner.shape)),
        mesh=inner,
        in_specs=in_specs,
        out_specs=out_specs,
        check_vma=False,
    )
```

```python
import functools
import math

import jax
import jax.numpy as jnp
from jax import lax
from jax.experimental import pallas as pl
from jax.experimental.pallas import tpu as pltpu
from jax.sharding import Mesh
from jax.sharding import PartitionSpec as P

HEAD_DIM = 64
PAIR = 2 * HEAD_DIM
EPS = 1e-12
FILL = -1000000000.0
SCALE = 1.0 / math.sqrt(HEAD_DIM)
LOG2E = math.log2(math.e)
F32 = jnp.float32
BF16 = jnp.bfloat16
NT = (((1,), (1,)), ((), ()))
NN = (((1,), (0,)), ((), ()))
TN = (((0,), (0,)), ((), ()))


def mm(a, b, dims=NN):
    return lax.dot_general(a, b, dims, preferred_element_type=F32)


def key_mask(info, row, shape):
    seq = shape[0]
    slot = lax.broadcasted_iota(jnp.int32, shape, 0) + info[0]
    position = jnp.where(slot >= seq, slot - seq, slot)
    return position < info[3 + row]


def head_lanes(value, head):
    lane = lax.broadcasted_iota(jnp.int32, value.shape, 1)
    keep = lane < HEAD_DIM if head == 0 else lane >= HEAD_DIM
    return jnp.where(keep, value, jnp.zeros_like(value))


def attend_kernel(info, q_ref, k_ref, v_ref, o_ref, lse_ref):
    row = pl.program_id(0)
    q, k, v = q_ref[0], k_ref[0], v_ref[0]
    valid = key_mask(info, row, (k.shape[0], q.shape[0]))
    v_t = v.T
    seq = k.shape[0]
    both = mm(jnp.concatenate([head_lanes(k, 0), head_lanes(k, 1)], axis=0), q, NT)
    parts = []
    for head in range(2):
        scores = both[head * seq : (head + 1) * seq] * (SCALE * LOG2E)
        scores = jnp.where(valid, scores, FILL * LOG2E)
        top = jnp.max(scores, axis=0, keepdims=True)
        weight = jnp.exp2(scores - top)
        total = jnp.sum(weight, axis=0, keepdims=True)
        lse_ref[0, 0, head : head + 1, :] = top + jnp.log2(total)
        probs = (weight * (1.0 / total)).astype(BF16)
        parts.append(mm(v_t[head * HEAD_DIM : (head + 1) * HEAD_DIM], probs))
    o_ref[0] = jnp.concatenate(parts, axis=0).T.astype(BF16)


def attend_back_kernel(info, q_ref, k_ref, v_ref, do_ref, lse_ref, d_ref, sum_ref):
    row = pl.program_id(0)
    pair = pl.program_id(1)
    n_pairs = pl.num_programs(1)
    q, k, v, do = q_ref[0], k_ref[0], v_ref[0], do_ref[0]
    valid = key_mask(info, row, (k.shape[0], q.shape[0]))
    k_t = k.T
    dq_t, dk, dv = [], [], []
    for head in range(2):
        scores = mm(head_lanes(k, head), q, NT) * (SCALE * LOG2E)
        scores = jnp.where(valid, scores, FILL * LOG2E)
        probs = jnp.exp2(scores - lse_ref[0, 0, head : head + 1, :])
        dv.append(mm(probs.astype(BF16), do))
        dprobs = mm(head_lanes(v, head), do, NT)
        delta = jnp.sum(probs * dprobs, axis=0, keepdims=True)
        dscores = (probs * (dprobs - delta)).astype(BF16)
        dk.append(mm(dscores, q))
        dq_t.append(mm(k_t[head * HEAD_DIM : (head + 1) * HEAD_DIM], dscores))
    first = lax.broadcasted_iota(jnp.int32, dv[0].shape, 1) < HEAD_DIM
    dq = jnp.concatenate(dq_t, axis=0).T * SCALE

    def put(slot, value):
        start = pl.multiple_of((slot * n_pairs + pair) * PAIR, PAIR)
        low = value.astype(BF16)
        d_ref[0, :, pl.ds(start, PAIR)] = low
        sum_ref[0, :, pl.ds(start, PAIR)] = jnp.sum(low.astype(F32), axis=0, keepdims=True)

    put(0, dq)
    put(1, jnp.where(first, dk[0], dk[1]) * SCALE)
    put(2, jnp.where(first, dv[0], dv[1]))


def attend_specs(seq, n_pairs):
    return [
        pl.BlockSpec((1, seq, PAIR), lambda r, p, info: (r, 0, p)),
        pl.BlockSpec((1, seq, PAIR), lambda r, p, info: (r, 0, n_pairs + p)),
        pl.BlockSpec((1, seq, PAIR), lambda r, p, info: (r, 0, 2 * n_pairs + p)),
    ]


MIB = 1024 * 1024
VMEM_MIB = {"enter": 50, "middle": 50, "middle_back": 50, "leave": 50}


def cost(micros):
    return pl.CostEstimate(flops=int(micros * 1.15e9), bytes_accessed=1000, transcendentals=0)


def attend(info, qkv):
    rows, seq, width = qkv.shape
    n_pairs = width // (3 * PAIR)
    return pl.pallas_call(
        attend_kernel,
        out_shape=(
            jax.ShapeDtypeStruct((rows, seq, n_pairs * PAIR), BF16),
            jax.ShapeDtypeStruct((rows, n_pairs, 2, seq), F32),
        ),
        grid_spec=pltpu.PrefetchScalarGridSpec(
            num_scalar_prefetch=1,
            grid=(rows, n_pairs),
            in_specs=attend_specs(seq, n_pairs),
            out_specs=(
                pl.BlockSpec((1, seq, PAIR), lambda r, p, info: (r, 0, p)),
                pl.BlockSpec((1, 1, 2, seq), lambda r, p, info: (r, p, 0, 0)),
            ),
        ),
        compiler_params=pltpu.CompilerParams(vmem_limit_bytes=20 * MIB),
        cost_estimate=cost(10),
        name="attend",
    )(info, qkv, qkv, qkv)


def attend_back(info, qkv, grad_mixed, lse):
    rows, seq, width = qkv.shape
    n_pairs = width // (3 * PAIR)
    return pl.pallas_call(
        attend_back_kernel,
        out_shape=(
            jax.ShapeDtypeStruct((rows, seq, width), BF16),
            jax.ShapeDtypeStruct((rows, 1, width), F32),
        ),
        grid_spec=pltpu.PrefetchScalarGridSpec(
            num_scalar_prefetch=1,
            grid=(rows, n_pairs),
            in_specs=attend_specs(seq, n_pairs)
            + [
                pl.BlockSpec((1, seq, PAIR), lambda r, p, info: (r, 0, p)),
                pl.BlockSpec((1, 1, 2, seq), lambda r, p, info: (r, p, 0, 0)),
            ],
            out_specs=(
                pl.BlockSpec((1, seq, width), lambda r, p, info: (r, 0, 0)),
                pl.BlockSpec((1, 1, width), lambda r, p, info: (r, 0, 0)),
            ),
        ),
        compiler_params=pltpu.CompilerParams(vmem_limit_bytes=24 * MIB),
        cost_estimate=cost(13),
        name="attend_back",
    )(info, qkv, qkv, qkv, grad_mixed, lse)


def feed_kernel(first, own, info, *refs):
    refs = list(refs)
    nm, wa0, wa1, wb0, wb1, bu = refs[:6]
    refs = refs[6:]
    if own:
        wu, wd = refs[:2]
        refs = refs[2:]
    nt_hbm, up_hbm = refs[:2]
    refs = refs[2:]
    if not first:
        y_hbm, gnm_hbm = refs[:2]
        refs = refs[2:]
    y_out, gnm_out, keep, send, gbu, nt, up, y, gnm, sems = refs
    step = pl.program_id(0)
    last = pl.num_programs(0) - 1
    core = info[1]
    copies = [
        pltpu.make_async_copy(up_hbm, up, sems.at[0]),
        pltpu.make_async_copy(nt_hbm, nt, sems.at[1]),
    ]
    if not first:
        copies += [
            pltpu.make_async_copy(y_hbm, y, sems.at[2]),
            pltpu.make_async_copy(gnm_hbm, gnm, sems.at[3]),
        ]
    out_y = pltpu.make_async_copy(y, y_out, sems.at[4])
    out_gnm = pltpu.make_async_copy(gnm, gnm_out, sems.at[5])

    @pl.when(step == 0)
    def _():
        for copy in copies:
            copy.start()
        for copy in copies:
            copy.wait()

    def whole(low, high):
        ends = low[...], high[...]
        if not own:
            flip = info[info.shape[0] - 1] != 0
            ends = jnp.where(flip, *ends[::-1]), jnp.where(flip, *ends)
        return jnp.concatenate(ends, axis=0)

    piece_a, piece_b = whole(wa0, wa1), whole(wb0, wb1)
    w_up = jnp.where(core == 0, piece_a, piece_b)
    w_down = jnp.where(core == 0, piece_b, piece_a)
    if own:
        w_up = jnp.where(step == 0, w_up, wu[...])
        w_down = jnp.where(step == 0, w_down, wd[...])
    h = mm(nm[...], w_up) + bu[...]
    cdf = 0.5 * (1.0 + lax.erf(h * (1.0 / math.sqrt(2.0))))
    active = (h * cdf).astype(BF16)
    slope = cdf + h * jnp.exp(-0.5 * h * h) * (1.0 / math.sqrt(2.0 * math.pi))
    grad_hidden = (mm(up[...], w_down, NT) * slope).astype(BF16)
    gbu[...] = jnp.sum(grad_hidden.astype(F32), axis=0, keepdims=True)
    if first:
        y[...] = mm(active, w_down)
        gnm[...] = mm(grad_hidden, w_up, NT)
    else:
        y[...] += mm(active, w_down)
        gnm[...] += mm(grad_hidden, w_up, NT)
    grad_down = mm(active, up[...], TN).astype(BF16)

    @pl.when(step == last)
    def _():
        out_y.start()
        out_gnm.start()

    grad_up = mm(nt[...], grad_hidden).astype(BF16)
    keep[0] = jnp.where(core == 0, grad_up, grad_down)
    send[0] = jnp.where(core == 0, grad_down, grad_up)

    @pl.when(step == last)
    def _():
        out_y.wait()
        out_gnm.wait()


def feed(info, nm, nt, up, wa, wb, bu, own=None, sums=None):
    tokens, width = nm.shape
    count = bu.shape[1] // width
    first = sums is None
    once = lambda shape: pl.BlockSpec(shape, lambda f, info: (0, 0), pipeline_mode=pl.Buffered(1))
    place = pl.BlockSpec(memory_space=pl.ANY)
    row = pl.BlockSpec((1, width), lambda f, info: (0, f))
    in_specs = [once((tokens, width))] + [once(wa[0].shape)] * 4 + [row]
    args = [nm, *wa, *wb, bu]
    if own is not None:
        in_specs += [
            pl.BlockSpec((width, width), lambda f, info: (0, jnp.maximum(f - 1, 0))),
            pl.BlockSpec((width, width), lambda f, info: (jnp.maximum(f - 1, 0), 0)),
        ]
        args += list(own)
    in_specs += [place] * 2
    args += [nt, up]
    if not first:
        in_specs += [place] * 2
        args += list(sums)
    grads = pl.BlockSpec((1, width, width), lambda f, info: (f, 0, 0))
    return pl.pallas_call(
        functools.partial(feed_kernel, first, own is not None),
        out_shape=(
            shaped(tokens, width, dtype=F32),
            shaped(tokens, width, dtype=F32),
            shaped(count, width, width),
            shaped(count, width, width),
            shaped(1, count * width, dtype=F32),
        ),
        grid_spec=pltpu.PrefetchScalarGridSpec(
            num_scalar_prefetch=1,
            grid=(count,),
            in_specs=in_specs,
            out_specs=(place, place, grads, grads, row),
            scratch_shapes=[
                pltpu.VMEM((width, tokens), BF16),
                pltpu.VMEM((tokens, width), BF16),
                pltpu.VMEM((tokens, width), F32),
                pltpu.VMEM((tokens, width), F32),
                pltpu.SemaphoreType.DMA((6,)),
            ],
        ),
        compiler_params=pltpu.CompilerParams(vmem_limit_bytes=46 * MIB),
        cost_estimate=cost(12 * count),
        name="feed_own" if own is not None else "feed_other",
    )(info, *args)


def norm(values):
    average = jnp.mean(values, axis=-1, keepdims=True)
    centred = values - average
    inv = lax.rsqrt(jnp.mean(centred * centred, axis=-1, keepdims=True) + EPS)
    return centred * inv, inv


def norm_back(grad, unit, inv, gain):
    scaled = grad * gain
    return inv * (
        scaled
        - jnp.mean(scaled, axis=-1, keepdims=True)
        - unit * jnp.mean(scaled * unit, axis=-1, keepdims=True)
    )


def stack(first, second):
    return jnp.concatenate([first, second], axis=0)


def row_grid(kernel, name, micros, rows, in_specs, out_shape, out_specs, args):
    return pl.pallas_call(
        kernel,
        out_shape=out_shape,
        grid_spec=pltpu.PrefetchScalarGridSpec(
            num_scalar_prefetch=1, grid=(rows,), in_specs=in_specs, out_specs=out_specs
        ),
        compiler_params=pltpu.CompilerParams(vmem_limit_bytes=VMEM_MIB.get(name, 28) * MIB),
        cost_estimate=cost(micros),
        name=name,
    )(*args)


def fixed(shape):
    return pl.BlockSpec(shape, lambda r, info: (0,) * len(shape))


def const(shape):
    return pl.BlockSpec(
        shape, lambda r, info: (0,) * len(shape), pipeline_mode=pl.Buffered(1)
    )


def per_row(*shape):
    return pl.BlockSpec((1,) + shape, lambda r, info: (r,) + (0,) * len(shape))


def kept_row(*shape):
    return pl.BlockSpec((1,) + shape, lambda r, info: (info[2] + r,) + (0,) * len(shape))


def shaped(*shape, dtype=BF16):
    return jax.ShapeDtypeStruct(shape, dtype)


def enter_kernel(info, tok, got, wq, wk, wv, bias, gain, shift, x_out, n_out, nt_out, qkv):
    heads = wq.shape[1]
    x = stack(tok[0], got[0])
    x_out[0] = x
    unit, _ = norm(x.astype(F32))
    normed = (unit * gain[...] + shift[...]).astype(BF16)
    n_out[0] = normed
    nt_out[...] = normed.T
    qkv[0, :, :heads] = (mm(normed, wq[...]) + bias[:, :heads]).astype(BF16)
    qkv[0, :, heads : 2 * heads] = mm(normed, wk[...]).astype(BF16)
    qkv[0, :, 2 * heads :] = (mm(normed, wv[...]) + bias[:, heads : 2 * heads]).astype(BF16)


def enter(info, tokens, got, wq, wk, wv, bias, gain, shift):
    rows, half, width = got.shape
    seq, heads = 2 * half, wq.shape[1]
    return row_grid(
        enter_kernel,
        "enter",
        0,
        rows,
        [kept_row(half, width), per_row(half, width)]
        + [const(wq.shape)] * 3
        + [const(bias.shape)]
        + [const((1, width))] * 2,
        (
            shaped(rows, seq, width),
            shaped(rows, seq, width),
            shaped(width, rows * seq),
            shaped(rows, seq, 3 * heads),
        ),
        (
            per_row(seq, width),
            per_row(seq, width),
            pl.BlockSpec((width, seq), lambda r, info: (0, r)),
            per_row(seq, 3 * heads),
        ),
        (info, tokens, got, wq, wk, wv, bias, gain[None], shift[None]),
    )


def other_heads_kernel(info, n, p0, p1, p2, p3, bias, qkv, w):
    heads = w.shape[1] // 3

    @pl.when(pl.program_id(0) == 0)
    def _():
        nbr, core = info[3 + pl.num_programs(0)], info[1]
        size = p0.shape[0]
        for index, piece in enumerate((p0, p1, p2, p3)):
            row = 1 - nbr if index >= 2 else nbr
            col = 1 - core if index % 2 else core
            start = pl.multiple_of((2 * row + col) * size, size)
            w[pl.ds(start, size), :] = piece[...]

    full = jnp.concatenate(
        [bias[:, :heads], jnp.zeros((1, heads), F32), bias[:, heads : 2 * heads]], axis=1
    )
    qkv[0] = (mm(n[0], w[...]) + full).astype(BF16)


def other_heads(info, n, pieces, bias):
    rows, seq, width = n.shape
    size, wide = pieces[0].shape
    return row_grid(
        other_heads_kernel,
        "other_heads",
        0,
        rows,
        [per_row(seq, width)] + [const((size, wide))] * 4 + [const(bias.shape)],
        (shaped(rows, seq, wide), shaped(width, wide)),
        (per_row(seq, wide), fixed((width, wide))),
        (info, n, *pieces, bias),
    )


def middle_kernel(
    info, x, m_own, m_oth, w_own, w_mine, w_cross, b_out, gain, shift, grad, got, res, nm, nm_t, up, w_oth
):
    @pl.when(pl.program_id(0) == 0)
    def _():
        size = w_mine.shape[0]
        w_oth[pl.ds(pl.multiple_of(info[1] * size, size), size), :] = w_mine[...]
        w_oth[pl.ds(pl.multiple_of((1 - info[1]) * size, size), size), :] = w_cross[...]

    attended = mm(m_own[0], w_own[...]) + mm(m_oth[0], w_oth[...])
    residual = x[0].astype(F32) + attended + b_out[...]
    res[0] = residual
    unit, _ = norm(residual)
    normed = (unit * gain[...] + shift[...]).astype(BF16)
    nm[0] = normed
    nm_t[...] = normed.T
    up[0] = stack(grad[0], got[0])


def middle(info, x, m_own, m_oth, w_own, w_mine, w_cross, b_out, gain, shift, grad, got):
    rows, seq, width = x.shape
    heads = w_own.shape[0]
    return row_grid(
        middle_kernel,
        "middle",
        0,
        rows,
        [per_row(seq, width), per_row(seq, heads), per_row(seq, heads)]
        + [const(w_own.shape), const(w_mine.shape), const(w_mine.shape)]
        + [const((1, width))] * 3
        + [kept_row(seq // 2, width), per_row(seq // 2, width)],
        (
            shaped(rows, seq, width, dtype=F32),
            shaped(rows, seq, width),
            shaped(width, rows * seq),
            shaped(rows, seq, width),
            shaped(heads, width),
        ),
        (
            per_row(seq, width),
            per_row(seq, width),
            pl.BlockSpec((width, seq), lambda r, info: (0, r)),
            per_row(seq, width),
            fixed((heads, width)),
        ),
        (info, x, m_own, m_oth, w_own, w_mine, w_cross, b_out[None], gain[None], shift[None], grad, got),
    )


def middle_back_kernel(
    info, gnm, res, y, up, gain, b_down, w_own, w_oth, keep, send, gres, glow_t, gm_own, gm_oth, sums
):
    half = keep.shape[1]
    residual, grad, upstream = res[0], gnm[0], up[0].astype(F32)
    out = (residual + y[0] + b_down[...]).astype(BF16)
    keep[0] = out[:half]
    send[0] = out[half:]
    unit, inv = norm(residual)
    total = upstream + norm_back(grad, unit, inv, gain[...])
    gres[0] = total
    low = total.astype(BF16)
    glow_t[...] = low.T
    gm_own[0] = mm(low, w_own[...], NT).astype(BF16)
    gm_oth[0] = mm(low, w_oth[...], NT).astype(BF16)

    @pl.when(pl.program_id(0) == 0)
    def _():
        sums[...] = jnp.zeros_like(sums)

    for index, value in enumerate((grad * unit, grad, total, upstream)):
        sums[index : index + 1, :] += jnp.sum(value, axis=0, keepdims=True)


def middle_back(info, gnm, res, y, up, gain, b_down, w_own, w_oth):
    rows, seq, width = res.shape
    heads = w_own.shape[0]
    row = per_row(seq, width)
    half = per_row(seq // 2, width)
    return row_grid(
        middle_back_kernel,
        "middle_back",
        0,
        rows,
        [row] * 4 + [const((1, width))] * 2 + [const((heads, width))] * 2,
        (
            shaped(rows, seq // 2, width),
            shaped(rows, seq // 2, width),
            shaped(rows, seq, width, dtype=F32),
            shaped(width, rows * seq),
            shaped(rows, seq, heads),
            shaped(rows, seq, heads),
            shaped(8, width, dtype=F32),
        ),
        (
            half,
            half,
            row,
            pl.BlockSpec((width, seq), lambda r, info: (0, r)),
            per_row(seq, heads),
            per_row(seq, heads),
            fixed((8, width)),
        ),
        (info, gnm, res, y, up, gain[None], b_down[None], w_own, w_oth),
    )


def weights_kernel(info, nt, d, glow_t, mixed, keep, send):
    heads = mixed.shape[1]
    g = mm(nt[...], d[...]).astype(BF16)
    o = mm(glow_t[...], mixed[...]).astype(BF16)
    cut = 2 * heads

    @pl.when(info[1] == 0)
    def _():
        keep[...] = g[:, :cut]
        send[:, :heads] = g[:, cut:]
        send[:, heads:] = o

    @pl.when(info[1] != 0)
    def _():
        send[...] = g[:, :cut]
        keep[:, :heads] = g[:, cut:]
        keep[:, heads:] = o


def weights(info, nt, d, glow_t, mixed, block=256):
    width, tokens = nt.shape
    heads = mixed.shape[1]
    part = pl.BlockSpec((block, tokens), lambda r, info: (r, 0))
    result = pl.BlockSpec((block, 2 * heads), lambda r, info: (r, 0))
    return row_grid(
        weights_kernel,
        "weights",
        0,
        width // block,
        [part, const(d.shape), part, const(mixed.shape)],
        (shaped(width, 2 * heads), shaped(width, 2 * heads)),
        (result, result),
        (info, nt, d, glow_t, mixed),
    )


def leave_kernel(info, d_own, d_oth, wq, wk, wv, w_oth, x, gres, gain, keep, send, sums):
    heads = wq.shape[1]
    half = keep.shape[1]
    grad = (
        mm(d_own[0, :, :heads], wq[...], NT)
        + mm(d_own[0, :, heads : 2 * heads], wk[...], NT)
        + mm(d_own[0, :, 2 * heads :], wv[...], NT)
        + mm(d_oth[0], w_oth[...], NT)
    )
    unit, inv = norm(x[0].astype(F32))
    total = gres[0] + norm_back(grad, unit, inv, gain[...])
    keep[0] = total[:half]
    send[0] = total[half:].astype(BF16)

    @pl.when(pl.program_id(0) == 0)
    def _():
        sums[...] = jnp.zeros_like(sums)

    for index, value in enumerate((grad * unit, grad)):
        sums[index : index + 1, :] += jnp.sum(value, axis=0, keepdims=True)


def leave(info, d_own, d_oth, wq, wk, wv, w_oth, x, gres, gain):
    rows, seq, width = x.shape
    row = per_row(seq, width)
    half = per_row(seq // 2, width)
    wide = per_row(seq, d_own.shape[2])
    return row_grid(
        leave_kernel,
        "leave",
        10,
        rows,
        [wide, wide]
        + [const(wq.shape)] * 3
        + [const(w_oth.shape), row, row, const((1, width))],
        (
            shaped(rows, seq // 2, width, dtype=F32),
            shaped(rows, seq // 2, width),
            shaped(8, width, dtype=F32),
        ),
        (half, half, fixed((8, width))),
        (info, d_own, d_oth, wq, wk, wv, w_oth, x, gres, gain[None]),
    )


def spread_kernel(info, mine, near, cross, both, q, k, v, o):
    heads = q.shape[1]
    here = pl.program_id(0) == info[info.shape[0] - 1]
    own = jnp.where(here, mine[...], near[...]).astype(F32)
    other = jnp.where(here, cross[...], both[...]).astype(F32)

    def write(first, second):
        q[...] = first[:, :heads]
        k[...] = first[:, heads:]
        v[...] = second[:, :heads]
        o[...] = second[:, heads:].T

    @pl.when(info[1] == 0)
    def _():
        write(own, other)

    @pl.when(info[1] != 0)
    def _():
        write(other, own)


def spread(info, *pieces):
    block, both = pieces[0].shape
    heads = both // 2
    plain = pl.BlockSpec((block, heads), lambda n, info: (n, 0))
    return row_grid(
        spread_kernel,
        "spread",
        3,
        2,
        [const((block, both))] * 4,
        (shaped(2 * block, heads, dtype=F32),) * 3 + (shaped(heads, 2 * block, dtype=F32),),
        (plain,) * 3 + (pl.BlockSpec((heads, block), lambda n, info: (0, n)),),
        (info, *pieces),
    )


def spread_feed_kernel(info, *refs):
    nbr, core = info[info.shape[0] - 1], info[1]
    up, down = refs[-2:]
    here = pl.program_id(1) == nbr
    for chunk in range(2):
        mine, near, cross, both = refs[4 * chunk : 4 * chunk + 4]

        @pl.when(pl.program_id(0) == chunk)
        def _():
            own = jnp.where(here, mine[...], near[...]).astype(F32)
            other = jnp.where(here, cross[...], both[...]).astype(F32)
            up[...] = jnp.where(core == 0, own, other)
            down[...] = jnp.where(core == 0, other, own)


def spread_feed(info, pieces):
    block, width = pieces[0].shape
    once = pl.BlockSpec((block, width), lambda k, n, info: (0, 0), pipeline_mode=pl.Buffered(1))
    return pl.pallas_call(
        spread_feed_kernel,
        out_shape=(shaped(width, 2 * width, dtype=F32), shaped(2 * width, width, dtype=F32)),
        grid_spec=pltpu.PrefetchScalarGridSpec(
            num_scalar_prefetch=1,
            grid=(2, 2),
            in_specs=[once] * 8,
            out_specs=(
                pl.BlockSpec((block, width), lambda k, n, info: (n, k)),
                pl.BlockSpec((block, width), lambda k, n, info: (2 * k + n, 0)),
            ),
        ),
        compiler_params=pltpu.CompilerParams(vmem_limit_bytes=24 * MIB),
        cost_estimate=cost(5),
        name="spread_feed",
    )(info, *pieces)


def swap(value, axis):
    return lax.ppermute(value, axis, [(0, 1), (1, 0)])


def part(value, index, count):
    size = value.shape[0] // count
    return lax.dynamic_slice_in_dim(value, index * size, size, 0)


class Rows:
    def __init__(self, array, matrix=None, start=0, size=None):
        self.array, self.matrix, self.start = array, matrix, start
        self.size = array.shape[-2] if size is None else size

    def half(self, index):
        size = self.size // 2
        return Rows(self.array, self.matrix, self.start + index * size, size)

    def read(self):
        if self.matrix is None:
            return lax.dynamic_slice_in_dim(self.array, self.start, self.size, 0)
        shape = (1, self.size, self.array.shape[-1])
        return lax.dynamic_slice(self.array, (self.matrix, self.start, 0), shape)[0]


class Either:
    def __init__(self, index, first, second):
        self.index, self.first, self.second = index, first, second

    def half(self, index):
        return Either(self.index, self.first.half(index), self.second.half(index))

    def read(self):
        return jnp.where(self.index == 0, self.first.read(), self.second.read())


class Stacked:
    def __init__(self, upper, lower):
        self.upper, self.lower = Rows(upper), Rows(lower)

    def half(self, index):
        return Either(index, self.upper, self.lower)


def total_low(addends):
    return add_low(*[addend.read() for addend in addends])


def join(index, mine, other):
    return jnp.where(index == 0, jnp.concatenate([mine, other]), jnp.concatenate([other, mine]))


def tie(*values):
    return lax.optimization_barrier(values)


def add_low(*addends):
    return sum(addend.astype(F32) for addend in addends).astype(BF16)


def ladder(sizes):
    steps = [("nbr", lax.axis_index("nbr"), [(0, 1), (1, 0)])]
    bit = 1
    while bit < sizes["rest"]:
        index = (lax.axis_index("rest") // bit) % 2
        steps.append(("rest", index, [(i, i ^ bit) for i in range(sizes["rest"])]))
        bit *= 2
    return steps


def halve(step):
    axis, index, perm = step

    def prepare(addends):
        sent = total_low([a.half(1 - index) for a in addends])
        return sent, tuple(a.half(index) for a in addends)

    return (
        prepare,
        lambda sent: (lax.ppermute(sent, axis, perm),),
        lambda kept, got: kept + (Rows(got),),
    )


def double(step):
    axis, index, perm = step

    def prepare(value):
        if isinstance(value, tuple):
            value = total_low(value)
        return value, value

    return prepare, lambda sent: (lax.ppermute(sent, axis, perm),), functools.partial(join, index)


def twice(value):
    return value, value


def to_pair(axis):
    return (
        lambda three: (three[1], three),
        lambda sent: (swap(sent, axis),),
        lambda three, got: three + (got,),
    )


def to_three():
    return (
        twice,
        lambda sent: (swap(sent, "nbr"), swap(sent, "core")),
        lambda value, near, cross: (value, near, cross),
    )


def add_over(axis, perm):
    return twice, lambda sent: (lax.ppermute(sent, axis, perm),), jnp.add


class Chain:
    def __init__(self, value, moves, behind=()):
        self.value, self.finish, self.moves, self.flying = value, None, list(moves), ()
        self.go(behind)

    def go(self, behind=(), values=()):
        if self.finish is not None:
            self.value, self.finish = self.finish(self.value, *self.flying), None
            self.flying = ()
        if self.moves:
            prepare, launch, self.finish = self.moves.pop(0)
            sent, self.value = prepare(self.value)
            if behind or values:
                sent, values = meet(behind, sent, list(values))
            self.flying = launch(sent)
        return values

    @property
    def done(self):
        return self.finish is None


def meet(chains, *values):
    flying, tied = lax.optimization_barrier(([c.flying for c in chains], list(values)))
    for c, transfers in zip(chains, flying):
        c.flying = tuple(transfers)
    return tied[0] if len(tied) == 1 else tied


def on_device(
    sizes,
    tokens,
    lengths,
    out_grad,
    ln1_gain,
    ln1_shift,
    w_query,
    b_query,
    w_key,
    w_value,
    b_value,
    w_out,
    b_out,
    ln2_gain,
    ln2_shift,
    w_up,
    b_up,
    w_down,
    b_down,
):
    side = lax.axis_index("mp")
    core = lax.axis_index("core")
    nbr = lax.axis_index("nbr")
    rows_dev, half, width = tokens.shape
    rows = rows_dev // 2
    seq = 2 * half
    total = rows * seq
    heads = w_query.shape[1]
    units = w_up.shape[1] // 2
    steps = ladder(sizes)

    def by_core(first, second):
        return jnp.where(core == 0, first, second)

    def flat(value):
        return value.reshape(total, value.shape[-1])

    info = jnp.concatenate(
        [jnp.stack([side * half, core, side * rows]), part(lengths, side, 2), nbr[None]]
    ).astype(jnp.int32)

    quarter = 2 * nbr + core
    w_send = jnp.concatenate([part(w, quarter, 4) for w in (w_query, w_key, w_value)], axis=1)
    t_send = part(tokens, 1 - side, 2)
    got_tokens = swap(t_send, "mp")
    w_mine = swap(w_send, "mp")
    bias_own = jnp.concatenate([b_query, b_value, b_up])
    bias_oth = swap(bias_own, "mp")
    up_halves = [w_up[:, :units], w_up[:, units:]]
    down_halves = [w_down[:units], w_down[units:]]
    f_send0 = part(by_core(up_halves[0], down_halves[0]), nbr, 2)
    f_whole1 = by_core(up_halves[1], down_halves[1])
    f_send1, f_send2 = f_whole1[: units // 2], f_whole1[units // 2 :]
    g_send = part(out_grad, 1 - side, 2)
    o_send = part(w_out, core, 2)
    got_tokens, f_send0, f_send1, f_send2, g_send, o_send = tie(
        got_tokens, f_send0, f_send1, f_send2, g_send, o_send
    )
    x, normed_in, nt, qkv_own = enter(
        info, tokens, got_tokens, w_query, w_key, w_value, bias_own[None], ln1_gain, ln1_shift
    )
    f_mine0 = swap(f_send0, "mp")
    o_mine = swap(o_send, "mp")
    qkv_own, w_mine, bias_oth = tie(qkv_own, w_mine, bias_oth)
    w_near = swap(w_mine, "nbr")
    mixed_own, lse_own = attend(info, qkv_own)
    mixed_own, w_near, g_send = tie(mixed_own, w_near, g_send)
    pieces = (w_mine, swap(w_mine, "core"), w_near, swap(w_near, "core"))
    got_grad = swap(g_send, "mp")
    qkv_oth, wqkv_oth = other_heads(info, normed_in, pieces, bias_oth[None])
    qkv_oth, f_mine0, f_send1, o_mine = tie(qkv_oth, f_mine0, f_send1, o_mine)
    f_near0 = swap(f_mine0, "nbr")
    f_mine1 = swap(f_send1, "mp")
    mixed_oth, lse_oth = attend(info, qkv_oth)
    mixed_oth, f_near0, got_grad = tie(mixed_oth, f_near0, got_grad)
    f_cross0 = swap(f_mine0, "core"), swap(f_near0, "core")
    residual, nm, nm_t, up, wout_oth = middle(
        info, x, mixed_own, mixed_oth, w_out, o_mine, swap(o_mine, "core"),
        b_out, ln2_gain, ln2_shift, out_grad, got_grad,
    )
    nm, f_mine1, f_send2 = tie(nm, f_mine1, f_send2)
    f_mine2 = swap(f_send2, "mp")
    bup_own = bias_own[2 * heads :][None]
    bup_oth = bias_oth[2 * heads :][None]
    args = (info, flat(nm), nm_t, flat(up))
    y, gnm, f_keep0, f_give0, gbup0 = feed(
        *args, (f_mine0, f_near0), f_cross0, bup_oth[:, :units]
    )
    f_cross1 = swap(f_mine1, "core")
    y, f_give0, f_mine2, f_cross1 = tie(y, f_give0[0], f_mine2, f_cross1)
    f_swap0, f_cross2 = swap(f_give0, "core"), swap(f_mine2, "core")
    y, f_oth0, f_cross2 = tie(y, add_low(f_keep0[0], f_swap0), f_cross2)
    f_got0 = swap(f_oth0, "mp")
    bup_rest = jnp.concatenate([bup_oth[:, units:], bup_own], axis=1)
    y, gnm, f_keep, f_give, gbup_rest = feed(
        *args, (f_mine1, f_mine2), (f_cross1, f_cross2), bup_rest, own=(w_up, w_down), sums=(y, gnm)
    )
    gbup1, gbup_own = gbup_rest[:, :units], gbup_rest[:, units:]
    gnm, f_give, f_got0 = tie(gnm, f_give, f_got0)
    f_swap = swap(f_give, "core")
    out_keep, out_send, grad_res, glow_t, gm_own, gm_oth, mid_sums = middle_back(
        info, gnm.reshape(rows, seq, width), residual, y.reshape(rows, seq, width), up,
        ln2_gain, b_down, w_out, wout_oth,
    )
    gm_oth, f_swap = tie(gm_oth, f_swap)
    f_got1 = swap(add_low(f_keep[0], f_swap[0]), "mp")
    halving = [halve(step) for step in steps]
    doubling = [double(step) for step in reversed(steps)]
    feed_moves = halving + doubling[:-1] + [to_three()]
    att_moves = feed_moves + [to_pair("core")]
    f0 = Chain((Rows(f_keep, 1), Rows(f_swap, 1), Rows(f_got0)), feed_moves)
    d_oth, bias_sum_oth = attend_back(info, qkv_oth, gm_oth, lse_oth)
    d_oth = meet([f0], d_oth)
    f0.go()
    a_keep, a_give = weights(info, nt, flat(d_oth), glow_t, flat(mixed_oth))
    a_give, f_got1 = meet([f0], a_give, f_got1)
    f1 = Chain((Rows(f_keep, 2), Rows(f_swap, 2), Rows(f_got1)), feed_moves)
    gm_own, a_oth = tie(gm_own, add_low(a_keep, swap(a_give, "core")))
    a_got0 = swap(a_oth[: width // 2], "mp")
    f0.go()
    d_own, bias_sum_own = attend_back(info, qkv_own, gm_own, lse_own)
    d_own, a_got0, a_last = meet([f0, f1], d_own, a_got0, a_oth[width // 2 :])
    a_got1 = swap(a_last, "mp")
    f1.go()
    f0.go()
    a_keep, a_give = weights(info, nt, flat(d_own), glow_t, flat(mixed_own))
    a_give, a_got1 = meet([f0, f1], a_give, a_got1)
    a_swap = swap(a_give, "core")
    d_own, a_swap, out_send = tie(d_own, a_swap, out_send)
    att = Chain((Rows(a_keep), Rows(a_swap), Stacked(a_got0, a_got1)), att_moves, (f1, f0))
    f1.go()
    f0.go()
    out_got = swap(out_send, "mp")
    dx_keep, dx_send, end_sums = leave(
        info, d_own, d_oth, w_query, w_key, w_value, wqkv_oth, x, grad_res, ln1_gain
    )
    dx_send, end_sums = att.go((f0, f1), (dx_send, end_sums))
    f1.go()
    f0.go()

    def bias_sums(d, gbup):
        sums = jnp.sum(d, axis=(0, 1))
        return [sums[:heads], sums[2 * heads :]] + [g[0] for g in gbup]

    def small_sums(end_sums):
        shared = [end_sums[0], end_sums[1]] + [mid_sums[i] for i in range(4)]
        mine = jnp.concatenate(shared + bias_sums(bias_sum_own, [gbup_own]))
        sent = jnp.concatenate(shared + bias_sums(bias_sum_oth, [gbup0, gbup1]))
        parts = swap(mine, "core"), swap(sent, "mp"), cross(sent)
        return [mine] + list(parts)

    def cross(value):
        return lax.ppermute(value, ("core", "mp"), [(i, 3 - i) for i in range(4)])

    terms = small_sums(end_sums)
    waits = {f0: 1, f1: 1}
    pieces = {}
    vec = dx_got = None
    stage = 1
    while att.moves:
        stage += 1
        live = [c for c in (vec,) if c is not None and not c.done]
        for c in (f1, f0):
            if not c.done and (c.moves or waits[c] == 0 or len(att.moves) == 1):
                live.append(c)
            elif not c.done:
                waits[c] -= 1
        if vec is None:
            out_got, terms = att.go(live, (out_got, terms))
            vec = Chain(
                (terms[0] + terms[2]) + (terms[1] + terms[3]),
                [add_over(axis, perm) for axis, _, perm in steps],
            )
        elif dx_got is None:
            (dx_send,) = att.go(live, (dx_send,))
            dx_got = swap(dx_send, "mp")
        elif len(att.moves) == 3:
            (out_got,) = att.go(live, (out_got,))
            block_out = join(side, out_keep, out_got)
        elif len(att.moves) == 2:
            live = [c for c in live if c is not vec]
            dx_got, block_out = att.go(live, (dx_got, block_out))
        elif len(att.moves) == 1:
            up_sum, down_sum = spread_feed(info, pieces[f0] + pieces[f1])
            up_sum, dx_got = tie(up_sum, dx_got)
            input_grad = join(side, dx_keep, dx_got.astype(F32))
            up_sum, down_sum, block_out, input_grad = att.go(
                live, (up_sum, down_sum, block_out, input_grad)
            )
        else:
            att.go(live)
        for c in live:
            c.go()
            if c in waits and c.done:
                pieces[c] = c.value + (swap(c.value[1], "core"),)
    while not vec.done:
        vec.go()

    common = [vec.value[i * width : (i + 1) * width] for i in range(6)]
    split = vec.value[6 * width :]
    att.go()
    q_sum, k_sum, v_sum, o_sum = spread(info, *att.value)
    return (
        block_out,
        input_grad,
        common[0],
        common[1],
        q_sum,
        split[:heads],
        k_sum,
        v_sum,
        split[heads : 2 * heads],
        o_sum,
        common[4],
        common[2],
        common[3],
        up_sum,
        split[2 * heads :],
        down_sum,
        common[5],
    )


def solution(mesh):
    n_dp, n_mp = mesh.shape["dp"], mesh.shape["mp"]
    names = ("rest", "nbr", "core", "mp")
    inner = Mesh(mesh.devices.reshape(n_dp // 4, 2, 2, n_mp), names)
    dp = ("rest", "nbr", "core")
    in_specs = (
        P(dp, "mp", None),
        P(dp),
        P(dp, "mp", None),
        P(),
        P(),
        P(None, "mp"),
        P("mp"),
        P(None, "mp"),
        P(None, "mp"),
        P("mp"),
        P("mp", None),
        P(),
        P(),
        P(),
        P(None, "mp"),
        P("mp"),
        P("mp", None),
        P(),
    )
    out_specs = (
        P(dp, "mp", None),
        P(dp, "mp", None),
        P(),
        P(),
        P(None, "mp"),
        P("mp"),
        P(None, "mp"),
        P(None, "mp"),
        P("mp"),
        P("mp", None),
        P(),
        P(),
        P(),
        P(None, "mp"),
        P("mp"),
        P("mp", None),
        P(),
    )
    return jax.shard_map(
        functools.partial(on_device, dict(inner.shape)),
        mesh=inner,
        in_specs=in_specs,
        out_specs=out_specs,
        check_vma=False,
    )
```
